32 devices in a mesh: space: 4 (over y, x), orb: 8 (over z, core).
Axes of the slice: x: 2, y: 2, z: 4, core: 2. Of those that a mesh axis runs over, the one named last changes fastest.
Arguments:
- orbitals: float32 [16, 16, 32, 1024], P('space', None, None, 'orb'), may hold values from -6 to 6
- potential: float32 [16, 16, 32], P('space'), may hold values from 0 to 2
Outputs:
- updated: float32 [16, 16, 32, 1024], P('space', None, None, 'orb')
The draws below stay inside these ranges and needn't reach their ends.
All inputs are finite; a program needn't handle non-finite values.
Results may differ from the reference program's by a relative error of at most 0.00007.
Values sent between devices are 32-bit elements; how exact they have to be, the bound alone decides.
A program may use at most 64 MiB of HBM per device.

```python
import jax
import jax.numpy as jnp
from jax import lax

NY = 16
NZ = 32
ORB_DEV = 128
PANEL = 512
DEGREE = 4
NX = 16
ORBS = 1024
PANEL_DEV = 64
N_ORB = 8


def levels(own_key, dims, split, low, largest):
    def one(dim, parts):
        steps = jax.random.uniform(jax.random.fold_in(jax.random.fold_in(own_key, 6), dim), (parts,), jnp.float32, low / len(split), largest / len(split))
        return jnp.repeat(jnp.exp(steps), dims[dim] // parts).reshape((-1,) + (1,) * (len(dims) - dim - 1))

    loudness = one(*split[0])
    for cut in split[1:]:
        loudness = loudness * one(*cut)
    return loudness


def bell_draw(own_key, shape, spread, most, shards=(), held_as=jnp.bfloat16):
    values = spread * jax.random.normal(own_key, shape, jnp.float32)
    if shards:
        values = values * levels(own_key, shape, shards, -0.22, 0.18)
    return jnp.clip(values, -most, most).astype(held_as)


def setup_inputs(seed: int = 0) -> dict:
    keys = jax.random.split(jax.random.key(seed), 3)
    return {
        "orbitals": bell_draw(keys[0], (NX, NY, NZ, ORBS), 1.0, 6.0, ((0, 4), (3, 8)), jnp.float32),
        "potential": jnp.clip(2.0 * jax.random.uniform(keys[1], (NX, NY, NZ), jnp.float32) ** levels(keys[1], (NX, NY, NZ), ((0, 4),), -0.2, 0.2), 0.0, 2.0),
    }


STENCIL = (-205.0 / 72.0, 8.0 / 5.0, -1.0 / 5.0, 8.0 / 315.0, -1.0 / 560.0)
SHIFT_MID = 7.25
HALF_WIDTH = 4.75

def hamilton(field, potential):
    laplace = 3.0 * STENCIL[0] * field
    for axis in range(3):
        for offset in range(1, 5):
            laplace = laplace + STENCIL[offset] * (jnp.roll(field, offset, axis) + jnp.roll(field, -offset, axis))
    return -0.5 * laplace + potential[..., None] * field

def chebyshev(block, potential):
    before = block
    current = (hamilton(block, potential) - SHIFT_MID * block) / HALF_WIDTH
    for order in range(DEGREE - 1):
        following = 2.0 * (hamilton(current, potential) - SHIFT_MID * current) / HALF_WIDTH - before
        before, current = (current, following)
    return current

def reference(orbitals, potential):
    points = NX * NY * NZ
    trail = ORB_DEV - PANEL_DEV
    blocks = jnp.moveaxis(orbitals.reshape(NX, NY, NZ, N_ORB, ORB_DEV), 3, 0)
    filtered = lax.map(lambda block: chebyshev(block, potential), blocks)
    panel = jnp.moveaxis(filtered[..., :PANEL_DEV], 0, 3).reshape(points, PANEL)
    trailing = jnp.moveaxis(filtered[..., PANEL_DEV:], 0, 3).reshape(points, N_ORB * trail)
    highest = lax.Precision.HIGHEST
    gram_full = jnp.dot(panel.T, panel, precision=highest) / points
    coupling = jnp.dot(panel.T, trailing, precision=highest) / points
    lower_factor = jnp.linalg.cholesky(gram_full)
    identity = jnp.eye(PANEL, dtype=jnp.float32)
    inverse = lax.linalg.triangular_solve(lower_factor, identity, left_side=True, lower=True)
    ortho = jnp.dot(panel, inverse.T, precision=highest)
    middle = jnp.dot(inverse, coupling, precision=highest)
    project = jnp.dot(inverse.T, middle, precision=highest)
    trailing_new = trailing - jnp.dot(panel, project, precision=highest)
    joined = jnp.concatenate([ortho.reshape(points, N_ORB, PANEL_DEV), trailing_new.reshape(points, N_ORB, trail)], axis=2)
    return joined.reshape(NX, NY, NZ, N_ORB * ORB_DEV)
```

```python
import functools

import jax
import jax.numpy as jnp
from jax import lax
from jax.experimental import pallas as pl
from jax.experimental.pallas import tpu as pltpu
from jax.sharding import PartitionSpec as P

PANEL = 512
DEGREE = 4

STENCIL = (-205.0 / 72.0, 8.0 / 5.0, -1.0 / 5.0, 8.0 / 315.0, -1.0 / 560.0)
SHIFT_MID = 7.25
HALF_WIDTH = 4.75
LANES = 128
REACH = 4
MESH = pl.DeviceIdType.MESH
HIGHEST = lax.Precision.HIGHEST


def dot(a, b, dims):
    return lax.dot_general(
        a, b, ((dims[:1], dims[1:]), ((), ())), precision=HIGHEST, preferred_element_type=jnp.float32
    )


def regroup(load, store, count, rows):
    width = LANES // count
    step = min(rows, max(8, 128 // count))
    group = lax.broadcasted_iota(jnp.int32, (step, LANES), 1) // width

    def body(block, carry):
        here = pl.ds(pl.multiple_of(block * step, step), step)
        parts = [load(r, here) for r in range(count)]
        for j in range(count):
            out = None
            for r in range(count):
                turn = ((r - j) * width) % LANES
                piece = pltpu.roll(parts[r], turn, 1) if turn else parts[r]
                out = piece if out is None else jnp.where(group == r, piece, out)
            store(j, here, out)
        return carry

    lax.fori_loop(0, rows // step, body, 0)


def exchange(slots, here, send_sem, recv_sem, send, land):
    copies = []
    for hop in range(1, slots):
        there = lax.rem(here + hop, slots)
        copy = pltpu.make_async_remote_copy(
            src_ref=send(there),
            dst_ref=land.at[here],
            send_sem=send_sem.at[hop],
            recv_sem=recv_sem.at[hop],
            device_id={"space": there},
            device_id_type=MESH,
        )
        copy.start()
        copies.append(copy)
    return copies


def wait_exchange(slots, here, send_sem, recv_sem, send, land):
    for hop in range(1, slots):
        there = lax.rem(here + hop, slots)
        source = lax.rem(here + slots - hop, slots)
        pltpu.make_async_remote_copy(
            src_ref=send(there),
            dst_ref=land.at[source],
            send_sem=send_sem.at[hop],
            recv_sem=recv_sem.at[hop],
            device_id={"space": there},
            device_id_type=MESH,
        ).wait()


def gather_orb(count, me, buf, send_sem, recv_sem, side_send, side_recv, arrived=lambda chip: None, during=None):
    chips = count // 2
    chip, core = me // 2, lax.rem(me, 2)
    partner = chip * 2 + (1 - core)

    def along(origin, to, way, step):
        slot = buf.at[origin * 2 + core]
        return pltpu.make_async_remote_copy(
            src_ref=slot,
            dst_ref=slot,
            send_sem=send_sem.at[way, step],
            recv_sem=recv_sem.at[way, step],
            device_id={"orb": to * 2 + core},
            device_id_type=MESH,
        )

    def across(origin, side, index):
        slot = buf.at[origin * 2 + side]
        return pltpu.make_async_remote_copy(
            src_ref=slot,
            dst_ref=slot,
            send_sem=side_send.at[index],
            recv_sem=side_recv.at[index],
            device_id={"orb": partner},
            device_id_type=MESH,
        )

    steps = chips - 1

    def finish(step):
        @pl.when(chip - 1 - step >= 0)
        def _():
            across(chip - 1 - step, 1 - core, 1 + step).wait_recv()
            arrived(chip - 1 - step)

        @pl.when(chip + 1 + step < chips)
        def _():
            across(chip + 1 + step, 1 - core, 1 + steps + step).wait_recv()
            arrived(chip + 1 + step)

    for step in range(steps):
        @pl.when((chip - step >= 0) & (chip + 1 < chips))
        def _():
            along(chip - step, chip + 1, 0, step).start()

        @pl.when((chip + step < chips) & (chip - 1 >= 0))
        def _():
            along(chip + step, chip - 1, 1, step).start()

        if step == 0:
            across(chip, core, 0).start()
            if during:
                during[0]()
        if step == (1 if during else 0):
            if during:
                during[1]()
            across(chip, 1 - core, 0).wait_recv()
            arrived(chip)
        if step:
            finish(step - 1)

        @pl.when(chip - 1 - step >= 0)
        def _():
            along(chip - 1 - step, chip, 0, step).wait_recv()
            across(chip - 1 - step, core, 1 + step).start()

        @pl.when(chip + 1 + step < chips)
        def _():
            along(chip + 1 + step, chip, 1, step).wait_recv()
            across(chip + 1 + step, core, 1 + steps + step).start()

    finish(steps - 1)
    across(chip, core, 0).wait_send()
    for step in range(steps):
        @pl.when((chip - step >= 0) & (chip + 1 < chips))
        def _():
            along(chip - step, chip + 1, 0, step).wait_send()

        @pl.when((chip + step < chips) & (chip - 1 >= 0))
        def _():
            along(chip + step, chip - 1, 1, step).wait_send()

        @pl.when(chip - 1 - step >= 0)
        def _():
            across(chip - 1 - step, core, 1 + step).wait_send()

        @pl.when(chip + 1 + step < chips)
        def _():
            across(chip + 1 + step, core, 1 + steps + step).wait_send()


def split_filter(
    slabs, shape, here, me, x_ref, pot_ref, own_ref, pack, land, pack_back, land_back, pot_land,
    wide_a, wide_b, level, gath, out_sems, pot_sems, back_sems,
):
    planes, rows_y, rows_z = shape
    points = planes * rows_y * rows_z
    slots = 2 * slabs
    width = LANES // slots
    rows = points // slots
    plane = 3 * rows
    thin = points // LANES
    step = 16
    slot = lax.broadcasted_iota(jnp.int32, (step, LANES), 1) // width

    def merge(parts):
        out = None
        for u, (value, v) in enumerate(parts):
            turn = ((u - v) * width) % LANES
            value = pltpu.roll(value, turn, 1) if turn else value
            out = value if out is None else jnp.where(slot == u, value, out)
        return out

    def over(body):
        def one(block, carry):
            body(pl.multiple_of(block * step, step))
            return carry

        lax.fori_loop(0, rows // step, one, 0)

    def half(buf, h):
        return buf.at[:, h * rows : (h + 1) * rows]

    def send(buf, landing, h, sems):
        exchange(slabs, here, *sems[h], lambda there: half(buf, h).at[there], half(landing, h))
        landing[here, h * rows : (h + 1) * rows] = buf[here, h * rows : (h + 1) * rows]

    def wait(buf, landing, h, sems):
        wait_exchange(slabs, here, *sems[h], lambda there: half(buf, h).at[there], half(landing, h))

    def pack_half(h):
        def body(at):
            parts = [x_ref[pl.ds(q * rows + at, step), :] for q in range(slots)]
            for j in range(slabs):
                pack[j, pl.ds(h * rows + at, step), :] = merge([(part, h * slabs + j) for part in parts])

        over(body)
        send(pack, land, h, out_sems)

    def put(target, p, row, value):
        odd = lax.rem(lax.broadcasted_iota(jnp.int32, value.shape, 1) // width, 2)
        size = value.shape[0]
        swapped = jnp.where(odd == 0, pltpu.roll(value, LANES - width, 1), pltpu.roll(value, width, 1))
        target[pl.ds((planes + p) * plane + rows + row, size), :] = value
        target[pl.ds((planes + p) * plane + row, size), :] = swapped
        target[pl.ds((planes + p) * plane + 2 * rows + row, size), :] = swapped
        target[pl.ds(p * plane + rows + row, size), :] = pltpu.roll(value, 2 * width, 1)
        target[pl.ds((2 * planes + p) * plane + rows + row, size), :] = pltpu.roll(value, LANES - 2 * width, 1)

    taps = [-0.5 * c / HALF_WIDTH for c in STENCIL]

    def sweep(source, target, first):
        def body(y, carry):
            for p in range(planes):
                def line(q, yy):
                    row = pl.multiple_of((planes + q) * plane + rows + yy * rows_z, rows_z)
                    return source[pl.ds(row, rows_z), :]

                row = pl.multiple_of(y * rows_z, rows_z)
                centre = line(p, y)
                total = level[pl.ds(p * rows + row, rows_z), :] * centre
                for m in range(1, REACH + 1):
                    near = line(p + m, y) + line(p - m, y) + line(p, y + m) + line(p, y - m)
                    near += pltpu.roll(centre, m, 0) + pltpu.roll(centre, rows_z - m, 0)
                    total += taps[m] * near
                if not first:
                    total = 2.0 * total - target[pl.ds((planes + p) * plane + rows + row, rows_z), :]
                put(target, p, row, total)
            return carry

        lax.fori_loop(0, rows_y // 2, body, 0)

    def filter_half(h):
        wait(pack, land, h, out_sems)

        def unpack(at):
            parts = [land[i, pl.ds(h * rows + at, step), :] for i in range(slabs)]
            for p in range(planes):
                put(wide_a, p, at, merge([(parts[u // 2], 2 * p + u % 2) for u in range(slots)]))

        over(unpack)
        sweep(wide_a, wide_b, True)
        source, target = wide_b, wide_a
        for _ in range(DEGREE - 1):
            sweep(source, target, False)
            source, target = target, source

        def body(at):
            parts = [source[pl.ds((planes + p) * plane + rows + at, step), :] for p in range(planes)]
            for i in range(slabs):
                pack_back[i, pl.ds(h * rows + at, step), :] = merge(
                    [(parts[q // 2], 2 * i + q % 2) for q in range(slots)]
                )

        over(body)
        send(pack_back, land_back, h, back_sems)

    pack_half(0)
    pack_half(1)
    pot_land[here] = pot_ref[...]
    wait_exchange(slabs, here, *pot_sems, lambda there: pot_ref, pot_land)
    lane_slot = lax.broadcasted_iota(jnp.int32, (thin, LANES), 1) // width
    fields = [pot_land[s] for s in range(slabs)]
    pieces = rows // thin
    for p in range(planes):
        for e in range(pieces):
            value = None
            for u in range(slots):
                l = (2 * p + u % 2) * pieces + e
                spread = jnp.broadcast_to(fields[u // 2][:, l : l + 1], (thin, LANES))
                value = spread if value is None else jnp.where(lane_slot == u, spread, value)
            level[pl.ds(p * rows + e * thin, thin), :] = (
                value - (SHIFT_MID + 1.5 * STENCIL[0])
            ) * (1.0 / HALF_WIDTH)

    filter_half(0)
    wait(pack_back, land_back, 0, back_sems)

    def fold_own(at):
        parts = [land_back[j, pl.ds(at, step), :] for j in range(slabs)]
        for k in range(slabs):
            gath[me, pl.ds(k * rows + at, step), :] = merge(
                [(parts[u % slabs], (u // slabs) * slabs + k) for u in range(slots)]
            )

    over(fold_own)

    def finish():
        wait(pack_back, land_back, 1, back_sems)

        def body(at):
            parts = [
                land_back[u % slabs, pl.ds((u // slabs) * rows + at, step), :] for u in range(slots)
            ]
            for q in range(slots):
                own_ref[pl.ds(q * rows + at, step), :] = merge([(part, q) for part in parts])

        over(body)

    return (lambda: filter_half(1)), finish


def filter_kernel(
    slabs, orbs, shape, split,
    x_ref, pot_ref, own_ref, panel_ref, gram_ref, cross_ref,
    pack, land, pack_back, land_back, pot_land, wide_a, wide_b, level, gath, part, part_land, rows_land,
    a_send, a_recv, p_send, p_recv, b_send, b_recv, c_send, c_recv, d_send, d_recv, e_send, e_recv, f_send, f_recv,
    g_send, g_recv, gs_send, gs_recv, h_send, h_recv, hs_send, hs_recv,
):
    planes, rows_y, rows_z = shape
    points = planes * rows_y * rows_z
    here, me = lax.axis_index("space"), lax.axis_index("orb")
    chunk = points // slabs
    width = LANES // slabs

    barrier = pltpu.get_barrier_semaphore()
    for hop in range(1, slabs):
        pl.semaphore_signal(
            barrier, inc=1, device_id={"space": lax.rem(here + hop, slabs)}, device_id_type=MESH
        )
    for hop in range(1, orbs):
        pl.semaphore_signal(
            barrier, inc=1, device_id={"orb": lax.rem(me + hop, orbs)}, device_id_type=MESH
        )
    pl.semaphore_wait(barrier, slabs - 1 + orbs - 1)

    exchange(slabs, here, p_send, p_recv, lambda there: pot_ref, pot_land)

    panel_dev = PANEL // orbs
    folds = LANES // panel_dev
    fold = points // folds
    during = None
    if split:
        during = split_filter(
            slabs, shape, here, me, x_ref, pot_ref, own_ref, pack, land, pack_back, land_back, pot_land,
            wide_a, wide_b, level, gath,
            ((a_send, a_recv), (e_send, e_recv)), (p_send, p_recv), ((b_send, b_recv), (f_send, f_recv)),
        )
    else:
        def store_pack(j, at, value):
            pack[j, at, :] = value

        regroup(lambda r, at: x_ref[pl.ds(r * chunk + at.start, at.size), :], store_pack, slabs, chunk)
        exchange(slabs, here, a_send, a_recv, lambda there: pack.at[there], land)
        land[here] = pack[here]
        pot_land[here] = pot_ref[...]
        wait_exchange(slabs, here, p_send, p_recv, lambda there: pot_ref, pot_land)

        thin = points // LANES
        lane_group = lax.broadcasted_iota(jnp.int32, (thin, LANES), 1) // width
        fields = [pot_land[s] for s in range(slabs)]
        for l in range(LANES):
            value = None
            for s in range(slabs):
                spread = jnp.broadcast_to(fields[s][:, l : l + 1], (thin, LANES))
                value = spread if value is None else jnp.where(lane_group == s, spread, value)
            level[pl.ds(l * thin, thin), :] = (value - (SHIFT_MID + 1.5 * STENCIL[0])) * (1.0 / HALF_WIDTH)

        wait_exchange(slabs, here, a_send, a_recv, lambda there: pack.at[there], land)

        def put(target, row, value):
            target[pl.ds(points + row, value.shape[0]), :] = value
            target[pl.ds(row, value.shape[0]), :] = pltpu.roll(value, width, 1)
            target[pl.ds(2 * points + row, value.shape[0]), :] = pltpu.roll(value, LANES - width, 1)

        regroup(
            lambda r, at: land[r, at, :],
            lambda j, at, value: put(wide_a, j * chunk + at.start, value),
            slabs, chunk,
        )

        plane = rows_y * rows_z
        taps = [-0.5 * c / HALF_WIDTH for c in STENCIL]

        def sweep(source, target, first):
            def body(y, carry):
                for p in range(planes):
                    def line(q, yy):
                        return source[pl.ds(pl.multiple_of(points + q * plane + yy * rows_z, rows_z), rows_z), :]

                    row = pl.multiple_of(p * plane + y * rows_z, rows_z)
                    centre = line(p, y)
                    total = level[pl.ds(row, rows_z), :] * centre
                    for m in range(1, REACH + 1):
                        near = line(p + m, y) + line(p - m, y)
                        near += line(p, lax.rem(y + m, rows_y)) + line(p, lax.rem(y + rows_y - m, rows_y))
                        near += pltpu.roll(centre, m, 0) + pltpu.roll(centre, rows_z - m, 0)
                        total += taps[m] * near
                    if not first:
                        before = target[pl.ds(pl.multiple_of(points + row, rows_z), rows_z), :]
                        total = 2.0 * total - before
                    put(target, row, total)
                return carry

            lax.fori_loop(0, rows_y, body, 0)

        sweep(wide_a, wide_b, True)
        source, target = wide_b, wide_a
        for _ in range(DEGREE - 1):
            sweep(source, target, False)
            source, target = target, source

        def store_back(j, at, value):
            pack_back[j, at, :] = value

        regroup(
            lambda r, at: source[pl.ds(points + r * chunk + at.start, at.size), :], store_back, slabs, chunk
        )
        exchange(slabs, here, b_send, b_recv, lambda there: pack_back.at[there], land_back)
        land_back[here] = pack_back[here]
        wait_exchange(slabs, here, b_send, b_recv, lambda there: pack_back.at[there], land_back)

        def store_own(j, at, value):
            own_ref[pl.ds(j * chunk + at.start, at.size), :] = value

        regroup(lambda r, at: land_back[r, at, :], store_own, slabs, chunk)

        step = min(fold, 32)
        fold_group = lax.broadcasted_iota(jnp.int32, (step, LANES), 1) // panel_dev

        def folded(block, carry):
            at = pl.multiple_of(block * step, step)
            out = None
            for r in range(folds):
                piece = own_ref[pl.ds(r * fold + at, step), :]
                piece = pltpu.roll(piece, r * panel_dev, 1) if r else piece
                out = piece if out is None else jnp.where(fold_group == r, piece, out)
            gath[me, pl.ds(at, step), :] = out
            return carry

        lax.fori_loop(0, fold // step, folded, 0)

    block = 512

    def take(tile):
        lanes = pl.ds(pl.multiple_of(tile * LANES, LANES), LANES)

        def store_panel(j, at, value):
            panel_ref[pl.ds(j * fold + at.start, at.size), lanes] = value

        regroup(lambda r, at: gath[tile * folds + r, at, :], store_panel, folds, fold)

        def product(k, total):
            at = pl.ds(pl.multiple_of(k * block, block), block)
            return total + dot(own_ref[at, :], panel_ref[at, lanes], (0, 0))

        part[:, lanes] = lax.fori_loop(
            0, points // block, product, jnp.zeros((LANES, LANES), jnp.float32)
        )

    if folds == 2:
        gather_orb(orbs, me, gath, g_send, g_recv, gs_send, gs_recv, take, during)
    else:
        gather_orb(orbs, me, gath, g_send, g_recv, gs_send, gs_recv)

        def each(tile, carry):
            take(tile)
            return carry

        lax.fori_loop(0, PANEL // LANES, each, 0)

    top, rest = part.at[:panel_dev], part.at[panel_dev:]
    top_land, rest_land = part_land.at[:, :panel_dev], part_land.at[:, panel_dev:]
    exchange(slabs, here, c_send, c_recv, lambda there: top, top_land)
    exchange(slabs, here, d_send, d_recv, lambda there: rest, rest_land)
    part_land[here] = part[...]
    points_all = points * slabs

    def summed(view):
        total = view[0]
        for s in range(1, slabs):
            total += view[s]
        return total / points_all

    wait_exchange(slabs, here, c_send, c_recv, lambda there: top, top_land)
    rows_land[me] = summed(top_land)
    gather_orb(orbs, me, rows_land, h_send, h_recv, hs_send, hs_recv)
    wait_exchange(slabs, here, d_send, d_recv, lambda there: rest, rest_land)
    cross_ref[:panel_dev, :] = jnp.zeros((panel_dev, PANEL), jnp.float32)
    cross_ref[panel_dev:, :] = summed(rest_land)
    for o in range(orbs):
        gram_ref[o * panel_dev : (o + 1) * panel_dev, :] = rows_land[o]


def block_inverse(a):
    n = LANES
    tiles = n // 8
    rows = lax.broadcasted_iota(jnp.int32, (8, n), 0)
    cols = lax.broadcasted_iota(jnp.int32, (8, n), 1)
    work = [a[8 * t : 8 * t + 8] for t in range(tiles)]
    unit = [jnp.where(rows + 8 * t == cols, 1.0, 0.0).astype(jnp.float32) for t in range(tiles)]
    for t0 in range(tiles):
        base = 8 * t0
        columns = [jnp.broadcast_to(work[t0][:, base + k : base + k + 1], (8, n)) for k in range(8)]
        small = {
            (i, k): jnp.broadcast_to(columns[k][i : i + 1], (8, n)) for i in range(8) for k in range(i + 1)
        }
        lower, scales = {}, []
        for j in range(8):
            scales.append(1.0 / small[j, j])
            for i in range(j + 1, 8):
                lower[i, j] = small[i, j] * scales[j]
            for i in range(j + 1, 8):
                for k in range(j + 1, i + 1):
                    small[i, k] = small[i, k] - lower[i, j] * small[k, j]
        turned = {}
        for j in range(8):
            for i in range(j + 1, 8):
                value = lower[i, j]
                for k in range(j + 1, i):
                    value = value + lower[i, k] * turned[k, j]
                turned[i, j] = -value
        a_row, u_row = work[t0], unit[t0]
        a_new, u_new = a_row, u_row
        for k in range(7):
            weight = jnp.zeros((8, n), jnp.float32)
            for i in range(k + 1, 8):
                weight = jnp.where(rows == i, turned[i, k], weight)
            a_new = a_new + weight * jnp.broadcast_to(a_row[k : k + 1], (8, n))
            u_new = u_new + weight * jnp.broadcast_to(u_row[k : k + 1], (8, n))
        work[t0], unit[t0] = a_new, u_new
        if t0 == tiles - 1:
            break
        a_out = u_out = None
        for i in range(8):
            weight = jnp.where(rows == i, scales[i], 0.0)
            for k in range(i):
                weight = jnp.where(rows == k, turned[i, k] * scales[i], weight)
            a_term = weight * jnp.broadcast_to(a_new[i : i + 1], (8, n))
            u_term = weight * jnp.broadcast_to(u_new[i : i + 1], (8, n))
            a_out = a_term if a_out is None else a_out + a_term
            u_out = u_term if u_out is None else u_out + u_term
        a_rows = [jnp.broadcast_to(a_out[k : k + 1], (8, n)) for k in range(8)]
        u_rows = [jnp.broadcast_to(u_out[k : k + 1], (8, n)) for k in range(8)]
        for t in range(t0 + 1, tiles):
            before = work[t]
            for k in range(8):
                column = jnp.broadcast_to(before[:, base + k : base + k + 1], (8, n))
                work[t] = work[t] - column * a_rows[k]
                unit[t] = unit[t] - column * u_rows[k]
    out = []
    for t in range(tiles):
        pivots = jnp.sum(jnp.where(rows + 8 * t == cols, work[t], 0.0), axis=1, keepdims=True)
        out.append(unit[t] * (1.0 / jnp.sqrt(pivots)))
    return jnp.concatenate(out, axis=0)


def solve_kernel(orbs, own_ref, panel_ref, gram_ref, cross_ref, out_ref, work, inverse, weights):
    panel_dev = PANEL // orbs
    me = lax.axis_index("orb")
    n = LANES
    blocks = PANEL // n
    work[...] = gram_ref[...]
    inverse[...] = jnp.zeros_like(inverse)

    def factor(b, carry):
        at = pl.multiple_of(b * n, n)
        diag = block_inverse(work[pl.ds(at, n), pl.ds(at, n)])
        inverse[pl.ds(at, n), pl.ds(at, n)] = diag
        for i in range(1, blocks):
            @pl.when(i > b)
            def _():
                work[i * n : (i + 1) * n, pl.ds(at, n)] = dot(
                    work[i * n : (i + 1) * n, pl.ds(at, n)], diag, (1, 1)
                )
        for i in range(1, blocks):
            @pl.when(i > b)
            def _():
                left = work[i * n : (i + 1) * n, pl.ds(at, n)]
                for k in range(1, i + 1):
                    @pl.when(k > b)
                    def _():
                        right = work[k * n : (k + 1) * n, pl.ds(at, n)]
                        work[i * n : (i + 1) * n, k * n : (k + 1) * n] -= dot(left, right, (1, 1))
        return carry

    lax.fori_loop(0, blocks, factor, 0)
    for i in range(1, blocks):
        span = i * n
        inner = dot(work[i * n : (i + 1) * n, :span], inverse[:span, :span], (1, 0))
        inverse[i * n : (i + 1) * n, :span] = -dot(
            inverse[i * n : (i + 1) * n, i * n : (i + 1) * n], inner, (1, 0)
        )

    middle = dot(cross_ref[...], inverse[...], (1, 1))
    weights[...] = -dot(middle, inverse[...], (1, 0))
    weights[:panel_dev, :] = inverse[pl.ds(pl.multiple_of(me * panel_dev, panel_dev), panel_dev), :]
    points = own_ref.shape[0]
    block = 256
    lanes = lax.broadcasted_iota(jnp.int32, (block, LANES), 1)

    def final(k, carry):
        at = pl.ds(pl.multiple_of(k * block, block), block)
        kept = jnp.where(lanes < panel_dev, 0.0, own_ref[at, :])
        out_ref[at, :] = kept + dot(panel_ref[at, :], weights[...], (1, 1))
        return carry

    lax.fori_loop(0, points // block, final, 0)


def pieces(x):
    high = x.astype(jnp.bfloat16)
    return high, (x - high.astype(jnp.float32)).astype(jnp.bfloat16)


def dot_pieces(a, b, dims):
    def one(left, right):
        return lax.dot_general(
            left, right, ((dims[:1], dims[1:]), ((), ())), preferred_element_type=jnp.float32
        )

    return one(a[0], b[0]) + (one(a[0], b[1]) + one(a[1], b[0]))


def unfolded(product, rows):
    half = LANES // 2
    lanes = lax.broadcasted_iota(jnp.int32, (half, LANES), 1)
    out = []
    for r in range(rows):
        sides = []
        for c in range(2):
            at = product[r * LANES : (r + 1) * LANES, c * LANES : (c + 1) * LANES]
            sides.append(at[:half] + pltpu.roll(at[half:], half, 1))
        out.append(jnp.where(lanes < half, sides[0], pltpu.roll(sides[1], half, 1)))
    return out


def link_orders():
    up = {0: [(0, 1), (0, 0)], 1: [(1, 1), (0, 1), (1, 0), (0, 0)],
          2: [(2, 1), (2, 0), (1, 1), (0, 1), (1, 0), (0, 0)]}
    down = {3 - z: [(3 - o, 1 - h) for o, h in order] for z, order in up.items()}
    return up, down


def early_kernel(
    slabs, orbs, shape,
    x_ref, pot_ref, gath, rest_ref, weight_ref,
    pack, land, pack_back, land_back, pot_land, wide_a, wide_b, level,
    gram_part, gram_land, gram_chip, gram_all, cross_part, cross_land, cross, work, inverse,
    a_send, a_recv, p_send, p_recv, b_send, b_recv, e_send, e_recv, f_send, f_recv,
    along_send, along_recv, across_send, across_recv,
    r_send, r_recv, z_send, z_recv, s_send, s_recv, t_send, t_recv, c_send, c_recv,
):
    planes, rows_y, rows_z = shape
    points = planes * rows_y * rows_z
    here, me = lax.axis_index("space"), lax.axis_index("orb")
    chips = orbs // 2
    chip, core = me // 2, lax.rem(me, 2)
    partner = chip * 2 + (1 - core)
    slots = 2 * slabs
    width = LANES // slots
    rows = points // slots
    plane = 3 * rows
    thin = points // LANES
    fold = points // 2
    part_rows = fold // 2
    panel_dev = PANEL // orbs
    points_all = points * slabs
    step = 16
    slot = lax.broadcasted_iota(jnp.int32, (step, LANES), 1) // width
    out_sems, back_sems = ((a_send, a_recv), (e_send, e_recv)), ((b_send, b_recv), (f_send, f_recv))

    barrier = pltpu.get_barrier_semaphore()
    for hop in range(1, slabs):
        pl.semaphore_signal(
            barrier, inc=1, device_id={"space": lax.rem(here + hop, slabs)}, device_id_type=MESH
        )
    for hop in range(1, orbs):
        pl.semaphore_signal(
            barrier, inc=1, device_id={"orb": lax.rem(me + hop, orbs)}, device_id_type=MESH
        )

    def merge(parts):
        out = None
        for u, (value, v) in enumerate(parts):
            turn = ((u - v) * width) % LANES
            value = pltpu.roll(value, turn, 1) if turn else value
            out = value if out is None else jnp.where(slot == u, value, out)
        return out

    def over(body):
        def one(block, carry):
            body(pl.multiple_of(block * step, step))
            return carry

        lax.fori_loop(0, rows // step, one, 0)

    def half(buf, h):
        return buf.at[:, h * rows : (h + 1) * rows]

    def send(buf, landing, h, sems):
        exchange(slabs, here, *sems[h], lambda there: half(buf, h).at[there], half(landing, h))
        landing[here, h * rows : (h + 1) * rows] = buf[here, h * rows : (h + 1) * rows]

    def wait(buf, landing, h, sems):
        wait_exchange(slabs, here, *sems[h], lambda there: half(buf, h).at[there], half(landing, h))

    def pack_half(h):
        def body(at):
            parts = [x_ref[pl.ds(q * rows + at, step), :] for q in range(slots)]
            for j in range(slabs):
                pack[j, pl.ds(h * rows + at, step), :] = merge([(part, h * slabs + j) for part in parts])

        over(body)

    def put(target, p, row, value):
        odd = lax.rem(lax.broadcasted_iota(jnp.int32, value.shape, 1) // width, 2)
        size = value.shape[0]
        swapped = jnp.where(odd == 0, pltpu.roll(value, LANES - width, 1), pltpu.roll(value, width, 1))
        target[pl.ds((planes + p) * plane + rows + row, size), :] = value
        target[pl.ds((planes + p) * plane + row, size), :] = swapped
        target[pl.ds((planes + p) * plane + 2 * rows + row, size), :] = swapped
        target[pl.ds(p * plane + rows + row, size), :] = pltpu.roll(value, 2 * width, 1)
        target[pl.ds((2 * planes + p) * plane + rows + row, size), :] = pltpu.roll(value, LANES - 2 * width, 1)

    taps = [-0.5 * c / HALF_WIDTH for c in STENCIL]

    def sweep(source, target, first):
        def body(y, carry):
            for p in range(planes):
                def line(q, yy):
                    row = pl.multiple_of((planes + q) * plane + rows + yy * rows_z, rows_z)
                    return source[pl.ds(row, rows_z), :]

                row = pl.multiple_of(y * rows_z, rows_z)
                centre = line(p, y)
                total = level[pl.ds(p * rows + row, rows_z), :] * centre
                for m in range(1, REACH + 1):
                    near = line(p + m, y) + line(p - m, y) + line(p, y + m) + line(p, y - m)
                    near += pltpu.roll(centre, m, 0) + pltpu.roll(centre, rows_z - m, 0)
                    total += taps[m] * near
                if not first:
                    total = 2.0 * total - target[pl.ds((planes + p) * plane + rows + row, rows_z), :]
                put(target, p, row, total)
            return carry

        lax.fori_loop(0, rows_y // 2, body, 0)

    def filter_half(h, during=None):
        with jax.named_scope("wait_a"):
            wait(pack, land, h, out_sems)

        def unpack(at):
            parts = [land[i, pl.ds(h * rows + at, step), :] for i in range(slabs)]
            for p in range(planes):
                put(wide_a, p, at, merge([(parts[u // 2], 2 * p + u % 2) for u in range(slots)]))

        with jax.named_scope("unpack"):
            over(unpack)
        with jax.named_scope("sweep"):
            sweep(wide_a, wide_b, True)
            source, target = wide_b, wide_a
            for order in range(DEGREE - 1):
                if during and order == DEGREE - 2:
                    during()
                sweep(source, target, False)
                source, target = target, source

        def body(at):
            parts = [source[pl.ds((planes + p) * plane + rows + at, step), :] for p in range(planes)]
            for i in range(slabs):
                pack_back[i, pl.ds(h * rows + at, step), :] = merge(
                    [(parts[q // 2], 2 * i + q % 2) for q in range(slots)]
                )

        with jax.named_scope("pack_b"):
            over(body)
            send(pack_back, land_back, h, back_sems)

    def fold_half(h, store):
        with jax.named_scope("wait_b"):
            wait(pack_back, land_back, h, back_sems)

        def body(at):
            parts = [land_back[j, pl.ds(h * rows + at, step), :] for j in range(slabs)]
            for k in range(slabs):
                store(
                    pl.ds(k * rows + at, step),
                    merge([(parts[u % slabs], (u // slabs) * slabs + k) for u in range(slots)]),
                )

        with jax.named_scope("fold"):
            over(body)

    with jax.named_scope("pack"):
        pack_half(0)
    with jax.named_scope("barrier"):
        pl.semaphore_wait(barrier, slabs - 1 + orbs - 1)
    exchange(slabs, here, p_send, p_recv, lambda there: pot_ref, pot_land)
    send(pack, land, 0, out_sems)
    with jax.named_scope("pack"):
        pack_half(1)
    send(pack, land, 1, out_sems)
    pot_land[here] = pot_ref[...]
    with jax.named_scope("level"):
        wait_exchange(slabs, here, p_send, p_recv, lambda there: pot_ref, pot_land)
        lane_slot = lax.broadcasted_iota(jnp.int32, (thin, LANES), 1) // width
        fields = [pot_land[s] for s in range(slabs)]
        for p in range(planes):
            for e in range(rows // thin):
                value = None
                for u in range(slots):
                    l = (2 * p + u % 2) * (rows // thin) + e
                    spread = jnp.broadcast_to(fields[u // 2][:, l : l + 1], (thin, LANES))
                    value = spread if value is None else jnp.where(lane_slot == u, spread, value)
                level[pl.ds(p * rows + e * thin, thin), :] = (
                    value - (SHIFT_MID + 1.5 * STENCIL[0])
                ) * (1.0 / HALF_WIDTH)

    up, down = link_orders()

    def along(origin, h, way):
        view = gath.at[origin * 2 + core, h * part_rows : (h + 1) * part_rows]
        return pltpu.make_async_remote_copy(
            src_ref=view,
            dst_ref=view,
            send_sem=along_send.at[way, origin * 2 + h],
            recv_sem=along_recv.at[way, origin * 2 + h],
            device_id={"orb": (chip + 1 - 2 * way) * 2 + core},
            device_id_type=MESH,
        )

    def across(origin, h, side):
        view = gath.at[origin * 2 + side, h * part_rows : (h + 1) * part_rows]
        return pltpu.make_async_remote_copy(
            src_ref=view,
            dst_ref=view,
            send_sem=across_send.at[origin * 2 + h],
            recv_sem=across_recv.at[origin * 2 + h],
            device_id={"orb": partner},
            device_id_type=MESH,
        )

    def on_chip(z, body):
        pl.when(chip == z)(body)

    def arrivals(z, t):
        found = []
        for way, orders in ((0, up), (1, down)):
            order = orders.get(z - 1 + 2 * way, [])
            if t < len(order):
                found.append((way, order[t]))
        return found

    def begin():
        for z in range(chips):
            def body():
                for way, orders in ((0, up), (1, down)):
                    if z in orders:
                        for item in orders[z]:
                            if item[0] != z:
                                break
                            along(*item, way).start()
                for h in range(2):
                    across(z, h, core).start()

            on_chip(z, body)

    def receive(t):
        with jax.named_scope("receive"):
            for z in range(chips):
                def body():
                    for way, item in arrivals(z, t):
                        along(*item, way).wait_recv()
                        across(*item, core).start()

                on_chip(z, body)

    def forward(t):
        for z in range(chips):
            def body():
                for way, item in arrivals(z, t):
                    order = (up, down)[way].get(z, [])
                    if item in order:
                        along(*item, way).start()
                        for later in order[order.index(item) + 1 :]:
                            if later[0] != z:
                                break
                            along(*later, way).start()

            on_chip(z, body)

    def settle(t):
        with jax.named_scope("settle"):
            for z in range(chips):
                def body():
                    for way, item in arrivals(z, t):
                        across(*item, 1 - core).wait_recv()

                on_chip(z, body)

    def settle_own():
        for z in range(chips):
            def body():
                for h in range(2):
                    across(z, h, 1 - core).wait_recv()

            on_chip(z, body)

    def drain():
        for z in range(chips):
            def body():
                for way, orders in ((0, up), (1, down)):
                    for item in orders.get(z, []):
                        along(*item, way).wait_send()
                for h in range(2):
                    across(z, h, core).wait_send()
                for t in range(2 * (chips - 1)):
                    for way, item in arrivals(z, t):
                        across(*item, core).wait_send()

            on_chip(z, body)

    filter_half(0)

    def store_panel(at, value):
        gath[me, at, :] = value

    fold_half(0, store_panel)
    begin()

    def first():
        receive(0)
        forward(0)

    filter_half(1, first)
    receive(1)
    settle_own()
    settle(0)
    settle(1)

    tiles = chips * (chips + 1) // 2
    share = tiles // 2
    block = share * LANES // slabs
    centre = (chip + 1) // 2 == 1

    def block_at(s):
        return pl.ds(pl.multiple_of(s * block, 8), block)

    def pair(z, at):
        return jnp.concatenate([gath[z * 2, at, :], gath[z * 2 + 1, at, :]], axis=1)

    @pl.when(centre)
    def _():
        at = pl.ds(pl.multiple_of((chip - 1) * part_rows, part_rows), part_rows)

        def tile(n, carry):
            t = core * share + n
            za = (t + 8) // 9 + (t + 6) // 9 + (t + 3) // 9
            zb = t - za * (za + 1) // 2
            product = dot_pieces(pieces(pair(za, at)), pieces(pair(zb, at)), (0, 0))
            for r, value in enumerate(unfolded(product, 2)):
                gram_part[pl.ds(pl.multiple_of(n * LANES + r * panel_dev, panel_dev), panel_dev), :] = value
            return carry

        with jax.named_scope("gram"):
            lax.fori_loop(0, share, tile, 0)
        exchange(slabs, here, r_send, r_recv, lambda there: gram_part.at[block_at(there)], gram_land)

    def store_rest(at, value):
        rest_ref[at, :] = value

    fold_half(1, store_rest)

    def spread(index, there):
        view = gram_chip.at[index]
        return pltpu.make_async_remote_copy(
            src_ref=view,
            dst_ref=view,
            send_sem=z_send.at[there],
            recv_sem=z_recv.at[index],
            device_id={"orb": there * 2 + core},
            device_id_type=MESH,
        )

    @pl.when(centre)
    def _():
        with jax.named_scope("wait_r"):
            wait_exchange(slabs, here, r_send, r_recv, lambda there: gram_part.at[block_at(there)], gram_land)
        gram_land[here] = gram_part[block_at(here), :]
        total = gram_land[0]
        for s in range(1, slabs):
            total += gram_land[s]
        gram_chip[chip - 1] = total / points_all

    for z in range(1, 3):
        def body():
            for there in range(chips):
                if there != z:
                    spread(z - 1, there).start()

        on_chip(z, body)
    forward(1)
    receive(2)
    forward(2)

    def couple(n, z):
        rows_k = 256
        with jax.named_scope("couple"):
            def product(k, total):
                at = pl.ds(pl.multiple_of(k * rows_k, rows_k), rows_k)
                return total + dot_pieces(pieces(rest_ref[at, :]), pieces(pair(z, at)), (0, 0))

            total = lax.fori_loop(
                0, fold // rows_k, product, jnp.zeros((LANES, 2 * LANES), jnp.float32)
            )
            value = unfolded(total, 1)[0]
            cross_part[n] = value
            cross_land[n, here] = value
        exchange(slabs, here, c_send.at[n], c_recv.at[n], lambda there: cross_part.at[n], cross_land.at[n])

    lower = chip // 2
    order = [chip, chip + 1 - 2 * lax.rem(chip, 2), 2 - lower, 3 - 3 * lower]
    couple(0, order[0])

    with jax.named_scope("wait_z"):
        for z in range(chips):
            def body():
                for index in range(2):
                    if z != index + 1:
                        spread(index, z).wait_recv()
                    else:
                        for there in range(chips):
                            if there != z:
                                spread(index, there).wait_send()

            on_chip(z, body)
    gram_all[core, block_at(here), :] = gram_chip[0] + gram_chip[1]

    def own_block(there):
        return gram_all.at[core, block_at(here)]

    def gram_side(side, s):
        view = gram_all.at[side, block_at(s)]
        return pltpu.make_async_remote_copy(
            src_ref=view,
            dst_ref=view,
            send_sem=t_send.at[s],
            recv_sem=t_recv.at[s],
            device_id={"orb": partner},
            device_id_type=MESH,
        )

    def plane_copy(hop, s, there):
        view = gram_all.at[core, block_at(s)]
        return pltpu.make_async_remote_copy(
            src_ref=view,
            dst_ref=view,
            send_sem=s_send.at[hop],
            recv_sem=s_recv.at[hop],
            device_id={"space": there},
            device_id_type=MESH,
        )

    for hop in range(1, slabs):
        plane_copy(hop, here, lax.rem(here + hop, slabs)).start()
    gram_side(core, here).start()
    couple(1, order[1])
    receive(3)
    forward(3)
    with jax.named_scope("wait_s"):
        for hop in range(1, slabs):
            source = lax.rem(here + slabs - hop, slabs)
            plane_copy(hop, source, lax.rem(here + hop, slabs)).wait_recv()
            gram_side(core, source).start()
        for s in range(slabs):
            gram_side(1 - core, s).wait_recv()

    n = LANES
    blocks = chips
    inverse[...] = jnp.zeros_like(inverse)
    for za in range(chips):
        for zb in range(za + 1):
            t = za * (za + 1) // 2 + zb
            work[za * n : (za + 1) * n, zb * n : (zb + 1) * n] = gram_all[
                t // share, (t % share) * n : (t % share + 1) * n, :
            ]

    def factor(b, carry):
        at = pl.multiple_of(b * n, n)
        with jax.named_scope("diag"):
            diag = block_inverse(work[pl.ds(at, n), pl.ds(at, n)])
            inverse[pl.ds(at, n), pl.ds(at, n)] = diag
        for i in range(1, blocks):
            @pl.when(i > b)
            def _():
                work[i * n : (i + 1) * n, pl.ds(at, n)] = dot(
                    work[i * n : (i + 1) * n, pl.ds(at, n)], diag, (1, 1)
                )
        for i in range(1, blocks):
            @pl.when(i > b)
            def _():
                left = work[i * n : (i + 1) * n, pl.ds(at, n)]
                for k in range(1, i + 1):
                    @pl.when(k > b)
                    def _():
                        right = work[k * n : (k + 1) * n, pl.ds(at, n)]
                        work[i * n : (i + 1) * n, k * n : (k + 1) * n] -= dot(left, right, (1, 1))

        @pl.when(b == 0)
        def _():
            receive(4)
            forward(4)

        @pl.when(b == 1)
        def _():
            settle(2)
            settle(3)
            settle(4)
            couple(2, order[2])

        @pl.when(b == 2)
        def _():
            receive(5)
            settle(5)
            couple(3, order[3])

        return carry

    with jax.named_scope("factor"):
        lax.fori_loop(0, blocks, factor, 0)
    with jax.named_scope("inverse"):
        for i in range(1, blocks):
            span = i * n
            inner = dot(work[i * n : (i + 1) * n, :span], inverse[:span, :span], (1, 0))
            inverse[i * n : (i + 1) * n, :span] = -dot(
                inverse[i * n : (i + 1) * n, i * n : (i + 1) * n], inner, (1, 0)
            )

    with jax.named_scope("cross"):
        for k in range(chips):
            wait_exchange(
                slabs, here, c_send.at[k], c_recv.at[k], lambda there: cross_part.at[k], cross_land.at[k]
            )
            total = cross_land[k, 0]
            for s in range(1, slabs):
                total += cross_land[k, s]
            cross[:, pl.ds(pl.multiple_of(order[k] * LANES, LANES), LANES)] = total / points_all
    with jax.named_scope("weights"):
        middle = dot(cross[...], inverse[...], (1, 1))
        trail = -dot(middle, inverse[...], (1, 0))
        own = inverse[pl.ds(pl.multiple_of(me * panel_dev, panel_dev), panel_dev), :]
        turned = jnp.concatenate([own, trail], axis=0).T
        weight_ref[...] = jnp.zeros_like(weight_ref)
        for o in range(orbs):
            value = turned[o * panel_dev : (o + 1) * panel_dev]
            weight_ref[o * LANES : o * LANES + panel_dev, :LANES] = value
            weight_ref[o * LANES + panel_dev : (o + 1) * LANES, LANES:] = value
    drain()
    for hop in range(1, slabs):
        plane_copy(hop, here, lax.rem(here + hop, slabs)).wait_send()
    for s in range(slabs):
        gram_side(core, s).wait_send()


def final_kernel(gath_ref, rest_ref, weight_ref, out_ref, high, low):
    orbs, fold, n = gath_ref.shape
    rows = out_ref.shape[1]
    i = pl.program_id(0)

    @pl.when(i == 0)
    def _():
        high[...], low[...] = pieces(weight_ref[...])

    at = pl.ds(pl.multiple_of(i * rows, rows), rows)
    total = None
    for z in range(orbs // 2):
        k = slice(z * 2 * n, (z + 1) * 2 * n)
        pair = jnp.concatenate([gath_ref[z * 2, at, :], gath_ref[z * 2 + 1, at, :]], axis=1)
        value = dot_pieces(pieces(pair), (high[k, :], low[k, :]), (1, 0))
        total = value if total is None else total + value
    lanes = lax.broadcasted_iota(jnp.int32, (rows, n), 1)
    kept = rest_ref[at, :]
    for h in range(2):
        held = kept if h else pltpu.roll(kept, n // 2, 1)
        out_ref[h] = jnp.where(lanes < n // 2, 0.0, held) + total[:, h * n : (h + 1) * n]


def early_device(slabs, orbs, orbitals, potential):
    planes, rows_y, rows_z, columns = orbitals.shape
    points = planes * rows_y * rows_z
    panel_dev = PANEL // orbs
    chips = orbs // 2
    thin = points // LANES
    fold = points // 2
    tiles = chips * (chips + 1) // 2
    block = tiles // 2 * LANES // slabs
    f32 = jnp.float32
    vmem = pl.BlockSpec(memory_space=pltpu.VMEM)
    dma = pltpu.SemaphoreType.DMA
    gath, rest, weight = pl.pallas_call(
        functools.partial(early_kernel, slabs, orbs, (planes, rows_y, rows_z)),
        out_shape=[
            jax.ShapeDtypeStruct((orbs, fold, LANES), f32),
            jax.ShapeDtypeStruct((fold, LANES), f32),
            jax.ShapeDtypeStruct((orbs * LANES, 2 * LANES), f32),
        ],
        in_specs=[vmem] * 2,
        out_specs=[vmem] * 3,
        scratch_shapes=[pltpu.VMEM((slabs, points // slabs, LANES), f32)] * 4
        + [
            pltpu.VMEM((slabs, thin, LANES), f32),
            pltpu.VMEM((9 * points // 2, LANES), f32),
            pltpu.VMEM((9 * points // 2, LANES), f32),
            pltpu.VMEM((points // 2, LANES), f32),
            pltpu.VMEM((slabs * block, LANES), f32),
            pltpu.VMEM((slabs, block, LANES), f32),
            pltpu.VMEM((2, block, LANES), f32),
            pltpu.VMEM((2, slabs * block, LANES), f32),
            pltpu.VMEM((chips, panel_dev, LANES), f32),
            pltpu.VMEM((chips, slabs, panel_dev, LANES), f32),
            pltpu.VMEM((panel_dev, PANEL), f32),
            pltpu.VMEM((PANEL, PANEL), f32),
            pltpu.VMEM((PANEL, PANEL), f32),
        ]
        + [dma((slabs,))] * 10
        + [dma((2, orbs))] * 2
        + [dma((orbs,))] * 2
        + [dma((slabs,))] * 2
        + [dma((chips,)), dma((2,))]
        + [dma((slabs,))] * 4
        + [dma((chips, slabs))] * 2,
        compiler_params=pltpu.CompilerParams(
            collective_id=0, has_side_effects=True, vmem_limit_bytes=40 << 20
        ),
    )(orbitals.reshape(points, columns), potential.reshape(LANES, thin).T)
    count = 4
    whole = [pl.BlockSpec(memory_space=pltpu.VMEM)] * 3
    out = pl.pallas_call(
        final_kernel,
        grid=(count,),
        out_shape=jax.ShapeDtypeStruct((2, fold, LANES), f32),
        in_specs=whole,
        out_specs=pl.BlockSpec((2, fold // count, LANES), lambda i: (0, i, 0)),
        scratch_shapes=[pltpu.VMEM((orbs * LANES, 2 * LANES), jnp.bfloat16)] * 2,
        compiler_params=pltpu.CompilerParams(vmem_limit_bytes=16 << 20),
    )(gath, rest, weight)
    return out.reshape(planes, rows_y, rows_z, columns)


def per_device(slabs, orbs, orbitals, potential):
    planes, rows_y, rows_z, columns = orbitals.shape
    points = planes * rows_y * rows_z
    panel_dev = PANEL // orbs
    folds = LANES // panel_dev
    thin = points // LANES
    f32 = jnp.float32
    vmem = pl.BlockSpec(memory_space=pltpu.VMEM)
    dma = pltpu.SemaphoreType.DMA
    steps = max(orbs // 2 - 1, 1)
    split = folds == 2 and planes == slabs and rows_y // 2 >= REACH and steps >= 2
    if split and orbs == 8 and PANEL == 4 * LANES and 5 * LANES % (8 * slabs) == 0:
        return early_device(slabs, orbs, orbitals, potential)
    flat = orbitals.reshape(points, columns)
    own, panel, gram, cross = pl.pallas_call(
        functools.partial(filter_kernel, slabs, orbs, (planes, rows_y, rows_z), split),
        out_shape=[
            jax.ShapeDtypeStruct((points, LANES), f32),
            jax.ShapeDtypeStruct((points, PANEL), f32),
            jax.ShapeDtypeStruct((PANEL, PANEL), f32),
            jax.ShapeDtypeStruct((LANES, PANEL), f32),
        ],
        in_specs=[vmem] * 2,
        out_specs=[vmem] * 4,
        scratch_shapes=[pltpu.VMEM((slabs, points // slabs, LANES), f32)] * 4
        + [
            pltpu.VMEM((slabs, thin, LANES), f32),
            pltpu.VMEM(((9 if split else 6) * points // 2, LANES), f32),
            pltpu.VMEM(((9 if split else 6) * points // 2, LANES), f32),
            pltpu.VMEM((points, LANES), f32),
            pltpu.VMEM((orbs, points // folds, LANES), f32),
            pltpu.VMEM((LANES, PANEL), f32),
            pltpu.VMEM((slabs, LANES, PANEL), f32),
            pltpu.VMEM((orbs, panel_dev, PANEL), f32),
        ]
        + [dma((slabs,))] * 14
        + [dma((2, steps))] * 2 + [dma((2 * steps + 1,))] * 2
        + [dma((2, steps))] * 2 + [dma((2 * steps + 1,))] * 2,
        compiler_params=pltpu.CompilerParams(
            collective_id=0, has_side_effects=True, vmem_limit_bytes=32 << 20
        ),
    )(flat, potential.reshape(LANES, thin).T)
    out = pl.pallas_call(
        functools.partial(solve_kernel, orbs),
        out_shape=jax.ShapeDtypeStruct((points, LANES), f32),
        in_specs=[vmem] * 4,
        out_specs=vmem,
        scratch_shapes=[
            pltpu.VMEM((PANEL, PANEL), f32),
            pltpu.VMEM((PANEL, PANEL), f32),
            pltpu.VMEM((LANES, PANEL), f32),
        ],
        compiler_params=pltpu.CompilerParams(vmem_limit_bytes=32 << 20),
    )(own, panel, gram, cross)
    return out.reshape(planes, rows_y, rows_z, columns)


def solution(mesh):
    placed = (P("space", None, None, "orb"), P("space", None, None))
    return jax.shard_map(
        functools.partial(per_device, mesh.shape["space"], mesh.shape["orb"]),
        mesh=mesh,
        in_specs=placed,
        out_specs=P("space", None, None, "orb"),
        check_vma=False,
    )
```

```python
import functools

import jax
import jax.numpy as jnp
from jax import lax
from jax.experimental import pallas as pl
from jax.experimental.pallas import tpu as pltpu
from jax.sharding import PartitionSpec as P

PANEL = 512
DEGREE = 4

STENCIL = (-205.0 / 72.0, 8.0 / 5.0, -1.0 / 5.0, 8.0 / 315.0, -1.0 / 560.0)
SHIFT_MID = 7.25
HALF_WIDTH = 4.75
LANES = 128
REACH = 4
MESH = pl.DeviceIdType.MESH
HIGHEST = lax.Precision.HIGHEST


def dot(a, b, dims):
    return lax.dot_general(
        a, b, ((dims[:1], dims[1:]), ((), ())), precision=HIGHEST, preferred_element_type=jnp.float32
    )


def regroup(load, store, count, rows):
    width = LANES // count
    step = min(rows, max(8, 128 // count))
    group = lax.broadcasted_iota(jnp.int32, (step, LANES), 1) // width

    def body(block, carry):
        here = pl.ds(pl.multiple_of(block * step, step), step)
        parts = [load(r, here) for r in range(count)]
        for j in range(count):
            out = None
            for r in range(count):
                turn = ((r - j) * width) % LANES
                piece = pltpu.roll(parts[r], turn, 1) if turn else parts[r]
                out = piece if out is None else jnp.where(group == r, piece, out)
            store(j, here, out)
        return carry

    lax.fori_loop(0, rows // step, body, 0)


def exchange(slots, here, send_sem, recv_sem, send, land):
    copies = []
    for hop in range(1, slots):
        there = lax.rem(here + hop, slots)
        copy = pltpu.make_async_remote_copy(
            src_ref=send(there),
            dst_ref=land.at[here],
            send_sem=send_sem.at[hop],
            recv_sem=recv_sem.at[hop],
            device_id={"space": there},
            device_id_type=MESH,
        )
        copy.start()
        copies.append(copy)
    return copies


def wait_exchange(slots, here, send_sem, recv_sem, send, land):
    for hop in range(1, slots):
        there = lax.rem(here + hop, slots)
        source = lax.rem(here + slots - hop, slots)
        pltpu.make_async_remote_copy(
            src_ref=send(there),
            dst_ref=land.at[source],
            send_sem=send_sem.at[hop],
            recv_sem=recv_sem.at[hop],
            device_id={"space": there},
            device_id_type=MESH,
        ).wait()


def gather_orb(count, me, buf, send_sem, recv_sem, side_send, side_recv, arrived=lambda chip: None, during=None):
    chips = count // 2
    chip, core = me // 2, lax.rem(me, 2)
    partner = chip * 2 + (1 - core)

    def along(origin, to, way, step):
        slot = buf.at[origin * 2 + core]
        return pltpu.make_async_remote_copy(
            src_ref=slot,
            dst_ref=slot,
            send_sem=send_sem.at[way, step],
            recv_sem=recv_sem.at[way, step],
            device_id={"orb": to * 2 + core},
            device_id_type=MESH,
        )

    def across(origin, side, index):
        slot = buf.at[origin * 2 + side]
        return pltpu.make_async_remote_copy(
            src_ref=slot,
            dst_ref=slot,
            send_sem=side_send.at[index],
            recv_sem=side_recv.at[index],
            device_id={"orb": partner},
            device_id_type=MESH,
        )

    steps = chips - 1

    def finish(step):
        @pl.when(chip - 1 - step >= 0)
        def _():
            across(chip - 1 - step, 1 - core, 1 + step).wait_recv()
            arrived(chip - 1 - step)

        @pl.when(chip + 1 + step < chips)
        def _():
            across(chip + 1 + step, 1 - core, 1 + steps + step).wait_recv()
            arrived(chip + 1 + step)

    for step in range(steps):
        @pl.when((chip - step >= 0) & (chip + 1 < chips))
        def _():
            along(chip - step, chip + 1, 0, step).start()

        @pl.when((chip + step < chips) & (chip - 1 >= 0))
        def _():
            along(chip + step, chip - 1, 1, step).start()

        if step == 0:
            across(chip, core, 0).start()
            if during:
                during[0]()
        if step == (1 if during else 0):
            if during:
                during[1]()
            across(chip, 1 - core, 0).wait_recv()
            arrived(chip)
        if step:
            finish(step - 1)

        @pl.when(chip - 1 - step >= 0)
        def _():
            along(chip - 1 - step, chip, 0, step).wait_recv()
            across(chip - 1 - step, core, 1 + step).start()

        @pl.when(chip + 1 + step < chips)
        def _():
            along(chip + 1 + step, chip, 1, step).wait_recv()
            across(chip + 1 + step, core, 1 + steps + step).start()

    finish(steps - 1)
    across(chip, core, 0).wait_send()
    for step in range(steps):
        @pl.when((chip - step >= 0) & (chip + 1 < chips))
        def _():
            along(chip - step, chip + 1, 0, step).wait_send()

        @pl.when((chip + step < chips) & (chip - 1 >= 0))
        def _():
            along(chip + step, chip - 1, 1, step).wait_send()

        @pl.when(chip - 1 - step >= 0)
        def _():
            across(chip - 1 - step, core, 1 + step).wait_send()

        @pl.when(chip + 1 + step < chips)
        def _():
            across(chip + 1 + step, core, 1 + steps + step).wait_send()


def split_filter(
    slabs, shape, here, me, x_ref, pot_ref, own_ref, pack, land, pack_back, land_back, pot_land,
    wide_a, wide_b, level, gath, out_sems, pot_sems, back_sems,
):
    planes, rows_y, rows_z = shape
    points = planes * rows_y * rows_z
    slots = 2 * slabs
    width = LANES // slots
    rows = points // slots
    plane = 3 * rows
    thin = points // LANES
    step = 16
    slot = lax.broadcasted_iota(jnp.int32, (step, LANES), 1) // width

    def merge(parts):
        out = None
        for u, (value, v) in enumerate(parts):
            turn = ((u - v) * width) % LANES
            value = pltpu.roll(value, turn, 1) if turn else value
            out = value if out is None else jnp.where(slot == u, value, out)
        return out

    def over(body):
        def one(block, carry):
            body(pl.multiple_of(block * step, step))
            return carry

        lax.fori_loop(0, rows // step, one, 0)

    def half(buf, h):
        return buf.at[:, h * rows : (h + 1) * rows]

    def send(buf, landing, h, sems):
        exchange(slabs, here, *sems[h], lambda there: half(buf, h).at[there], half(landing, h))
        landing[here, h * rows : (h + 1) * rows] = buf[here, h * rows : (h + 1) * rows]

    def wait(buf, landing, h, sems):
        wait_exchange(slabs, here, *sems[h], lambda there: half(buf, h).at[there], half(landing, h))

    def pack_half(h):
        def body(at):
            parts = [x_ref[pl.ds(q * rows + at, step), :] for q in range(slots)]
            for j in range(slabs):
                pack[j, pl.ds(h * rows + at, step), :] = merge([(part, h * slabs + j) for part in parts])

        over(body)
        send(pack, land, h, out_sems)

    def put(target, p, row, value):
        odd = lax.rem(lax.broadcasted_iota(jnp.int32, value.shape, 1) // width, 2)
        size = value.shape[0]
        swapped = jnp.where(odd == 0, pltpu.roll(value, LANES - width, 1), pltpu.roll(value, width, 1))
        target[pl.ds((planes + p) * plane + rows + row, size), :] = value
        target[pl.ds((planes + p) * plane + row, size), :] = swapped
        target[pl.ds((planes + p) * plane + 2 * rows + row, size), :] = swapped
        target[pl.ds(p * plane + rows + row, size), :] = pltpu.roll(value, 2 * width, 1)
        target[pl.ds((2 * planes + p) * plane + rows + row, size), :] = pltpu.roll(value, LANES - 2 * width, 1)

    taps = [-0.5 * c / HALF_WIDTH for c in STENCIL]

    def sweep(source, target, first):
        def body(y, carry):
            for p in range(planes):
                def line(q, yy):
                    row = pl.multiple_of((planes + q) * plane + rows + yy * rows_z, rows_z)
                    return source[pl.ds(row, rows_z), :]

                row = pl.multiple_of(y * rows_z, rows_z)
                centre = line(p, y)
                total = level[pl.ds(p * rows + row, rows_z), :] * centre
                for m in range(1, REACH + 1):
                    near = line(p + m, y) + line(p - m, y) + line(p, y + m) + line(p, y - m)
                    near += pltpu.roll(centre, m, 0) + pltpu.roll(centre, rows_z - m, 0)
                    total += taps[m] * near
                if not first:
                    total = 2.0 * total - target[pl.ds((planes + p) * plane + rows + row, rows_z), :]
                put(target, p, row, total)
            return carry

        lax.fori_loop(0, rows_y // 2, body, 0)

    def filter_half(h):
        wait(pack, land, h, out_sems)

        def unpack(at):
            parts = [land[i, pl.ds(h * rows + at, step), :] for i in range(slabs)]
            for p in range(planes):
                put(wide_a, p, at, merge([(parts[u // 2], 2 * p + u % 2) for u in range(slots)]))

        over(unpack)
        sweep(wide_a, wide_b, True)
        source, target = wide_b, wide_a
        for _ in range(DEGREE - 1):
            sweep(source, target, False)
            source, target = target, source

        def body(at):
            parts = [source[pl.ds((planes + p) * plane + rows + at, step), :] for p in range(planes)]
            for i in range(slabs):
                pack_back[i, pl.ds(h * rows + at, step), :] = merge(
                    [(parts[q // 2], 2 * i + q % 2) for q in range(slots)]
                )

        over(body)
        send(pack_back, land_back, h, back_sems)

    pack_half(0)
    pack_half(1)
    pot_land[here] = pot_ref[...]
    wait_exchange(slabs, here, *pot_sems, lambda there: pot_ref, pot_land)
    lane_slot = lax.broadcasted_iota(jnp.int32, (thin, LANES), 1) // width
    fields = [pot_land[s] for s in range(slabs)]
    pieces = rows // thin
    for p in range(planes):
        for e in range(pieces):
            value = None
            for u in range(slots):
                l = (2 * p + u % 2) * pieces + e
                spread = jnp.broadcast_to(fields[u // 2][:, l : l + 1], (thin, LANES))
                value = spread if value is None else jnp.where(lane_slot == u, spread, value)
            level[pl.ds(p * rows + e * thin, thin), :] = (
                value - (SHIFT_MID + 1.5 * STENCIL[0])
            ) * (1.0 / HALF_WIDTH)

    filter_half(0)
    wait(pack_back, land_back, 0, back_sems)

    def fold_own(at):
        parts = [land_back[j, pl.ds(at, step), :] for j in range(slabs)]
        for k in range(slabs):
            gath[me, pl.ds(k * rows + at, step), :] = merge(
                [(parts[u % slabs], (u // slabs) * slabs + k) for u in range(slots)]
            )

    over(fold_own)

    def finish():
        wait(pack_back, land_back, 1, back_sems)

        def body(at):
            parts = [
                land_back[u % slabs, pl.ds((u // slabs) * rows + at, step), :] for u in range(slots)
            ]
            for q in range(slots):
                own_ref[pl.ds(q * rows + at, step), :] = merge([(part, q) for part in parts])

        over(body)

    return (lambda: filter_half(1)), finish


def filter_kernel(
    slabs, orbs, shape, split,
    x_ref, pot_ref, own_ref, panel_ref, gram_ref, cross_ref,
    pack, land, pack_back, land_back, pot_land, wide_a, wide_b, level, gath, part, part_land, rows_land,
    a_send, a_recv, p_send, p_recv, b_send, b_recv, c_send, c_recv, d_send, d_recv, e_send, e_recv, f_send, f_recv,
    g_send, g_recv, gs_send, gs_recv, h_send, h_recv, hs_send, hs_recv,
):
    planes, rows_y, rows_z = shape
    points = planes * rows_y * rows_z
    here, me = lax.axis_index("space"), lax.axis_index("orb")
    chunk = points // slabs
    width = LANES // slabs

    barrier = pltpu.get_barrier_semaphore()
    for hop in range(1, slabs):
        pl.semaphore_signal(
            barrier, inc=1, device_id={"space": lax.rem(here + hop, slabs)}, device_id_type=MESH
        )
    for hop in range(1, orbs):
        pl.semaphore_signal(
            barrier, inc=1, device_id={"orb": lax.rem(me + hop, orbs)}, device_id_type=MESH
        )
    pl.semaphore_wait(barrier, slabs - 1 + orbs - 1)

    exchange(slabs, here, p_send, p_recv, lambda there: pot_ref, pot_land)

    panel_dev = PANEL // orbs
    folds = LANES // panel_dev
    fold = points // folds
    during = None
    if split:
        during = split_filter(
            slabs, shape, here, me, x_ref, pot_ref, own_ref, pack, land, pack_back, land_back, pot_land,
            wide_a, wide_b, level, gath,
            ((a_send, a_recv), (e_send, e_recv)), (p_send, p_recv), ((b_send, b_recv), (f_send, f_recv)),
        )
    else:
        def store_pack(j, at, value):
            pack[j, at, :] = value

        regroup(lambda r, at: x_ref[pl.ds(r * chunk + at.start, at.size), :], store_pack, slabs, chunk)
        exchange(slabs, here, a_send, a_recv, lambda there: pack.at[there], land)
        land[here] = pack[here]
        pot_land[here] = pot_ref[...]
        wait_exchange(slabs, here, p_send, p_recv, lambda there: pot_ref, pot_land)

        thin = points // LANES
        lane_group = lax.broadcasted_iota(jnp.int32, (thin, LANES), 1) // width
        fields = [pot_land[s] for s in range(slabs)]
        for l in range(LANES):
            value = None
            for s in range(slabs):
                spread = jnp.broadcast_to(fields[s][:, l : l + 1], (thin, LANES))
                value = spread if value is None else jnp.where(lane_group == s, spread, value)
            level[pl.ds(l * thin, thin), :] = (value - (SHIFT_MID + 1.5 * STENCIL[0])) * (1.0 / HALF_WIDTH)

        wait_exchange(slabs, here, a_send, a_recv, lambda there: pack.at[there], land)

        def put(target, row, value):
            target[pl.ds(points + row, value.shape[0]), :] = value
            target[pl.ds(row, value.shape[0]), :] = pltpu.roll(value, width, 1)
            target[pl.ds(2 * points + row, value.shape[0]), :] = pltpu.roll(value, LANES - width, 1)

        regroup(
            lambda r, at: land[r, at, :],
            lambda j, at, value: put(wide_a, j * chunk + at.start, value),
            slabs, chunk,
        )

        plane = rows_y * rows_z
        taps = [-0.5 * c / HALF_WIDTH for c in STENCIL]

        def sweep(source, target, first):
            def body(y, carry):
                for p in range(planes):
                    def line(q, yy):
                        return source[pl.ds(pl.multiple_of(points + q * plane + yy * rows_z, rows_z), rows_z), :]

                    row = pl.multiple_of(p * plane + y * rows_z, rows_z)
                    centre = line(p, y)
                    total = level[pl.ds(row, rows_z), :] * centre
                    for m in range(1, REACH + 1):
                        near = line(p + m, y) + line(p - m, y)
                        near += line(p, lax.rem(y + m, rows_y)) + line(p, lax.rem(y + rows_y - m, rows_y))
                        near += pltpu.roll(centre, m, 0) + pltpu.roll(centre, rows_z - m, 0)
                        total += taps[m] * near
                    if not first:
                        before = target[pl.ds(pl.multiple_of(points + row, rows_z), rows_z), :]
                        total = 2.0 * total - before
                    put(target, row, total)
                return carry

            lax.fori_loop(0, rows_y, body, 0)

        sweep(wide_a, wide_b, True)
        source, target = wide_b, wide_a
        for _ in range(DEGREE - 1):
            sweep(source, target, False)
            source, target = target, source

        def store_back(j, at, value):
            pack_back[j, at, :] = value

        regroup(
            lambda r, at: source[pl.ds(points + r * chunk + at.start, at.size), :], store_back, slabs, chunk
        )
        exchange(slabs, here, b_send, b_recv, lambda there: pack_back.at[there], land_back)
        land_back[here] = pack_back[here]
        wait_exchange(slabs, here, b_send, b_recv, lambda there: pack_back.at[there], land_back)

        def store_own(j, at, value):
            own_ref[pl.ds(j * chunk + at.start, at.size), :] = value

        regroup(lambda r, at: land_back[r, at, :], store_own, slabs, chunk)

        step = min(fold, 32)
        fold_group = lax.broadcasted_iota(jnp.int32, (step, LANES), 1) // panel_dev

        def folded(block, carry):
            at = pl.multiple_of(block * step, step)
            out = None
            for r in range(folds):
                piece = own_ref[pl.ds(r * fold + at, step), :]
                piece = pltpu.roll(piece, r * panel_dev, 1) if r else piece
                out = piece if out is None else jnp.where(fold_group == r, piece, out)
            gath[me, pl.ds(at, step), :] = out
            return carry

        lax.fori_loop(0, fold // step, folded, 0)

    block = 512

    def take(tile):
        lanes = pl.ds(pl.multiple_of(tile * LANES, LANES), LANES)

        def store_panel(j, at, value):
            panel_ref[pl.ds(j * fold + at.start, at.size), lanes] = value

        regroup(lambda r, at: gath[tile * folds + r, at, :], store_panel, folds, fold)

        def product(k, total):
            at = pl.ds(pl.multiple_of(k * block, block), block)
            return total + dot(own_ref[at, :], panel_ref[at, lanes], (0, 0))

        part[:, lanes] = lax.fori_loop(
            0, points // block, product, jnp.zeros((LANES, LANES), jnp.float32)
        )

    if folds == 2:
        gather_orb(orbs, me, gath, g_send, g_recv, gs_send, gs_recv, take, during)
    else:
        gather_orb(orbs, me, gath, g_send, g_recv, gs_send, gs_recv)

        def each(tile, carry):
            take(tile)
            return carry

        lax.fori_loop(0, PANEL // LANES, each, 0)

    top, rest = part.at[:panel_dev], part.at[panel_dev:]
    top_land, rest_land = part_land.at[:, :panel_dev], part_land.at[:, panel_dev:]
    exchange(slabs, here, c_send, c_recv, lambda there: top, top_land)
    exchange(slabs, here, d_send, d_recv, lambda there: rest, rest_land)
    part_land[here] = part[...]
    points_all = points * slabs

    def summed(view):
        total = view[0]
        for s in range(1, slabs):
            total += view[s]
        return total / points_all

    wait_exchange(slabs, here, c_send, c_recv, lambda there: top, top_land)
    rows_land[me] = summed(top_land)
    gather_orb(orbs, me, rows_land, h_send, h_recv, hs_send, hs_recv)
    wait_exchange(slabs, here, d_send, d_recv, lambda there: rest, rest_land)
    cross_ref[:panel_dev, :] = jnp.zeros((panel_dev, PANEL), jnp.float32)
    cross_ref[panel_dev:, :] = summed(rest_land)
    for o in range(orbs):
        gram_ref[o * panel_dev : (o + 1) * panel_dev, :] = rows_land[o]


def block_inverse(a):
    n = LANES
    tiles = n // 8
    rows = lax.broadcasted_iota(jnp.int32, (8, n), 0)
    cols = lax.broadcasted_iota(jnp.int32, (8, n), 1)
    work = [a[8 * t : 8 * t + 8] for t in range(tiles)]
    unit = [jnp.where(rows + 8 * t == cols, 1.0, 0.0).astype(jnp.float32) for t in range(tiles)]
    for t0 in range(tiles):
        base = 8 * t0
        columns = [jnp.broadcast_to(work[t0][:, base + k : base + k + 1], (8, n)) for k in range(8)]
        small = {
            (i, k): jnp.broadcast_to(columns[k][i : i + 1], (8, n)) for i in range(8) for k in range(i + 1)
        }
        lower, scales = {}, []
        for j in range(8):
            scales.append(1.0 / small[j, j])
            for i in range(j + 1, 8):
                lower[i, j] = small[i, j] * scales[j]
            for i in range(j + 1, 8):
                for k in range(j + 1, i + 1):
                    small[i, k] = small[i, k] - lower[i, j] * small[k, j]
        turned = {}
        for j in range(8):
            for i in range(j + 1, 8):
                value = lower[i, j]
                for k in range(j + 1, i):
                    value = value + lower[i, k] * turned[k, j]
                turned[i, j] = -value
        a_row, u_row = work[t0], unit[t0]
        a_new, u_new = a_row, u_row
        for k in range(7):
            weight = jnp.zeros((8, n), jnp.float32)
            for i in range(k + 1, 8):
                weight = jnp.where(rows == i, turned[i, k], weight)
            a_new = a_new + weight * jnp.broadcast_to(a_row[k : k + 1], (8, n))
            u_new = u_new + weight * jnp.broadcast_to(u_row[k : k + 1], (8, n))
        work[t0], unit[t0] = a_new, u_new
        if t0 == tiles - 1:
            break
        a_out = u_out = None
        for i in range(8):
            weight = jnp.where(rows == i, scales[i], 0.0)
            for k in range(i):
                weight = jnp.where(rows == k, turned[i, k] * scales[i], weight)
            a_term = weight * jnp.broadcast_to(a_new[i : i + 1], (8, n))
            u_term = weight * jnp.broadcast_to(u_new[i : i + 1], (8, n))
            a_out = a_term if a_out is None else a_out + a_term
            u_out = u_term if u_out is None else u_out + u_term
        a_rows = [jnp.broadcast_to(a_out[k : k + 1], (8, n)) for k in range(8)]
        u_rows = [jnp.broadcast_to(u_out[k : k + 1], (8, n)) for k in range(8)]
        for t in range(t0 + 1, tiles):
            before = work[t]
            for k in range(8):
                column = jnp.broadcast_to(before[:, base + k : base + k + 1], (8, n))
                work[t] = work[t] - column * a_rows[k]
                unit[t] = unit[t] - column * u_rows[k]
    out = []
    for t in range(tiles):
        pivots = jnp.sum(jnp.where(rows + 8 * t == cols, work[t], 0.0), axis=1, keepdims=True)
        out.append(unit[t] * (1.0 / jnp.sqrt(pivots)))
    return jnp.concatenate(out, axis=0)


def solve_kernel(orbs, own_ref, panel_ref, gram_ref, cross_ref, out_ref, work, inverse, weights):
    panel_dev = PANEL // orbs
    me = lax.axis_index("orb")
    n = LANES
    blocks = PANEL // n
    work[...] = gram_ref[...]
    inverse[...] = jnp.zeros_like(inverse)

    def factor(b, carry):
        at = pl.multiple_of(b * n, n)
        diag = block_inverse(work[pl.ds(at, n), pl.ds(at, n)])
        inverse[pl.ds(at, n), pl.ds(at, n)] = diag
        for i in range(1, blocks):
            @pl.when(i > b)
            def _():
                work[i * n : (i + 1) * n, pl.ds(at, n)] = dot(
                    work[i * n : (i + 1) * n, pl.ds(at, n)], diag, (1, 1)
                )
        for i in range(1, blocks):
            @pl.when(i > b)
            def _():
                left = work[i * n : (i + 1) * n, pl.ds(at, n)]
                for k in range(1, i + 1):
                    @pl.when(k > b)
                    def _():
                        right = work[k * n : (k + 1) * n, pl.ds(at, n)]
                        work[i * n : (i + 1) * n, k * n : (k + 1) * n] -= dot(left, right, (1, 1))
        return carry

    lax.fori_loop(0, blocks, factor, 0)
    for i in range(1, blocks):
        span = i * n
        inner = dot(work[i * n : (i + 1) * n, :span], inverse[:span, :span], (1, 0))
        inverse[i * n : (i + 1) * n, :span] = -dot(
            inverse[i * n : (i + 1) * n, i * n : (i + 1) * n], inner, (1, 0)
        )

    middle = dot(cross_ref[...], inverse[...], (1, 1))
    weights[...] = -dot(middle, inverse[...], (1, 0))
    weights[:panel_dev, :] = inverse[pl.ds(pl.multiple_of(me * panel_dev, panel_dev), panel_dev), :]
    points = own_ref.shape[0]
    block = 256
    lanes = lax.broadcasted_iota(jnp.int32, (block, LANES), 1)

    def final(k, carry):
        at = pl.ds(pl.multiple_of(k * block, block), block)
        kept = jnp.where(lanes < panel_dev, 0.0, own_ref[at, :])
        out_ref[at, :] = kept + dot(panel_ref[at, :], weights[...], (1, 1))
        return carry

    lax.fori_loop(0, points // block, final, 0)


def pieces(x):
    high = x.astype(jnp.bfloat16)
    return high, (x - high.astype(jnp.float32)).astype(jnp.bfloat16)


def dot_pieces(a, b, dims):
    def one(left, right):
        return lax.dot_general(
            left, right, ((dims[:1], dims[1:]), ((), ())), preferred_element_type=jnp.float32
        )

    return one(a[0], b[0]) + (one(a[0], b[1]) + one(a[1], b[0]))


def unfolded(product, rows):
    half = LANES // 2
    lanes = lax.broadcasted_iota(jnp.int32, (half, LANES), 1)
    out = []
    for r in range(rows):
        sides = []
        for c in range(2):
            at = product[r * LANES : (r + 1) * LANES, c * LANES : (c + 1) * LANES]
            sides.append(at[:half] + pltpu.roll(at[half:], half, 1))
        out.append(jnp.where(lanes < half, sides[0], pltpu.roll(sides[1], half, 1)))
    return out


def link_orders():
    def both(table):
        out = {z: list(items) for z, items in table.items()}
        for z, items in table.items():
            out[3 - z] = [(1 - way, 3 - o, 1 - h) for way, o, h in items]
        return out

    starts = both({0: [(0, 0, 0), (0, 0, 1)], 1: [(0, 1, 1), (1, 1, 0), (1, 1, 1)]})
    arrive = [
        both({0: [(1, 1, 0), (1, 1, 1)], 1: [(0, 0, 0), (1, 2, 0), (1, 3, 0)]}),
        both({0: [(1, 2, 0)], 1: [(0, 0, 1), (1, 2, 1)]}),
        both({0: [(1, 3, 0)], 1: [(1, 3, 1)]}),
        both({0: [(1, 2, 1)]}),
        both({0: [(1, 3, 1)]}),
    ]
    passed = [
        both({1: [(0, 1, 0), (1, 2, 0)]}),
        both({1: [(0, 0, 0), (1, 3, 0)]}),
        both({1: [(1, 2, 1)]}),
        both({1: [(1, 3, 1)]}),
    ]
    return starts, arrive, passed


def early_kernel(
    slabs, orbs, shape,
    x_ref, pot_ref, gath, rest_ref, weight_ref,
    pack, land, pack_back, land_back, pot_land, wide_a, wide_b, level,
    gram_part, gram_land, gram_chip, gram_all, cross_part, cross_land, cross, work, inverse,
    a_send, a_recv, p_send, p_recv, b_send, b_recv, e_send, e_recv, f_send, f_recv,
    along_send, along_recv, direct_send, across_send, across_recv,
    r_send, r_recv, z_send, z_recv, s_send, s_recv, t_send, t_recv, c_send, c_recv,
):
    planes, rows_y, rows_z = shape
    points = planes * rows_y * rows_z
    here, me = lax.axis_index("space"), lax.axis_index("orb")
    chips = orbs // 2
    chip, core = me // 2, lax.rem(me, 2)
    partner = chip * 2 + (1 - core)
    slots = 2 * slabs
    width = LANES // slots
    rows = points // slots
    plane = 3 * rows
    thin = points // LANES
    fold = points // 2
    part_rows = fold // 2
    panel_dev = PANEL // orbs
    points_all = points * slabs
    step = 16
    slot = lax.broadcasted_iota(jnp.int32, (step, LANES), 1) // width
    out_sems, back_sems = ((a_send, a_recv), (e_send, e_recv)), ((b_send, b_recv), (f_send, f_recv))

    barrier = pltpu.get_barrier_semaphore()
    for hop in range(1, slabs):
        pl.semaphore_signal(
            barrier, inc=1, device_id={"space": lax.rem(here + hop, slabs)}, device_id_type=MESH
        )
    for hop in range(1, orbs):
        pl.semaphore_signal(
            barrier, inc=1, device_id={"orb": lax.rem(me + hop, orbs)}, device_id_type=MESH
        )

    def merge(parts):
        out = None
        for u, (value, v) in enumerate(parts):
            turn = ((u - v) * width) % LANES
            value = pltpu.roll(value, turn, 1) if turn else value
            out = value if out is None else jnp.where(slot == u, value, out)
        return out

    def over(body):
        def one(block, carry):
            body(pl.multiple_of(block * step, step))
            return carry

        lax.fori_loop(0, rows // step, one, 0)

    def half(buf, h):
        return buf.at[:, h * rows : (h + 1) * rows]

    def send(buf, landing, h, sems):
        exchange(slabs, here, *sems[h], lambda there: half(buf, h).at[there], half(landing, h))
        landing[here, h * rows : (h + 1) * rows] = buf[here, h * rows : (h + 1) * rows]

    def wait(buf, landing, h, sems):
        wait_exchange(slabs, here, *sems[h], lambda there: half(buf, h).at[there], half(landing, h))

    def pack_half(h):
        def body(at):
            parts = [x_ref[pl.ds(q * rows + at, step), :] for q in range(slots)]
            for j in range(slabs):
                pack[j, pl.ds(h * rows + at, step), :] = merge([(part, h * slabs + j) for part in parts])

        over(body)

    def put(target, p, row, value):
        odd = lax.rem(lax.broadcasted_iota(jnp.int32, value.shape, 1) // width, 2)
        size = value.shape[0]
        swapped = jnp.where(odd == 0, pltpu.roll(value, LANES - width, 1), pltpu.roll(value, width, 1))
        target[pl.ds((planes + p) * plane + rows + row, size), :] = value
        target[pl.ds((planes + p) * plane + row, size), :] = swapped
        target[pl.ds((planes + p) * plane + 2 * rows + row, size), :] = swapped
        target[pl.ds(p * plane + rows + row, size), :] = pltpu.roll(value, 2 * width, 1)
        target[pl.ds((2 * planes + p) * plane + rows + row, size), :] = pltpu.roll(value, LANES - 2 * width, 1)

    taps = [-0.5 * c / HALF_WIDTH for c in STENCIL]

    def sweep(source, target, first):
        def body(y, carry):
            for p in range(planes):
                def line(q, yy):
                    row = pl.multiple_of((planes + q) * plane + rows + yy * rows_z, rows_z)
                    return source[pl.ds(row, rows_z), :]

                row = pl.multiple_of(y * rows_z, rows_z)
                centre = line(p, y)
                total = level[pl.ds(p * rows + row, rows_z), :] * centre
                for m in range(1, REACH + 1):
                    near = line(p + m, y) + line(p - m, y) + line(p, y + m) + line(p, y - m)
                    near += pltpu.roll(centre, m, 0) + pltpu.roll(centre, rows_z - m, 0)
                    total += taps[m] * near
                if not first:
                    total = 2.0 * total - target[pl.ds((planes + p) * plane + rows + row, rows_z), :]
                put(target, p, row, total)
            return carry

        lax.fori_loop(0, rows_y // 2, body, 0)

    def filter_half(h):
        with jax.named_scope("wait_a"):
            wait(pack, land, h, out_sems)
        if h == 0:
            send(pack, land, 1, out_sems)

        def unpack(at):
            parts = [land[i, pl.ds(h * rows + at, step), :] for i in range(slabs)]
            for p in range(planes):
                put(wide_a, p, at, merge([(parts[u // 2], 2 * p + u % 2) for u in range(slots)]))

        with jax.named_scope("unpack"):
            over(unpack)
        with jax.named_scope("sweep"):
            sweep(wide_a, wide_b, True)
            source, target = wide_b, wide_a
            for _ in range(DEGREE - 1):
                sweep(source, target, False)
                source, target = target, source

        def body(at):
            parts = [source[pl.ds((planes + p) * plane + rows + at, step), :] for p in range(planes)]
            for i in range(slabs):
                pack_back[i, pl.ds(h * rows + at, step), :] = merge(
                    [(parts[q // 2], 2 * i + q % 2) for q in range(slots)]
                )

        with jax.named_scope("pack_b"):
            over(body)

    def fold_half(h, store):
        with jax.named_scope("wait_b"):
            wait(pack_back, land_back, h, back_sems)

        def body(at):
            parts = [land_back[j, pl.ds(h * rows + at, step), :] for j in range(slabs)]
            for k in range(slabs):
                store(
                    pl.ds(k * rows + at, step),
                    merge([(parts[u % slabs], (u // slabs) * slabs + k) for u in range(slots)]),
                )

        with jax.named_scope("fold"):
            over(body)

    with jax.named_scope("pack"):
        pack_half(0)
    with jax.named_scope("barrier"):
        pl.semaphore_wait(barrier, slabs - 1 + orbs - 1)
    exchange(slabs, here, p_send, p_recv, lambda there: pot_ref, pot_land)
    send(pack, land, 0, out_sems)
    with jax.named_scope("pack"):
        pack_half(1)
    pot_land[here] = pot_ref[...]
    with jax.named_scope("level"):
        wait_exchange(slabs, here, p_send, p_recv, lambda there: pot_ref, pot_land)
        lane_slot = lax.broadcasted_iota(jnp.int32, (thin, LANES), 1) // width
        fields = [pot_land[s] for s in range(slabs)]
        for p in range(planes):
            for e in range(rows // thin):
                value = None
                for u in range(slots):
                    l = (2 * p + u % 2) * (rows // thin) + e
                    spread = jnp.broadcast_to(fields[u // 2][:, l : l + 1], (thin, LANES))
                    value = spread if value is None else jnp.where(lane_slot == u, spread, value)
                level[pl.ds(p * rows + e * thin, thin), :] = (
                    value - (SHIFT_MID + 1.5 * STENCIL[0])
                ) * (1.0 / HALF_WIDTH)

    starts, arrive, passed = link_orders()

    def along(way, origin, h):
        view = gath.at[origin * 2 + core, h * part_rows : (h + 1) * part_rows]
        return pltpu.make_async_remote_copy(
            src_ref=view,
            dst_ref=view,
            send_sem=along_send.at[way, origin * 2 + h],
            recv_sem=along_recv.at[way, origin * 2 + h],
            device_id={"orb": (chip + 1 - 2 * way) * 2 + core},
            device_id_type=MESH,
        )

    def direct(z):
        way, h = (0, 1) if z == 0 else (1, 0)
        view = gath.at[z * 2 + core, h * part_rows : (h + 1) * part_rows]
        return pltpu.make_async_remote_copy(
            src_ref=view,
            dst_ref=view,
            send_sem=direct_send.at[0],
            recv_sem=along_recv.at[way, z * 2 + h],
            device_id={"orb": (z + 2 - 4 * way) * 2 + core},
            device_id_type=MESH,
        )

    def across(origin, h, side):
        view = gath.at[origin * 2 + side, h * part_rows : (h + 1) * part_rows]
        return pltpu.make_async_remote_copy(
            src_ref=view,
            dst_ref=view,
            send_sem=across_send.at[origin * 2 + h],
            recv_sem=across_recv.at[origin * 2 + h],
            device_id={"orb": partner},
            device_id_type=MESH,
        )

    def on_chip(z, body):
        pl.when(chip == z)(body)

    def by_chip(table, body):
        for z in table:
            def run():
                for item in table[z]:
                    body(*item)

            on_chip(z, run)

    own_items = {z: [(0, z, h) for h in range(2)] for z in range(chips)}

    def begin():
        for z in (0, chips - 1):
            on_chip(z, lambda: direct(z).start())
        by_chip(starts, lambda *item: along(*item).start())
        by_chip(own_items, lambda way, o, h: across(o, h, core).start())

    def receive(t):
        def one(way, o, h):
            along(way, o, h).wait_recv()
            across(o, h, core).start()

        with jax.named_scope("receive"):
            by_chip(arrive[t], one)

    def forward(t):
        by_chip(passed[t], lambda *item: along(*item).start())

    def settle(t):
        with jax.named_scope("settle"):
            by_chip(arrive[t], lambda way, o, h: across(o, h, 1 - core).wait_recv())

    def settle_own():
        by_chip(own_items, lambda way, o, h: across(o, h, 1 - core).wait_recv())

    def drain():
        for z in (0, chips - 1):
            on_chip(z, lambda: direct(z).wait_send())
        for table in [starts] + passed:
            by_chip(table, lambda *item: along(*item).wait_send())
        for table in [own_items] + arrive:
            by_chip(table, lambda way, o, h: across(o, h, core).wait_send())

    filter_half(0)
    send(pack_back, land_back, 0, back_sems)

    def store_panel(at, value):
        gath[me, at, :] = value

    fold_half(0, store_panel)
    begin()

    filter_half(1)
    receive(0)
    forward(0)
    settle_own()
    settle(0)

    tiles = chips * (chips + 1) // 2
    share = tiles // 2
    block = share * LANES // slabs
    centre = (chip + 1) // 2 == 1

    def block_at(s):
        return pl.ds(pl.multiple_of(s * block, 8), block)

    def pair(z, at):
        return jnp.concatenate([gath[z * 2, at, :], gath[z * 2 + 1, at, :]], axis=1)

    @pl.when(centre)
    def _():
        at = pl.ds(pl.multiple_of((chip - 1) * part_rows, part_rows), part_rows)

        def tile(n, carry):
            t = core * share + n
            za = (t + 8) // 9 + (t + 6) // 9 + (t + 3) // 9
            zb = t - za * (za + 1) // 2
            product = dot_pieces(pieces(pair(za, at)), pieces(pair(zb, at)), (0, 0))
            for r, value in enumerate(unfolded(product, 2)):
                gram_part[pl.ds(pl.multiple_of(n * LANES + r * panel_dev, panel_dev), panel_dev), :] = value
            return carry

        with jax.named_scope("gram"):
            lax.fori_loop(0, share, tile, 0)
        exchange(slabs, here, r_send, r_recv, lambda there: gram_part.at[block_at(there)], gram_land)

    send(pack_back, land_back, 1, back_sems)

    def spread(index, there):
        view = gram_chip.at[index]
        return pltpu.make_async_remote_copy(
            src_ref=view,
            dst_ref=view,
            send_sem=z_send.at[there],
            recv_sem=z_recv.at[index],
            device_id={"orb": there * 2 + core},
            device_id_type=MESH,
        )

    @pl.when(centre)
    def _():
        with jax.named_scope("wait_r"):
            wait_exchange(slabs, here, r_send, r_recv, lambda there: gram_part.at[block_at(there)], gram_land)
        gram_land[here] = gram_part[block_at(here), :]
        total = gram_land[0]
        for s in range(1, slabs):
            total += gram_land[s]
        gram_chip[chip - 1] = total / points_all

    for z in range(1, 3):
        def body():
            for there in range(chips):
                if there != z:
                    spread(z - 1, there).start()

        on_chip(z, body)
    forward(1)

    with jax.named_scope("wait_z"):
        for z in range(chips):
            def body():
                for index in range(2):
                    if z != index + 1:
                        spread(index, z).wait_recv()
                    else:
                        for there in range(chips):
                            if there != z:
                                spread(index, there).wait_send()

            on_chip(z, body)
    gram_all[core, block_at(here), :] = gram_chip[0] + gram_chip[1]

    def gram_side(side, s):
        view = gram_all.at[side, block_at(s)]
        return pltpu.make_async_remote_copy(
            src_ref=view,
            dst_ref=view,
            send_sem=t_send.at[s],
            recv_sem=t_recv.at[s],
            device_id={"orb": partner},
            device_id_type=MESH,
        )

    def plane_copy(hop, s, there):
        view = gram_all.at[core, block_at(s)]
        return pltpu.make_async_remote_copy(
            src_ref=view,
            dst_ref=view,
            send_sem=s_send.at[hop],
            recv_sem=s_recv.at[hop],
            device_id={"space": there},
            device_id_type=MESH,
        )

    for hop in range(1, slabs):
        plane_copy(hop, here, lax.rem(here + hop, slabs)).start()
    gram_side(core, here).start()

    def store_rest(at, value):
        rest_ref[at, :] = value

    fold_half(1, store_rest)

    def couple(n, z):
        rows_k = 256
        with jax.named_scope("couple"):
            def product(k, total):
                at = pl.ds(pl.multiple_of(k * rows_k, rows_k), rows_k)
                return total + dot_pieces(pieces(rest_ref[at, :]), pieces(pair(z, at)), (0, 0))

            total = lax.fori_loop(
                0, fold // rows_k, product, jnp.zeros((LANES, 2 * LANES), jnp.float32)
            )
            value = unfolded(total, 1)[0]
            cross_part[n] = value
            cross_land[n, here] = value
        exchange(slabs, here, c_send.at[n], c_recv.at[n], lambda there: cross_part.at[n], cross_land.at[n])

    lower = chip // 2
    order = [chip, chip + 1 - 2 * lax.rem(chip, 2), 2 - lower, 3 - 3 * lower]
    receive(1)
    forward(2)
    with jax.named_scope("wait_s"):
        for hop in range(1, slabs):
            source = lax.rem(here + slabs - hop, slabs)
            plane_copy(hop, source, lax.rem(here + hop, slabs)).wait_recv()
            gram_side(core, source).start()
    couple(0, order[0])
    settle(1)
    with jax.named_scope("wait_t"):
        for s in range(slabs):
            gram_side(1 - core, s).wait_recv()

    n = LANES
    blocks = chips
    inverse[...] = jnp.zeros_like(inverse)
    for za in range(chips):
        for zb in range(za + 1):
            t = za * (za + 1) // 2 + zb
            work[za * n : (za + 1) * n, zb * n : (zb + 1) * n] = gram_all[
                t // share, (t % share) * n : (t % share + 1) * n, :
            ]

    def factor(b, carry):
        at = pl.multiple_of(b * n, n)
        with jax.named_scope("diag"):
            diag = block_inverse(work[pl.ds(at, n), pl.ds(at, n)])
            inverse[pl.ds(at, n), pl.ds(at, n)] = diag
        for i in range(1, blocks):
            @pl.when(i > b)
            def _():
                work[i * n : (i + 1) * n, pl.ds(at, n)] = dot(
                    work[i * n : (i + 1) * n, pl.ds(at, n)], diag, (1, 1)
                )
        for i in range(1, blocks):
            @pl.when(i > b)
            def _():
                left = work[i * n : (i + 1) * n, pl.ds(at, n)]
                for k in range(1, i + 1):
                    @pl.when(k > b)
                    def _():
                        right = work[k * n : (k + 1) * n, pl.ds(at, n)]
                        work[i * n : (i + 1) * n, k * n : (k + 1) * n] -= dot(left, right, (1, 1))

        @pl.when(b == 0)
        def _():
            receive(2)
            forward(3)
            couple(1, order[1])
            receive(3)

        @pl.when(b == 1)
        def _():
            settle(2)
            settle(3)
            couple(2, order[2])
            receive(4)

        @pl.when(b == 2)
        def _():
            settle(4)
            couple(3, order[3])

        return carry

    with jax.named_scope("factor"):
        lax.fori_loop(0, blocks, factor, 0)
    with jax.named_scope("inverse"):
        for i in range(1, blocks):
            span = i * n
            inner = dot(work[i * n : (i + 1) * n, :span], inverse[:span, :span], (1, 0))
            inverse[i * n : (i + 1) * n, :span] = -dot(
                inverse[i * n : (i + 1) * n, i * n : (i + 1) * n], inner, (1, 0)
            )

    with jax.named_scope("cross"):
        for k in range(chips):
            wait_exchange(
                slabs, here, c_send.at[k], c_recv.at[k], lambda there: cross_part.at[k], cross_land.at[k]
            )
            total = cross_land[k, 0]
            for s in range(1, slabs):
                total += cross_land[k, s]
            cross[:, pl.ds(pl.multiple_of(order[k] * LANES, LANES), LANES)] = total / points_all
    with jax.named_scope("weights"):
        middle = dot(cross[...], inverse[...], (1, 1))
        trail = -dot(middle, inverse[...], (1, 0))
        own = inverse[pl.ds(pl.multiple_of(me * panel_dev, panel_dev), panel_dev), :]
        turned = jnp.concatenate([own, trail], axis=0).T
        weight_ref[...] = jnp.zeros_like(weight_ref)
        for o in range(orbs):
            value = turned[o * panel_dev : (o + 1) * panel_dev]
            weight_ref[o * LANES : o * LANES + panel_dev, :LANES] = value
            weight_ref[o * LANES + panel_dev : (o + 1) * LANES, LANES:] = value
    drain()
    for hop in range(1, slabs):
        plane_copy(hop, here, lax.rem(here + hop, slabs)).wait_send()
    for s in range(slabs):
        gram_side(core, s).wait_send()


def final_kernel(gath_ref, rest_ref, weight_ref, out_ref, high, low):
    orbs, fold, n = gath_ref.shape
    rows = out_ref.shape[1]
    i = pl.program_id(0)

    @pl.when(i == 0)
    def _():
        high[...], low[...] = pieces(weight_ref[...])

    at = pl.ds(pl.multiple_of(i * rows, rows), rows)
    total = None
    for z in range(orbs // 2):
        k = slice(z * 2 * n, (z + 1) * 2 * n)
        pair = jnp.concatenate([gath_ref[z * 2, at, :], gath_ref[z * 2 + 1, at, :]], axis=1)
        value = dot_pieces(pieces(pair), (high[k, :], low[k, :]), (1, 0))
        total = value if total is None else total + value
    lanes = lax.broadcasted_iota(jnp.int32, (rows, n), 1)
    kept = rest_ref[at, :]
    for h in range(2):
        held = kept if h else pltpu.roll(kept, n // 2, 1)
        out_ref[h] = jnp.where(lanes < n // 2, 0.0, held) + total[:, h * n : (h + 1) * n]


def early_device(slabs, orbs, orbitals, potential):
    planes, rows_y, rows_z, columns = orbitals.shape
    points = planes * rows_y * rows_z
    panel_dev = PANEL // orbs
    chips = orbs // 2
    thin = points // LANES
    fold = points // 2
    tiles = chips * (chips + 1) // 2
    block = tiles // 2 * LANES // slabs
    f32 = jnp.float32
    vmem = pl.BlockSpec(memory_space=pltpu.VMEM)
    dma = pltpu.SemaphoreType.DMA
    gath, rest, weight = pl.pallas_call(
        functools.partial(early_kernel, slabs, orbs, (planes, rows_y, rows_z)),
        out_shape=[
            jax.ShapeDtypeStruct((orbs, fold, LANES), f32),
            jax.ShapeDtypeStruct((fold, LANES), f32),
            jax.ShapeDtypeStruct((orbs * LANES, 2 * LANES), f32),
        ],
        in_specs=[vmem] * 2,
        out_specs=[vmem] * 3,
        scratch_shapes=[pltpu.VMEM((slabs, points // slabs, LANES), f32)] * 4
        + [
            pltpu.VMEM((slabs, thin, LANES), f32),
            pltpu.VMEM((9 * points // 2, LANES), f32),
            pltpu.VMEM((9 * points // 2, LANES), f32),
            pltpu.VMEM((points // 2, LANES), f32),
            pltpu.VMEM((slabs * block, LANES), f32),
            pltpu.VMEM((slabs, block, LANES), f32),
            pltpu.VMEM((2, block, LANES), f32),
            pltpu.VMEM((2, slabs * block, LANES), f32),
            pltpu.VMEM((chips, panel_dev, LANES), f32),
            pltpu.VMEM((chips, slabs, panel_dev, LANES), f32),
            pltpu.VMEM((panel_dev, PANEL), f32),
            pltpu.VMEM((PANEL, PANEL), f32),
            pltpu.VMEM((PANEL, PANEL), f32),
        ]
        + [dma((slabs,))] * 10
        + [dma((2, orbs))] * 2
        + [dma((1,))]
        + [dma((orbs,))] * 2
        + [dma((slabs,))] * 2
        + [dma((chips,)), dma((2,))]
        + [dma((slabs,))] * 4
        + [dma((chips, slabs))] * 2,
        compiler_params=pltpu.CompilerParams(
            collective_id=0, has_side_effects=True, vmem_limit_bytes=40 << 20
        ),
    )(orbitals.reshape(points, columns), potential.reshape(LANES, thin).T)
    count = 4
    whole = [pl.BlockSpec(memory_space=pltpu.VMEM)] * 3
    out = pl.pallas_call(
        final_kernel,
        grid=(count,),
        out_shape=jax.ShapeDtypeStruct((2, fold, LANES), f32),
        in_specs=whole,
        out_specs=pl.BlockSpec((2, fold // count, LANES), lambda i: (0, i, 0)),
        scratch_shapes=[pltpu.VMEM((orbs * LANES, 2 * LANES), jnp.bfloat16)] * 2,
        compiler_params=pltpu.CompilerParams(vmem_limit_bytes=16 << 20),
    )(gath, rest, weight)
    return out.reshape(planes, rows_y, rows_z, columns)


def per_device(slabs, orbs, orbitals, potential):
    planes, rows_y, rows_z, columns = orbitals.shape
    points = planes * rows_y * rows_z
    panel_dev = PANEL // orbs
    folds = LANES // panel_dev
    thin = points // LANES
    f32 = jnp.float32
    vmem = pl.BlockSpec(memory_space=pltpu.VMEM)
    dma = pltpu.SemaphoreType.DMA
    steps = max(orbs // 2 - 1, 1)
    split = folds == 2 and planes == slabs and rows_y // 2 >= REACH and steps >= 2
    if split and orbs == 8 and PANEL == 4 * LANES and 5 * LANES % (8 * slabs) == 0:
        return early_device(slabs, orbs, orbitals, potential)
    flat = orbitals.reshape(points, columns)
    own, panel, gram, cross = pl.pallas_call(
        functools.partial(filter_kernel, slabs, orbs, (planes, rows_y, rows_z), split),
        out_shape=[
            jax.ShapeDtypeStruct((points, LANES), f32),
            jax.ShapeDtypeStruct((points, PANEL), f32),
            jax.ShapeDtypeStruct((PANEL, PANEL), f32),
            jax.ShapeDtypeStruct((LANES, PANEL), f32),
        ],
        in_specs=[vmem] * 2,
        out_specs=[vmem] * 4,
        scratch_shapes=[pltpu.VMEM((slabs, points // slabs, LANES), f32)] * 4
        + [
            pltpu.VMEM((slabs, thin, LANES), f32),
            pltpu.VMEM(((9 if split else 6) * points // 2, LANES), f32),
            pltpu.VMEM(((9 if split else 6) * points // 2, LANES), f32),
            pltpu.VMEM((points, LANES), f32),
            pltpu.VMEM((orbs, points // folds, LANES), f32),
            pltpu.VMEM((LANES, PANEL), f32),
            pltpu.VMEM((slabs, LANES, PANEL), f32),
            pltpu.VMEM((orbs, panel_dev, PANEL), f32),
        ]
        + [dma((slabs,))] * 14
        + [dma((2, steps))] * 2 + [dma((2 * steps + 1,))] * 2
        + [dma((2, steps))] * 2 + [dma((2 * steps + 1,))] * 2,
        compiler_params=pltpu.CompilerParams(
            collective_id=0, has_side_effects=True, vmem_limit_bytes=32 << 20
        ),
    )(flat, potential.reshape(LANES, thin).T)
    out = pl.pallas_call(
        functools.partial(solve_kernel, orbs),
        out_shape=jax.ShapeDtypeStruct((points, LANES), f32),
        in_specs=[vmem] * 4,
        out_specs=vmem,
        scratch_shapes=[
            pltpu.VMEM((PANEL, PANEL), f32),
            pltpu.VMEM((PANEL, PANEL), f32),
            pltpu.VMEM((LANES, PANEL), f32),
        ],
        compiler_params=pltpu.CompilerParams(vmem_limit_bytes=32 << 20),
    )(own, panel, gram, cross)
    return out.reshape(planes, rows_y, rows_z, columns)


def solution(mesh):
    placed = (P("space", None, None, "orb"), P("space", None, None))
    return jax.shard_map(
        functools.partial(per_device, mesh.shape["space"], mesh.shape["orb"]),
        mesh=mesh,
        in_specs=placed,
        out_specs=P("space", None, None, "orb"),
        check_vma=False,
    )
```

```python
import functools

import jax
import jax.numpy as jnp
from jax import lax
from jax.experimental import pallas as pl
from jax.experimental.pallas import tpu as pltpu
from jax.sharding import PartitionSpec as P

PANEL = 512
DEGREE = 4

STENCIL = (-205.0 / 72.0, 8.0 / 5.0, -1.0 / 5.0, 8.0 / 315.0, -1.0 / 560.0)
SHIFT_MID = 7.25
HALF_WIDTH = 4.75
LANES = 128
REACH = 4
MESH = pl.DeviceIdType.MESH
HIGHEST = lax.Precision.HIGHEST


def dot(a, b, dims):
    return lax.dot_general(
        a, b, ((dims[:1], dims[1:]), ((), ())), precision=HIGHEST, preferred_element_type=jnp.float32
    )


def regroup(load, store, count, rows):
    width = LANES // count
    step = min(rows, max(8, 128 // count))
    group = lax.broadcasted_iota(jnp.int32, (step, LANES), 1) // width

    def body(block, carry):
        here = pl.ds(pl.multiple_of(block * step, step), step)
        parts = [load(r, here) for r in range(count)]
        for j in range(count):
            out = None
            for r in range(count):
                turn = ((r - j) * width) % LANES
                piece = pltpu.roll(parts[r], turn, 1) if turn else parts[r]
                out = piece if out is None else jnp.where(group == r, piece, out)
            store(j, here, out)
        return carry

    lax.fori_loop(0, rows // step, body, 0)


def exchange(slots, here, send_sem, recv_sem, send, land):
    copies = []
    for hop in range(1, slots):
        there = lax.rem(here + hop, slots)
        copy = pltpu.make_async_remote_copy(
            src_ref=send(there),
            dst_ref=land.at[here],
            send_sem=send_sem.at[hop],
            recv_sem=recv_sem.at[hop],
            device_id={"space": there},
            device_id_type=MESH,
        )
        copy.start()
        copies.append(copy)
    return copies


def wait_exchange(slots, here, send_sem, recv_sem, send, land):
    for hop in range(1, slots):
        there = lax.rem(here + hop, slots)
        source = lax.rem(here + slots - hop, slots)
        pltpu.make_async_remote_copy(
            src_ref=send(there),
            dst_ref=land.at[source],
            send_sem=send_sem.at[hop],
            recv_sem=recv_sem.at[hop],
            device_id={"space": there},
            device_id_type=MESH,
        ).wait()


def gather_orb(count, me, buf, send_sem, recv_sem, side_send, side_recv, arrived=lambda chip: None, during=None):
    chips = count // 2
    chip, core = me // 2, lax.rem(me, 2)
    partner = chip * 2 + (1 - core)

    def along(origin, to, way, step):
        slot = buf.at[origin * 2 + core]
        return pltpu.make_async_remote_copy(
            src_ref=slot,
            dst_ref=slot,
            send_sem=send_sem.at[way, step],
            recv_sem=recv_sem.at[way, step],
            device_id={"orb": to * 2 + core},
            device_id_type=MESH,
        )

    def across(origin, side, index):
        slot = buf.at[origin * 2 + side]
        return pltpu.make_async_remote_copy(
            src_ref=slot,
            dst_ref=slot,
            send_sem=side_send.at[index],
            recv_sem=side_recv.at[index],
            device_id={"orb": partner},
            device_id_type=MESH,
        )

    steps = chips - 1

    def finish(step):
        @pl.when(chip - 1 - step >= 0)
        def _():
            across(chip - 1 - step, 1 - core, 1 + step).wait_recv()
            arrived(chip - 1 - step)

        @pl.when(chip + 1 + step < chips)
        def _():
            across(chip + 1 + step, 1 - core, 1 + steps + step).wait_recv()
            arrived(chip + 1 + step)

    for step in range(steps):
        @pl.when((chip - step >= 0) & (chip + 1 < chips))
        def _():
            along(chip - step, chip + 1, 0, step).start()

        @pl.when((chip + step < chips) & (chip - 1 >= 0))
        def _():
            along(chip + step, chip - 1, 1, step).start()

        if step == 0:
            across(chip, core, 0).start()
            if during:
                during[0]()
        if step == (1 if during else 0):
            if during:
                during[1]()
            across(chip, 1 - core, 0).wait_recv()
            arrived(chip)
        if step:
            finish(step - 1)

        @pl.when(chip - 1 - step >= 0)
        def _():
            along(chip - 1 - step, chip, 0, step).wait_recv()
            across(chip - 1 - step, core, 1 + step).start()

        @pl.when(chip + 1 + step < chips)
        def _():
            along(chip + 1 + step, chip, 1, step).wait_recv()
            across(chip + 1 + step, core, 1 + steps + step).start()

    finish(steps - 1)
    across(chip, core, 0).wait_send()
    for step in range(steps):
        @pl.when((chip - step >= 0) & (chip + 1 < chips))
        def _():
            along(chip - step, chip + 1, 0, step).wait_send()

        @pl.when((chip + step < chips) & (chip - 1 >= 0))
        def _():
            along(chip + step, chip - 1, 1, step).wait_send()

        @pl.when(chip - 1 - step >= 0)
        def _():
            across(chip - 1 - step, core, 1 + step).wait_send()

        @pl.when(chip + 1 + step < chips)
        def _():
            across(chip + 1 + step, core, 1 + steps + step).wait_send()


def split_filter(
    slabs, shape, here, me, x_ref, pot_ref, own_ref, pack, land, pack_back, land_back, pot_land,
    wide_a, wide_b, level, gath, out_sems, pot_sems, back_sems,
):
    planes, rows_y, rows_z = shape
    points = planes * rows_y * rows_z
    slots = 2 * slabs
    width = LANES // slots
    rows = points // slots
    plane = 3 * rows
    thin = points // LANES
    step = 16
    slot = lax.broadcasted_iota(jnp.int32, (step, LANES), 1) // width

    def merge(parts):
        out = None
        for u, (value, v) in enumerate(parts):
            turn = ((u - v) * width) % LANES
            value = pltpu.roll(value, turn, 1) if turn else value
            out = value if out is None else jnp.where(slot == u, value, out)
        return out

    def over(body):
        def one(block, carry):
            body(pl.multiple_of(block * step, step))
            return carry

        lax.fori_loop(0, rows // step, one, 0)

    def half(buf, h):
        return buf.at[:, h * rows : (h + 1) * rows]

    def send(buf, landing, h, sems):
        exchange(slabs, here, *sems[h], lambda there: half(buf, h).at[there], half(landing, h))
        landing[here, h * rows : (h + 1) * rows] = buf[here, h * rows : (h + 1) * rows]

    def wait(buf, landing, h, sems):
        wait_exchange(slabs, here, *sems[h], lambda there: half(buf, h).at[there], half(landing, h))

    def pack_half(h):
        def body(at):
            parts = [x_ref[pl.ds(q * rows + at, step), :] for q in range(slots)]
            for j in range(slabs):
                pack[j, pl.ds(h * rows + at, step), :] = merge([(part, h * slabs + j) for part in parts])

        over(body)
        send(pack, land, h, out_sems)

    def put(target, p, row, value):
        odd = lax.rem(lax.broadcasted_iota(jnp.int32, value.shape, 1) // width, 2)
        size = value.shape[0]
        swapped = jnp.where(odd == 0, pltpu.roll(value, LANES - width, 1), pltpu.roll(value, width, 1))
        target[pl.ds((planes + p) * plane + rows + row, size), :] = value
        target[pl.ds((planes + p) * plane + row, size), :] = swapped
        target[pl.ds((planes + p) * plane + 2 * rows + row, size), :] = swapped
        target[pl.ds(p * plane + rows + row, size), :] = pltpu.roll(value, 2 * width, 1)
        target[pl.ds((2 * planes + p) * plane + rows + row, size), :] = pltpu.roll(value, LANES - 2 * width, 1)

    taps = [-0.5 * c / HALF_WIDTH for c in STENCIL]

    def sweep(source, target, first):
        def body(y, carry):
            for p in range(planes):
                def line(q, yy):
                    row = pl.multiple_of((planes + q) * plane + rows + yy * rows_z, rows_z)
                    return source[pl.ds(row, rows_z), :]

                row = pl.multiple_of(y * rows_z, rows_z)
                centre = line(p, y)
                total = level[pl.ds(p * rows + row, rows_z), :] * centre
                for m in range(1, REACH + 1):
                    near = line(p + m, y) + line(p - m, y) + line(p, y + m) + line(p, y - m)
                    near += pltpu.roll(centre, m, 0) + pltpu.roll(centre, rows_z - m, 0)
                    total += taps[m] * near
                if not first:
                    total = 2.0 * total - target[pl.ds((planes + p) * plane + rows + row, rows_z), :]
                put(target, p, row, total)
            return carry

        lax.fori_loop(0, rows_y // 2, body, 0)

    def filter_half(h):
        wait(pack, land, h, out_sems)

        def unpack(at):
            parts = [land[i, pl.ds(h * rows + at, step), :] for i in range(slabs)]
            for p in range(planes):
                put(wide_a, p, at, merge([(parts[u // 2], 2 * p + u % 2) for u in range(slots)]))

        over(unpack)
        sweep(wide_a, wide_b, True)
        source, target = wide_b, wide_a
        for _ in range(DEGREE - 1):
            sweep(source, target, False)
            source, target = target, source

        def body(at):
            parts = [source[pl.ds((planes + p) * plane + rows + at, step), :] for p in range(planes)]
            for i in range(slabs):
                pack_back[i, pl.ds(h * rows + at, step), :] = merge(
                    [(parts[q // 2], 2 * i + q % 2) for q in range(slots)]
                )

        over(body)
        send(pack_back, land_back, h, back_sems)

    pack_half(0)
    pack_half(1)
    pot_land[here] = pot_ref[...]
    wait_exchange(slabs, here, *pot_sems, lambda there: pot_ref, pot_land)
    lane_slot = lax.broadcasted_iota(jnp.int32, (thin, LANES), 1) // width
    fields = [pot_land[s] for s in range(slabs)]
    pieces = rows // thin
    for p in range(planes):
        for e in range(pieces):
            value = None
            for u in range(slots):
                l = (2 * p + u % 2) * pieces + e
                spread = jnp.broadcast_to(fields[u // 2][:, l : l + 1], (thin, LANES))
                value = spread if value is None else jnp.where(lane_slot == u, spread, value)
            level[pl.ds(p * rows + e * thin, thin), :] = (
                value - (SHIFT_MID + 1.5 * STENCIL[0])
            ) * (1.0 / HALF_WIDTH)

    filter_half(0)
    wait(pack_back, land_back, 0, back_sems)

    def fold_own(at):
        parts = [land_back[j, pl.ds(at, step), :] for j in range(slabs)]
        for k in range(slabs):
            gath[me, pl.ds(k * rows + at, step), :] = merge(
                [(parts[u % slabs], (u // slabs) * slabs + k) for u in range(slots)]
            )

    over(fold_own)

    def finish():
        wait(pack_back, land_back, 1, back_sems)

        def body(at):
            parts = [
                land_back[u % slabs, pl.ds((u // slabs) * rows + at, step), :] for u in range(slots)
            ]
            for q in range(slots):
                own_ref[pl.ds(q * rows + at, step), :] = merge([(part, q) for part in parts])

        over(body)

    return (lambda: filter_half(1)), finish


def filter_kernel(
    slabs, orbs, shape, split,
    x_ref, pot_ref, own_ref, panel_ref, gram_ref, cross_ref,
    pack, land, pack_back, land_back, pot_land, wide_a, wide_b, level, gath, part, part_land, rows_land,
    a_send, a_recv, p_send, p_recv, b_send, b_recv, c_send, c_recv, d_send, d_recv, e_send, e_recv, f_send, f_recv,
    g_send, g_recv, gs_send, gs_recv, h_send, h_recv, hs_send, hs_recv,
):
    planes, rows_y, rows_z = shape
    points = planes * rows_y * rows_z
    here, me = lax.axis_index("space"), lax.axis_index("orb")
    chunk = points // slabs
    width = LANES // slabs

    barrier = pltpu.get_barrier_semaphore()
    for hop in range(1, slabs):
        pl.semaphore_signal(
            barrier, inc=1, device_id={"space": lax.rem(here + hop, slabs)}, device_id_type=MESH
        )
    for hop in range(1, orbs):
        pl.semaphore_signal(
            barrier, inc=1, device_id={"orb": lax.rem(me + hop, orbs)}, device_id_type=MESH
        )
    pl.semaphore_wait(barrier, slabs - 1 + orbs - 1)

    exchange(slabs, here, p_send, p_recv, lambda there: pot_ref, pot_land)

    panel_dev = PANEL // orbs
    folds = LANES // panel_dev
    fold = points // folds
    during = None
    if split:
        during = split_filter(
            slabs, shape, here, me, x_ref, pot_ref, own_ref, pack, land, pack_back, land_back, pot_land,
            wide_a, wide_b, level, gath,
            ((a_send, a_recv), (e_send, e_recv)), (p_send, p_recv), ((b_send, b_recv), (f_send, f_recv)),
        )
    else:
        def store_pack(j, at, value):
            pack[j, at, :] = value

        regroup(lambda r, at: x_ref[pl.ds(r * chunk + at.start, at.size), :], store_pack, slabs, chunk)
        exchange(slabs, here, a_send, a_recv, lambda there: pack.at[there], land)
        land[here] = pack[here]
        pot_land[here] = pot_ref[...]
        wait_exchange(slabs, here, p_send, p_recv, lambda there: pot_ref, pot_land)

        thin = points // LANES
        lane_group = lax.broadcasted_iota(jnp.int32, (thin, LANES), 1) // width
        fields = [pot_land[s] for s in range(slabs)]
        for l in range(LANES):
            value = None
            for s in range(slabs):
                spread = jnp.broadcast_to(fields[s][:, l : l + 1], (thin, LANES))
                value = spread if value is None else jnp.where(lane_group == s, spread, value)
            level[pl.ds(l * thin, thin), :] = (value - (SHIFT_MID + 1.5 * STENCIL[0])) * (1.0 / HALF_WIDTH)

        wait_exchange(slabs, here, a_send, a_recv, lambda there: pack.at[there], land)

        def put(target, row, value):
            target[pl.ds(points + row, value.shape[0]), :] = value
            target[pl.ds(row, value.shape[0]), :] = pltpu.roll(value, width, 1)
            target[pl.ds(2 * points + row, value.shape[0]), :] = pltpu.roll(value, LANES - width, 1)

        regroup(
            lambda r, at: land[r, at, :],
            lambda j, at, value: put(wide_a, j * chunk + at.start, value),
            slabs, chunk,
        )

        plane = rows_y * rows_z
        taps = [-0.5 * c / HALF_WIDTH for c in STENCIL]

        def sweep(source, target, first):
            def body(y, carry):
                for p in range(planes):
                    def line(q, yy):
                        return source[pl.ds(pl.multiple_of(points + q * plane + yy * rows_z, rows_z), rows_z), :]

                    row = pl.multiple_of(p * plane + y * rows_z, rows_z)
                    centre = line(p, y)
                    total = level[pl.ds(row, rows_z), :] * centre
                    for m in range(1, REACH + 1):
                        near = line(p + m, y) + line(p - m, y)
                        near += line(p, lax.rem(y + m, rows_y)) + line(p, lax.rem(y + rows_y - m, rows_y))
                        near += pltpu.roll(centre, m, 0) + pltpu.roll(centre, rows_z - m, 0)
                        total += taps[m] * near
                    if not first:
                        before = target[pl.ds(pl.multiple_of(points + row, rows_z), rows_z), :]
                        total = 2.0 * total - before
                    put(target, row, total)
                return carry

            lax.fori_loop(0, rows_y, body, 0)

        sweep(wide_a, wide_b, True)
        source, target = wide_b, wide_a
        for _ in range(DEGREE - 1):
            sweep(source, target, False)
            source, target = target, source

        def store_back(j, at, value):
            pack_back[j, at, :] = value

        regroup(
            lambda r, at: source[pl.ds(points + r * chunk + at.start, at.size), :], store_back, slabs, chunk
        )
        exchange(slabs, here, b_send, b_recv, lambda there: pack_back.at[there], land_back)
        land_back[here] = pack_back[here]
        wait_exchange(slabs, here, b_send, b_recv, lambda there: pack_back.at[there], land_back)

        def store_own(j, at, value):
            own_ref[pl.ds(j * chunk + at.start, at.size), :] = value

        regroup(lambda r, at: land_back[r, at, :], store_own, slabs, chunk)

        step = min(fold, 32)
        fold_group = lax.broadcasted_iota(jnp.int32, (step, LANES), 1) // panel_dev

        def folded(block, carry):
            at = pl.multiple_of(block * step, step)
            out = None
            for r in range(folds):
                piece = own_ref[pl.ds(r * fold + at, step), :]
                piece = pltpu.roll(piece, r * panel_dev, 1) if r else piece
                out = piece if out is None else jnp.where(fold_group == r, piece, out)
            gath[me, pl.ds(at, step), :] = out
            return carry

        lax.fori_loop(0, fold // step, folded, 0)

    block = 512

    def take(tile):
        lanes = pl.ds(pl.multiple_of(tile * LANES, LANES), LANES)

        def store_panel(j, at, value):
            panel_ref[pl.ds(j * fold + at.start, at.size), lanes] = value

        regroup(lambda r, at: gath[tile * folds + r, at, :], store_panel, folds, fold)

        def product(k, total):
            at = pl.ds(pl.multiple_of(k * block, block), block)
            return total + dot(own_ref[at, :], panel_ref[at, lanes], (0, 0))

        part[:, lanes] = lax.fori_loop(
            0, points // block, product, jnp.zeros((LANES, LANES), jnp.float32)
        )

    if folds == 2:
        gather_orb(orbs, me, gath, g_send, g_recv, gs_send, gs_recv, take, during)
    else:
        gather_orb(orbs, me, gath, g_send, g_recv, gs_send, gs_recv)

        def each(tile, carry):
            take(tile)
            return carry

        lax.fori_loop(0, PANEL // LANES, each, 0)

    top, rest = part.at[:panel_dev], part.at[panel_dev:]
    top_land, rest_land = part_land.at[:, :panel_dev], part_land.at[:, panel_dev:]
    exchange(slabs, here, c_send, c_recv, lambda there: top, top_land)
    exchange(slabs, here, d_send, d_recv, lambda there: rest, rest_land)
    part_land[here] = part[...]
    points_all = points * slabs

    def summed(view):
        total = view[0]
        for s in range(1, slabs):
            total += view[s]
        return total / points_all

    wait_exchange(slabs, here, c_send, c_recv, lambda there: top, top_land)
    rows_land[me] = summed(top_land)
    gather_orb(orbs, me, rows_land, h_send, h_recv, hs_send, hs_recv)
    wait_exchange(slabs, here, d_send, d_recv, lambda there: rest, rest_land)
    cross_ref[:panel_dev, :] = jnp.zeros((panel_dev, PANEL), jnp.float32)
    cross_ref[panel_dev:, :] = summed(rest_land)
    for o in range(orbs):
        gram_ref[o * panel_dev : (o + 1) * panel_dev, :] = rows_land[o]


def block_inverse(a):
    n = LANES
    tiles = n // 8
    rows = lax.broadcasted_iota(jnp.int32, (8, n), 0)
    cols = lax.broadcasted_iota(jnp.int32, (8, n), 1)
    work = [a[8 * t : 8 * t + 8] for t in range(tiles)]
    unit = [jnp.where(rows + 8 * t == cols, 1.0, 0.0).astype(jnp.float32) for t in range(tiles)]
    for t0 in range(tiles):
        base = 8 * t0
        columns = [jnp.broadcast_to(work[t0][:, base + k : base + k + 1], (8, n)) for k in range(8)]
        small = {
            (i, k): jnp.broadcast_to(columns[k][i : i + 1], (8, n)) for i in range(8) for k in range(i + 1)
        }
        lower, scales = {}, []
        for j in range(8):
            scales.append(1.0 / small[j, j])
            for i in range(j + 1, 8):
                lower[i, j] = small[i, j] * scales[j]
            for i in range(j + 1, 8):
                for k in range(j + 1, i + 1):
                    small[i, k] = small[i, k] - lower[i, j] * small[k, j]
        turned = {}
        for j in range(8):
            for i in range(j + 1, 8):
                value = lower[i, j]
                for k in range(j + 1, i):
                    value = value + lower[i, k] * turned[k, j]
                turned[i, j] = -value
        a_row, u_row = work[t0], unit[t0]
        a_new, u_new = a_row, u_row
        for k in range(7):
            weight = jnp.zeros((8, n), jnp.float32)
            for i in range(k + 1, 8):
                weight = jnp.where(rows == i, turned[i, k], weight)
            a_new = a_new + weight * jnp.broadcast_to(a_row[k : k + 1], (8, n))
            u_new = u_new + weight * jnp.broadcast_to(u_row[k : k + 1], (8, n))
        work[t0], unit[t0] = a_new, u_new
        if t0 == tiles - 1:
            break
        a_out = u_out = None
        for i in range(8):
            weight = jnp.where(rows == i, scales[i], 0.0)
            for k in range(i):
                weight = jnp.where(rows == k, turned[i, k] * scales[i], weight)
            a_term = weight * jnp.broadcast_to(a_new[i : i + 1], (8, n))
            u_term = weight * jnp.broadcast_to(u_new[i : i + 1], (8, n))
            a_out = a_term if a_out is None else a_out + a_term
            u_out = u_term if u_out is None else u_out + u_term
        a_rows = [jnp.broadcast_to(a_out[k : k + 1], (8, n)) for k in range(8)]
        u_rows = [jnp.broadcast_to(u_out[k : k + 1], (8, n)) for k in range(8)]
        for t in range(t0 + 1, tiles):
            before = work[t]
            for k in range(8):
                column = jnp.broadcast_to(before[:, base + k : base + k + 1], (8, n))
                work[t] = work[t] - column * a_rows[k]
                unit[t] = unit[t] - column * u_rows[k]
    out = []
    for t in range(tiles):
        pivots = jnp.sum(jnp.where(rows + 8 * t == cols, work[t], 0.0), axis=1, keepdims=True)
        out.append(unit[t] * (1.0 / jnp.sqrt(pivots)))
    return jnp.concatenate(out, axis=0)


def solve_kernel(orbs, own_ref, panel_ref, gram_ref, cross_ref, out_ref, work, inverse, weights):
    panel_dev = PANEL // orbs
    me = lax.axis_index("orb")
    n = LANES
    blocks = PANEL // n
    work[...] = gram_ref[...]
    inverse[...] = jnp.zeros_like(inverse)

    def factor(b, carry):
        at = pl.multiple_of(b * n, n)
        diag = block_inverse(work[pl.ds(at, n), pl.ds(at, n)])
        inverse[pl.ds(at, n), pl.ds(at, n)] = diag
        for i in range(1, blocks):
            @pl.when(i > b)
            def _():
                work[i * n : (i + 1) * n, pl.ds(at, n)] = dot(
                    work[i * n : (i + 1) * n, pl.ds(at, n)], diag, (1, 1)
                )
        for i in range(1, blocks):
            @pl.when(i > b)
            def _():
                left = work[i * n : (i + 1) * n, pl.ds(at, n)]
                for k in range(1, i + 1):
                    @pl.when(k > b)
                    def _():
                        right = work[k * n : (k + 1) * n, pl.ds(at, n)]
                        work[i * n : (i + 1) * n, k * n : (k + 1) * n] -= dot(left, right, (1, 1))
        return carry

    lax.fori_loop(0, blocks, factor, 0)
    for i in range(1, blocks):
        span = i * n
        inner = dot(work[i * n : (i + 1) * n, :span], inverse[:span, :span], (1, 0))
        inverse[i * n : (i + 1) * n, :span] = -dot(
            inverse[i * n : (i + 1) * n, i * n : (i + 1) * n], inner, (1, 0)
        )

    middle = dot(cross_ref[...], inverse[...], (1, 1))
    weights[...] = -dot(middle, inverse[...], (1, 0))
    weights[:panel_dev, :] = inverse[pl.ds(pl.multiple_of(me * panel_dev, panel_dev), panel_dev), :]
    points = own_ref.shape[0]
    block = 256
    lanes = lax.broadcasted_iota(jnp.int32, (block, LANES), 1)

    def final(k, carry):
        at = pl.ds(pl.multiple_of(k * block, block), block)
        kept = jnp.where(lanes < panel_dev, 0.0, own_ref[at, :])
        out_ref[at, :] = kept + dot(panel_ref[at, :], weights[...], (1, 1))
        return carry

    lax.fori_loop(0, points // block, final, 0)


def pieces(x):
    high = x.astype(jnp.bfloat16)
    return high, (x - high.astype(jnp.float32)).astype(jnp.bfloat16)


def dot_pieces(a, b, dims):
    def one(left, right):
        return lax.dot_general(
            left, right, ((dims[:1], dims[1:]), ((), ())), preferred_element_type=jnp.float32
        )

    return one(a[0], b[0]) + (one(a[0], b[1]) + one(a[1], b[0]))


def unfolded(product, rows):
    half = LANES // 2
    lanes = lax.broadcasted_iota(jnp.int32, (half, LANES), 1)
    out = []
    for r in range(rows):
        sides = []
        for c in range(2):
            at = product[r * LANES : (r + 1) * LANES, c * LANES : (c + 1) * LANES]
            sides.append(at[:half] + pltpu.roll(at[half:], half, 1))
        out.append(jnp.where(lanes < half, sides[0], pltpu.roll(sides[1], half, 1)))
    return out


def link_orders():
    def both(table):
        out = {z: list(items) for z, items in table.items()}
        for z, items in table.items():
            out[3 - z] = [(1 - way, 3 - o, 1 - h) for way, o, h in items]
        return out

    starts = [
        {0: [(0, 0, 0)], 1: [(1, 1, 0)], 2: [(1, 2, 0), (0, 2, 0)]},
        {0: [(0, 0, 1)], 1: [(0, 1, 1), (1, 1, 1)], 2: [(0, 2, 1)], 3: [(1, 3, 1), (1, 3, 0)]},
    ]
    arrive = [
        both({1: [(1, 2, 0)]}),
        both({0: [(1, 1, 0), (1, 1, 1)], 1: [(0, 0, 0), (1, 3, 0)]}),
        both({0: [(1, 2, 0)], 1: [(0, 0, 1), (1, 2, 1)]}),
        both({0: [(1, 3, 0)], 1: [(1, 3, 1)]}),
        both({0: [(1, 2, 1)]}),
        both({0: [(1, 3, 1)]}),
    ]
    passed = [
        both({1: [(1, 2, 0)]}),
        both({1: [(0, 1, 0)]}),
        both({1: [(0, 0, 0), (1, 3, 0)]}),
        both({1: [(1, 2, 1)]}),
        both({1: [(1, 3, 1)]}),
    ]
    return starts, arrive, passed


def tile_inverse(a):
    n = LANES
    tiles = n // 8
    rows = lax.broadcasted_iota(jnp.int32, (8, n), 0)
    lanes = lax.broadcasted_iota(jnp.int32, (8, n), 1)

    def row_of(value, k):
        return jnp.broadcast_to(value[k : k + 1], (8, n))

    def column_of(value, k):
        return jnp.broadcast_to(value[:, k : k + 1], (8, n))

    def tree(terms):
        while len(terms) > 1:
            paired = [terms[i] + terms[i + 1] for i in range(0, len(terms) - 1, 2)]
            terms = paired + terms[len(terms) - len(terms) % 2 :]
        return terms[0]

    work = [a[8 * t : 8 * t + 8] for t in range(tiles)]
    cols = [column_of(work[0], k) for k in range(8)]
    out = []
    for t0 in range(tiles):
        base = 8 * t0
        last = t0 == tiles - 1
        if not last:
            side = [column_of(work[t0 + 1], base + k) for k in range(8)]
            ahead = [column_of(work[t0 + 1], base + 8 + k) for k in range(8)]
            moved = list(side)
        below, pivots, scales = [], [], []
        for j in range(8):
            pivot = row_of(cols[j], j)
            scale = 1.0 / pivot
            lead = jnp.where(rows > j, cols[j], 0.0)
            pivots.append(pivot)
            scales.append(scale)
            below.append(lead * scale)
            for k in range(j + 1, 8):
                part = row_of(cols[k], j) * scale
                cols[k] = cols[k] - lead * part
                if not last:
                    moved[k] = moved[k] - moved[j] * part
        above = cols
        if not last:
            scaled = [moved[j] * scales[j] for j in range(8)]
            cols = [
                ahead[k] - tree([scaled[j] * row_of(moved[j], k) for j in range(8)]) for k in range(8)
            ]
        inside = (lanes >= base) & (lanes < base + 8)
        value = jnp.where(inside, jnp.where(lanes == rows + base, 1.0, 0.0), work[t0])
        root, turn = pivots[0], scales[0]
        for j in range(8):
            value = value - below[j] * row_of(value, j)
            if j:
                root = jnp.where(rows == j, pivots[j], root)
                turn = jnp.where(rows == j, scales[j], turn)
        out.append(jnp.where(lanes < base + 8, value * lax.rsqrt(root), 0.0))
        if last:
            break
        value = value * turn
        for k in range(7, 0, -1):
            value = value - jnp.where(rows < k, above[k] * turn, 0.0) * row_of(value, k)
        leads = [row_of(value, k) for k in range(8)]
        for t in range(t0 + 1, tiles):
            before = work[t]
            columns = side if t == t0 + 1 else [column_of(before, base + k) for k in range(8)]
            work[t] = jnp.where(inside, 0.0, before) - tree([columns[k] * leads[k] for k in range(8)])
    return jnp.concatenate(out, axis=0)


def early_kernel(
    slabs, orbs, shape,
    x_hbm, pot_ref, gath, rest_ref, weight_ref,
    x_ref, pot_wide, pot_mine, pack, land, pack_back, land_back, pot_land, wide_a, wide_b, level,
    gram_part, gram_land, gram_chip, gram_all, cross_part, cross_land, cross, work, inverse,
    x_sem, a_send, a_recv, p_send, p_recv, b_send, b_recv,
    along_send, along_recv, direct_send, across_send, across_recv,
    r_send, r_recv, z_send, z_recv, s_send, s_recv, t_send, t_recv, c_send, c_recv,
):
    planes, rows_y, rows_z = shape
    points = planes * rows_y * rows_z
    here, me = lax.axis_index("space"), lax.axis_index("orb")
    chips = orbs // 2
    chip, core = me // 2, lax.rem(me, 2)
    partner = chip * 2 + (1 - core)
    slots = 2 * slabs
    width = LANES // slots
    rows = points // slots
    plane = 3 * rows
    sub = rows // 2
    fold = points // 2
    part_rows = fold // 2
    panel_dev = PANEL // orbs
    points_all = points * slabs
    step = 16
    slot = lax.broadcasted_iota(jnp.int32, (step, LANES), 1) // width

    def fetch(c):
        view = slice(c * sub, (c + 1) * sub)
        return pltpu.make_async_copy(x_hbm.at[:, view], x_ref.at[:, view], x_sem.at[c])

    for c in range(2):
        fetch(c).start()

    barrier = pltpu.get_barrier_semaphore()
    for hop in range(1, slabs):
        pl.semaphore_signal(
            barrier, inc=1, device_id={"space": lax.rem(here + hop, slabs)}, device_id_type=MESH
        )
    for hop in range(1, orbs):
        pl.semaphore_signal(
            barrier, inc=1, device_id={"orb": lax.rem(me + hop, orbs)}, device_id_type=MESH
        )

    def merge(parts):
        out = None
        for u, (value, v) in enumerate(parts):
            turn = ((u - v) * width) % LANES
            value = pltpu.roll(value, turn, 1) if turn else value
            out = value if out is None else jnp.where(slot == u, value, out)
        return out

    def over(c, body):
        def one(block, carry):
            body(pl.multiple_of(c * sub + block * step, step))
            return carry

        lax.fori_loop(0, sub // step, one, 0)

    def span(h, c):
        return slice(h * rows + c * sub, h * rows + (c + 1) * sub)

    def send(buf, landing, h, c, sems):
        at, k = span(h, c), h * 2 + c
        exchange(
            slabs, here, sems[0].at[k], sems[1].at[k], lambda there: buf.at[there, at], landing.at[:, at]
        )
        landing[here, at] = buf[here, at]

    def wait(buf, landing, h, c, sems):
        at, k = span(h, c), h * 2 + c
        wait_exchange(
            slabs, here, sems[0].at[k], sems[1].at[k], lambda there: buf.at[there, at], landing.at[:, at]
        )

    out_sems, back_sems = (a_send, a_recv), (b_send, b_recv)

    def pack_part(h, c):
        def body(at):
            parts = [x_ref[q, pl.ds(at, step), :] for q in range(slots)]
            for j in range(slabs):
                pack[j, pl.ds(h * rows + at, step), :] = merge([(part, h * slabs + j) for part in parts])

        with jax.named_scope("pack"):
            over(c, body)

    def put(target, p, row, value):
        odd = lax.rem(lax.broadcasted_iota(jnp.int32, value.shape, 1) // width, 2)
        size = value.shape[0]
        swapped = jnp.where(odd == 0, pltpu.roll(value, LANES - width, 1), pltpu.roll(value, width, 1))
        target[pl.ds((planes + p) * plane + rows + row, size), :] = value
        target[pl.ds((planes + p) * plane + row, size), :] = swapped
        target[pl.ds((planes + p) * plane + 2 * rows + row, size), :] = swapped
        target[pl.ds(p * plane + rows + row, size), :] = pltpu.roll(value, 2 * width, 1)
        target[pl.ds((2 * planes + p) * plane + rows + row, size), :] = pltpu.roll(value, LANES - 2 * width, 1)

    taps = [-0.5 * c / HALF_WIDTH for c in STENCIL]

    def sweep(source, target, first, low=0, high=rows_y // 2):
        def body(y, carry):
            for p in range(planes):
                def line(q, yy):
                    row = pl.multiple_of((planes + q) * plane + rows + yy * rows_z, rows_z)
                    return source[pl.ds(row, rows_z), :]

                row = pl.multiple_of(y * rows_z, rows_z)
                centre = line(p, y)
                total = level[pl.ds(p * rows + row, rows_z), :] * centre
                for m in range(1, REACH + 1):
                    near = line(p + m, y) + line(p - m, y) + line(p, y + m) + line(p, y - m)
                    near += pltpu.roll(centre, m, 0) + pltpu.roll(centre, rows_z - m, 0)
                    total += taps[m] * near
                if not first:
                    total = 2.0 * total - target[pl.ds((planes + p) * plane + rows + row, rows_z), :]
                put(target, p, row, total)
            return carry

        lax.fori_loop(low, high, body, 0)

    def filter_half(h, during, ready):
        for c in range(2):
            with jax.named_scope("wait_a"):
                wait(pack, land, h, c, out_sems)

            def unpack(at):
                parts = [land[i, pl.ds(h * rows + at, step), :] for i in range(slabs)]
                for p in range(planes):
                    put(wide_a, p, at, merge([(parts[u // 2], 2 * p + u % 2) for u in range(slots)]))

            with jax.named_scope("unpack"):
                over(c, unpack)
        during[0]()
        source, target = wide_a, wide_b
        with jax.named_scope("sweep"):
            for order in range(DEGREE - 1):
                if order == 2:
                    during[1]()
                sweep(source, target, order == 0)
                source, target = target, source
        for c in range(2):
            with jax.named_scope("sweep"):
                sweep(source, target, False, c * rows_y // 4, (c + 1) * rows_y // 4)

            def body(at):
                parts = [target[pl.ds((planes + p) * plane + rows + at, step), :] for p in range(planes)]
                for i in range(slabs):
                    pack_back[i, pl.ds(h * rows + at, step), :] = merge(
                        [(parts[q // 2], 2 * i + q % 2) for q in range(slots)]
                    )

            with jax.named_scope("pack_b"):
                over(c, body)
            ready(c)

    def fold_part(h, c, store):
        with jax.named_scope("wait_b"):
            wait(pack_back, land_back, h, c, back_sems)

        def body(at):
            parts = [land_back[j, pl.ds(h * rows + at, step), :] for j in range(slabs)]
            for k in range(slabs):
                row = pl.multiple_of(c * part_rows + k * sub + at - c * sub, step)
                store(
                    pl.ds(row, step),
                    merge([(parts[u % slabs], (u // slabs) * slabs + k) for u in range(slots)]),
                )

        with jax.named_scope("fold"):
            over(c, body)

    pot_wide[...] = jnp.zeros_like(pot_wide)
    pot_wide[: planes * rows_y, :rows_z] = pot_ref[...]
    pot_mine[...] = pot_wide[...].T[:rows_z]
    fetch(0).wait()
    pack_part(0, 0)
    with jax.named_scope("barrier"):
        pl.semaphore_wait(barrier, slabs - 1 + orbs - 1)
    exchange(slabs, here, p_send, p_recv, lambda there: pot_mine, pot_land)
    send(pack, land, 0, 0, out_sems)
    fetch(1).wait()
    pack_part(0, 1)
    send(pack, land, 0, 1, out_sems)
    for c in range(2):
        pack_part(1, c)
    pot_land[here] = pot_mine[...]
    with jax.named_scope("level"):
        wait_exchange(slabs, here, p_send, p_recv, lambda there: pot_mine, pot_land)
        lane_slot = lax.broadcasted_iota(jnp.int32, (rows_z, LANES), 1) // width
        fields = [pot_land[s] for s in range(slabs)]
        for p in range(planes):
            for y in range(rows_y // 2):
                value = None
                for u in range(slots):
                    l = p * rows_y + u % 2 * (rows_y // 2) + y
                    spread = jnp.broadcast_to(fields[u // 2][:, l : l + 1], (rows_z, LANES))
                    value = spread if value is None else jnp.where(lane_slot == u, spread, value)
                level[pl.ds(p * rows + y * rows_z, rows_z), :] = (
                    value - (SHIFT_MID + 1.5 * STENCIL[0])
                ) * (1.0 / HALF_WIDTH)

    starts, arrive, passed = link_orders()

    def along(way, origin, h):
        view = gath.at[origin * 2 + core, h * part_rows : (h + 1) * part_rows]
        return pltpu.make_async_remote_copy(
            src_ref=view,
            dst_ref=view,
            send_sem=along_send.at[way, origin * 2 + h],
            recv_sem=along_recv.at[way, origin * 2 + h],
            device_id={"orb": (chip + 1 - 2 * way) * 2 + core},
            device_id_type=MESH,
        )

    def direct(z):
        way, h = (0, 1) if z == 0 else (1, 0)
        view = gath.at[z * 2 + core, h * part_rows : (h + 1) * part_rows]
        return pltpu.make_async_remote_copy(
            src_ref=view,
            dst_ref=view,
            send_sem=direct_send.at[0],
            recv_sem=along_recv.at[way, z * 2 + h],
            device_id={"orb": (z + 2 - 4 * way) * 2 + core},
            device_id_type=MESH,
        )

    def across(origin, h, side):
        view = gath.at[origin * 2 + side, h * part_rows : (h + 1) * part_rows]
        return pltpu.make_async_remote_copy(
            src_ref=view,
            dst_ref=view,
            send_sem=across_send.at[origin * 2 + h],
            recv_sem=across_recv.at[origin * 2 + h],
            device_id={"orb": partner},
            device_id_type=MESH,
        )

    def on_chip(z, body):
        pl.when(chip == z)(body)

    def by_chip(table, body):
        for z in table:
            def run():
                for item in table[z]:
                    body(*item)

            on_chip(z, run)

    own_items = {z: [(0, z, h) for h in range(2)] for z in range(chips)}

    def begin(c):
        on_chip((chips - 1) * (1 - c), lambda: direct((chips - 1) * (1 - c)).start())
        by_chip(starts[c], lambda *item: along(*item).start())
        for z in range(chips):
            on_chip(z, lambda: across(z, c, core).start())

    def receive(t):
        def one(way, o, h):
            along(way, o, h).wait_recv()
            across(o, h, core).start()

        with jax.named_scope("receive"):
            by_chip(arrive[t], one)

    def forward(t):
        by_chip(passed[t], lambda *item: along(*item).start())

    def settle(t):
        with jax.named_scope("settle"):
            by_chip(arrive[t], lambda way, o, h: across(o, h, 1 - core).wait_recv())

    def settle_own():
        by_chip(own_items, lambda way, o, h: across(o, h, 1 - core).wait_recv())

    def drain():
        for z in (0, chips - 1):
            on_chip(z, lambda: direct(z).wait_send())
        for table in starts + passed:
            by_chip(table, lambda *item: along(*item).wait_send())
        for table in [own_items] + arrive:
            by_chip(table, lambda way, o, h: across(o, h, core).wait_send())

    def send_trailing():
        for c in range(2):
            send(pack, land, 1, c, out_sems)

    filter_half(
        0, (send_trailing, lambda: None), lambda c: send(pack_back, land_back, 0, c, back_sems)
    )

    def store_panel(at, value):
        gath[me, at, :] = value

    for c in range(2):
        fold_part(0, c, store_panel)
        begin(c)

    def early():
        receive(0)
        forward(0)

    filter_half(1, (lambda: None, early), lambda c: None)
    receive(1)
    forward(1)
    settle_own()
    settle(0)
    settle(1)

    tiles = chips * (chips + 1) // 2
    share = tiles // 2
    block = share * LANES // slabs
    centre = (chip + 1) // 2 == 1

    def block_at(s):
        return pl.ds(pl.multiple_of(s * block, 8), block)

    def pair(z, at):
        return jnp.concatenate([gath[z * 2, at, :], gath[z * 2 + 1, at, :]], axis=1)

    @pl.when(centre)
    def _():
        at = pl.ds(pl.multiple_of((chip - 1) * part_rows, part_rows), part_rows)

        def tile(n, carry):
            t = core * share + n
            za = (t + 8) // 9 + (t + 6) // 9 + (t + 3) // 9
            zb = t - za * (za + 1) // 2
            product = dot_pieces(pieces(pair(za, at)), pieces(pair(zb, at)), (0, 0))
            for r, value in enumerate(unfolded(product, 2)):
                gram_part[pl.ds(pl.multiple_of(n * LANES + r * panel_dev, panel_dev), panel_dev), :] = value
            return carry

        with jax.named_scope("gram"):
            lax.fori_loop(0, share, tile, 0)
        exchange(slabs, here, r_send, r_recv, lambda there: gram_part.at[block_at(there)], gram_land)

    for c in range(2):
        send(pack_back, land_back, 1, c, back_sems)

    def spread(index, there):
        view = gram_chip.at[index]
        return pltpu.make_async_remote_copy(
            src_ref=view,
            dst_ref=view,
            send_sem=z_send.at[there],
            recv_sem=z_recv.at[index],
            device_id={"orb": there * 2 + core},
            device_id_type=MESH,
        )

    @pl.when(centre)
    def _():
        with jax.named_scope("wait_r"):
            wait_exchange(slabs, here, r_send, r_recv, lambda there: gram_part.at[block_at(there)], gram_land)
        gram_land[here] = gram_part[block_at(here), :]
        total = gram_land[0]
        for s in range(1, slabs):
            total += gram_land[s]
        gram_chip[chip - 1] = total / points_all

    for z in range(1, 3):
        def body():
            for there in range(chips):
                if there != z:
                    spread(z - 1, there).start()

        on_chip(z, body)
    forward(2)

    with jax.named_scope("wait_z"):
        for z in range(chips):
            def body():
                for index in range(2):
                    if z != index + 1:
                        spread(index, z).wait_recv()
                    else:
                        for there in range(chips):
                            if there != z:
                                spread(index, there).wait_send()

            on_chip(z, body)
    gram_all[core, block_at(here), :] = gram_chip[0] + gram_chip[1]

    def gram_side(side, s):
        view = gram_all.at[side, block_at(s)]
        return pltpu.make_async_remote_copy(
            src_ref=view,
            dst_ref=view,
            send_sem=t_send.at[s],
            recv_sem=t_recv.at[s],
            device_id={"orb": partner},
            device_id_type=MESH,
        )

    def plane_copy(hop, s, there):
        view = gram_all.at[core, block_at(s)]
        return pltpu.make_async_remote_copy(
            src_ref=view,
            dst_ref=view,
            send_sem=s_send.at[hop],
            recv_sem=s_recv.at[hop],
            device_id={"space": there},
            device_id_type=MESH,
        )

    for hop in range(1, slabs):
        plane_copy(hop, here, lax.rem(here + hop, slabs)).start()
    gram_side(core, here).start()

    def store_rest(at, value):
        rest_ref[at, :] = value

    for c in range(2):
        fold_part(1, c, store_rest)

    def couple_part(z, k):
        at = pl.ds(pl.multiple_of(k * 2 * LANES, 2 * LANES), 2 * LANES)
        return dot_pieces(pieces(rest_ref[at, :]), pieces(pair(z, at)), (0, 0))

    def couple_send(n, total):
        value = unfolded(total, 1)[0]
        cross_part[n] = value
        cross_land[n, here] = value
        exchange(slabs, here, c_send.at[n], c_recv.at[n], lambda there: cross_part.at[n], cross_land.at[n])

    def couple(n, z):
        with jax.named_scope("couple"):
            total = lax.fori_loop(
                0, fold // (2 * LANES), lambda k, total: total + couple_part(z, k),
                jnp.zeros((LANES, 2 * LANES), jnp.float32),
            )
        couple_send(n, total)

    lower = chip // 2
    order = [chip, chip + 1 - 2 * lax.rem(chip, 2), 2 - lower, 3 - 3 * lower]
    receive(2)
    forward(3)
    with jax.named_scope("wait_s"):
        for hop in range(1, slabs):
            source = lax.rem(here + slabs - hop, slabs)
            plane_copy(hop, source, lax.rem(here + hop, slabs)).wait_recv()
            gram_side(core, source).start()
    couple(0, order[0])
    settle(2)
    receive(3)
    forward(4)
    couple(1, order[1])
    with jax.named_scope("wait_t"):
        for s in range(slabs):
            gram_side(1 - core, s).wait_recv()

    n = LANES
    inverse[...] = jnp.zeros_like(inverse)
    for za in range(chips):
        for zb in range(za + 1):
            t = za * (za + 1) // 2 + zb
            work[za * n : (za + 1) * n, zb * n : (zb + 1) * n] = gram_all[
                t // share, (t % share) * n : (t % share + 1) * n, :
            ]

    def between(b):
        if b == 0:
            receive(4)
        if b == 1:
            settle(3)
            settle(4)
        if b == 2:
            receive(5)
            settle(5)
            couple(3, order[3])

    for b in range(chips):
        at, past = slice(b * n, (b + 1) * n), slice((b + 1) * n, PANEL)
        with jax.named_scope("diag"):
            diag_in = work[at, at]
            if b:
                before, done = slice((b - 1) * n, b * n), slice(0, b * n)
                if b < chips - 1:
                    lower_part = work[past, before]
                    work[past, at] -= dot(lower_part, work[at, before], (1, 1))
                    work[past, past] -= dot(lower_part, lower_part, (1, 1))
                inner = dot(work[at, done], inverse[done, done], (1, 0))
            if b == 2:
                tied = couple_part(order[2], 0)
                for k in range(1, fold // (2 * LANES)):
                    tied = tied + couple_part(order[2], k)
            diag = tile_inverse(diag_in)
            inverse[at, at] = diag
            if b == 2:
                couple_send(2, tied)
        with jax.named_scope("panel"):
            if b < chips - 1:
                scaled = dot(work[past, at], diag, (1, 1))
                work[past, at] = scaled
                work[(b + 1) * n : (b + 2) * n, (b + 1) * n : (b + 2) * n] -= dot(scaled[:n], scaled[:n], (1, 1))
            if b:
                inverse[at, done] = -dot(diag, inner, (1, 0))
        between(b)

    with jax.named_scope("cross"):
        for k in range(chips):
            wait_exchange(
                slabs, here, c_send.at[k], c_recv.at[k], lambda there: cross_part.at[k], cross_land.at[k]
            )
            total = cross_land[k, 0]
            for s in range(1, slabs):
                total += cross_land[k, s]
            cross[:, pl.ds(pl.multiple_of(order[k] * LANES, LANES), LANES)] = total / points_all
    with jax.named_scope("weights"):
        middle = dot(cross[...], inverse[...], (1, 1))
        trail = -dot(middle, inverse[...], (1, 0))
        own = inverse[pl.ds(pl.multiple_of(me * panel_dev, panel_dev), panel_dev), :]
        turned = jnp.concatenate([own, trail], axis=0).T
        weight_ref[...] = jnp.zeros_like(weight_ref)
        for o in range(orbs):
            value = turned[o * panel_dev : (o + 1) * panel_dev]
            weight_ref[o * LANES : o * LANES + panel_dev, :LANES] = value
            weight_ref[o * LANES + panel_dev : (o + 1) * LANES, LANES:] = value
    drain()
    for hop in range(1, slabs):
        plane_copy(hop, here, lax.rem(here + hop, slabs)).wait_send()
    for s in range(slabs):
        gram_side(core, s).wait_send()


def final_kernel(gath_ref, rest_ref, weight_ref, out_ref, high, low):
    orbs, fold, n = gath_ref.shape
    rows = out_ref.shape[1] * out_ref.shape[3]
    i = pl.program_id(0)

    @pl.when(i == 0)
    def _():
        high[...], low[...] = pieces(weight_ref[...])

    at = pl.ds(pl.multiple_of(i * rows, rows), rows)
    total = None
    for z in range(orbs // 2):
        k = slice(z * 2 * n, (z + 1) * 2 * n)
        pair = jnp.concatenate([gath_ref[z * 2, at, :], gath_ref[z * 2 + 1, at, :]], axis=1)
        value = dot_pieces(pieces(pair), (high[k, :], low[k, :]), (1, 0))
        total = value if total is None else total + value
    lanes = lax.broadcasted_iota(jnp.int32, (rows, n), 1)
    kept = rest_ref[at, :]
    count = out_ref.shape[1]
    for h in range(2):
        held = kept if h else pltpu.roll(kept, n // 2, 1)
        value = jnp.where(lanes < n // 2, 0.0, held) + total[:, h * n : (h + 1) * n]
        for k in range(count):
            out_ref[h, k, 0] = value[k * (rows // count) : (k + 1) * (rows // count)]


def early_device(slabs, orbs, orbitals, potential):
    planes, rows_y, rows_z, columns = orbitals.shape
    points = planes * rows_y * rows_z
    panel_dev = PANEL // orbs
    chips = orbs // 2
    slots = 2 * slabs
    rows = points // slots
    fold = points // 2
    tiles = chips * (chips + 1) // 2
    block = tiles // 2 * LANES // slabs
    f32 = jnp.float32
    vmem = pl.BlockSpec(memory_space=pltpu.VMEM)
    dma = pltpu.SemaphoreType.DMA
    gath, rest, weight = pl.pallas_call(
        functools.partial(early_kernel, slabs, orbs, (planes, rows_y, rows_z)),
        out_shape=[
            jax.ShapeDtypeStruct((orbs, fold, LANES), f32),
            jax.ShapeDtypeStruct((fold, LANES), f32),
            jax.ShapeDtypeStruct((orbs * LANES, 2 * LANES), f32),
        ],
        in_specs=[pl.BlockSpec(memory_space=pltpu.HBM), vmem],
        out_specs=[vmem] * 3,
        scratch_shapes=[
            pltpu.VMEM((slots, rows, LANES), f32),
            pltpu.VMEM((LANES, LANES), f32),
            pltpu.VMEM((rows_z, LANES), f32),
        ]
        + [pltpu.VMEM((slabs, points // slabs, LANES), f32)] * 4
        + [
            pltpu.VMEM((slabs, rows_z, LANES), f32),
            pltpu.VMEM((9 * points // 2, LANES), f32),
            pltpu.VMEM((9 * points // 2, LANES), f32),
            pltpu.VMEM((points // 2, LANES), f32),
            pltpu.VMEM((slabs * block, LANES), f32),
            pltpu.VMEM((slabs, block, LANES), f32),
            pltpu.VMEM((2, block, LANES), f32),
            pltpu.VMEM((2, slabs * block, LANES), f32),
            pltpu.VMEM((chips, panel_dev, LANES), f32),
            pltpu.VMEM((chips, slabs, panel_dev, LANES), f32),
            pltpu.VMEM((panel_dev, PANEL), f32),
            pltpu.VMEM((PANEL, PANEL), f32),
            pltpu.VMEM((PANEL, PANEL), f32),
        ]
        + [dma((2,))]
        + [dma((4, slabs))] * 2
        + [dma((slabs,))] * 2
        + [dma((4, slabs))] * 2
        + [dma((2, orbs))] * 2
        + [dma((1,))]
        + [dma((orbs,))] * 2
        + [dma((slabs,))] * 2
        + [dma((chips,)), dma((2,))]
        + [dma((slabs,))] * 4
        + [dma((chips, slabs))] * 2,
        compiler_params=pltpu.CompilerParams(
            collective_id=0, has_side_effects=True, vmem_limit_bytes=40 << 20
        ),
    )(orbitals.reshape(slots, rows, columns), potential.reshape(planes * rows_y, rows_z))
    whole = [pl.BlockSpec(memory_space=pltpu.VMEM)] * 3
    out = pl.pallas_call(
        final_kernel,
        grid=(slabs,),
        out_shape=jax.ShapeDtypeStruct((2, slabs, 2, rows // 2, LANES), f32),
        in_specs=whole,
        out_specs=pl.BlockSpec(
            (2, slabs // 2, 1, rows // 2, LANES), lambda i: (0, i % 2, i // 2, 0, 0)
        ),
        scratch_shapes=[pltpu.VMEM((orbs * LANES, 2 * LANES), jnp.bfloat16)] * 2,
        compiler_params=pltpu.CompilerParams(vmem_limit_bytes=16 << 20),
    )(gath, rest, weight)
    return out.reshape(planes, rows_y, rows_z, columns)


def per_device(slabs, orbs, orbitals, potential):
    planes, rows_y, rows_z, columns = orbitals.shape
    points = planes * rows_y * rows_z
    panel_dev = PANEL // orbs
    folds = LANES // panel_dev
    thin = points // LANES
    f32 = jnp.float32
    vmem = pl.BlockSpec(memory_space=pltpu.VMEM)
    dma = pltpu.SemaphoreType.DMA
    steps = max(orbs // 2 - 1, 1)
    split = folds == 2 and planes == slabs and rows_y // 2 >= REACH and steps >= 2
    if split and orbs == 8 and slabs == 4 and PANEL == 4 * LANES and planes * rows_y <= LANES:
        return early_device(slabs, orbs, orbitals, potential)
    flat = orbitals.reshape(points, columns)
    own, panel, gram, cross = pl.pallas_call(
        functools.partial(filter_kernel, slabs, orbs, (planes, rows_y, rows_z), split),
        out_shape=[
            jax.ShapeDtypeStruct((points, LANES), f32),
            jax.ShapeDtypeStruct((points, PANEL), f32),
            jax.ShapeDtypeStruct((PANEL, PANEL), f32),
            jax.ShapeDtypeStruct((LANES, PANEL), f32),
        ],
        in_specs=[vmem] * 2,
        out_specs=[vmem] * 4,
        scratch_shapes=[pltpu.VMEM((slabs, points // slabs, LANES), f32)] * 4
        + [
            pltpu.VMEM((slabs, thin, LANES), f32),
            pltpu.VMEM(((9 if split else 6) * points // 2, LANES), f32),
            pltpu.VMEM(((9 if split else 6) * points // 2, LANES), f32),
            pltpu.VMEM((points, LANES), f32),
            pltpu.VMEM((orbs, points // folds, LANES), f32),
            pltpu.VMEM((LANES, PANEL), f32),
            pltpu.VMEM((slabs, LANES, PANEL), f32),
            pltpu.VMEM((orbs, panel_dev, PANEL), f32),
        ]
        + [dma((slabs,))] * 14
        + [dma((2, steps))] * 2 + [dma((2 * steps + 1,))] * 2
        + [dma((2, steps))] * 2 + [dma((2 * steps + 1,))] * 2,
        compiler_params=pltpu.CompilerParams(
            collective_id=0, has_side_effects=True, vmem_limit_bytes=32 << 20
        ),
    )(flat, potential.reshape(LANES, thin).T)
    out = pl.pallas_call(
        functools.partial(solve_kernel, orbs),
        out_shape=jax.ShapeDtypeStruct((points, LANES), f32),
        in_specs=[vmem] * 4,
        out_specs=vmem,
        scratch_shapes=[
            pltpu.VMEM((PANEL, PANEL), f32),
            pltpu.VMEM((PANEL, PANEL), f32),
            pltpu.VMEM((LANES, PANEL), f32),
        ],
        compiler_params=pltpu.CompilerParams(vmem_limit_bytes=32 << 20),
    )(own, panel, gram, cross)
    return out.reshape(planes, rows_y, rows_z, columns)


def solution(mesh):
    placed = (P("space", None, None, "orb"), P("space", None, None))
    return jax.shard_map(
        functools.partial(per_device, mesh.shape["space"], mesh.shape["orb"]),
        mesh=mesh,
        in_specs=placed,
        out_specs=P("space", None, None, "orb"),
        check_vma=False,
    )
```

```python
import functools

import jax
import jax.numpy as jnp
from jax import lax
from jax.experimental import pallas as pl
from jax.experimental.pallas import tpu as pltpu
from jax.sharding import PartitionSpec as P

PANEL = 512
DEGREE = 4

STENCIL = (-205.0 / 72.0, 8.0 / 5.0, -1.0 / 5.0, 8.0 / 315.0, -1.0 / 560.0)
SHIFT_MID = 7.25
HALF_WIDTH = 4.75
LANES = 128
REACH = 4
MESH = pl.DeviceIdType.MESH
HIGHEST = lax.Precision.HIGHEST


def dot(a, b, dims):
    return lax.dot_general(
        a, b, ((dims[:1], dims[1:]), ((), ())), precision=HIGHEST, preferred_element_type=jnp.float32
    )


def regroup(load, store, count, rows):
    width = LANES // count
    step = min(rows, max(8, 128 // count))
    group = lax.broadcasted_iota(jnp.int32, (step, LANES), 1) // width

    def body(block, carry):
        here = pl.ds(pl.multiple_of(block * step, step), step)
        parts = [load(r, here) for r in range(count)]
        for j in range(count):
            out = None
            for r in range(count):
                turn = ((r - j) * width) % LANES
                piece = pltpu.roll(parts[r], turn, 1) if turn else parts[r]
                out = piece if out is None else jnp.where(group == r, piece, out)
            store(j, here, out)
        return carry

    lax.fori_loop(0, rows // step, body, 0)


def exchange(slots, here, send_sem, recv_sem, send, land):
    copies = []
    for hop in range(1, slots):
        there = lax.rem(here + hop, slots)
        copy = pltpu.make_async_remote_copy(
            src_ref=send(there),
            dst_ref=land.at[here],
            send_sem=send_sem.at[hop],
            recv_sem=recv_sem.at[hop],
            device_id={"space": there},
            device_id_type=MESH,
        )
        copy.start()
        copies.append(copy)
    return copies


def wait_exchange(slots, here, send_sem, recv_sem, send, land):
    for hop in range(1, slots):
        there = lax.rem(here + hop, slots)
        source = lax.rem(here + slots - hop, slots)
        pltpu.make_async_remote_copy(
            src_ref=send(there),
            dst_ref=land.at[source],
            send_sem=send_sem.at[hop],
            recv_sem=recv_sem.at[hop],
            device_id={"space": there},
            device_id_type=MESH,
        ).wait()


def gather_orb(count, me, buf, send_sem, recv_sem, side_send, side_recv, arrived=lambda chip: None, during=None):
    chips = count // 2
    chip, core = me // 2, lax.rem(me, 2)
    partner = chip * 2 + (1 - core)

    def along(origin, to, way, step):
        slot = buf.at[origin * 2 + core]
        return pltpu.make_async_remote_copy(
            src_ref=slot,
            dst_ref=slot,
            send_sem=send_sem.at[way, step],
            recv_sem=recv_sem.at[way, step],
            device_id={"orb": to * 2 + core},
            device_id_type=MESH,
        )

    def across(origin, side, index):
        slot = buf.at[origin * 2 + side]
        return pltpu.make_async_remote_copy(
            src_ref=slot,
            dst_ref=slot,
            send_sem=side_send.at[index],
            recv_sem=side_recv.at[index],
            device_id={"orb": partner},
            device_id_type=MESH,
        )

    steps = chips - 1

    def finish(step):
        @pl.when(chip - 1 - step >= 0)
        def _():
            across(chip - 1 - step, 1 - core, 1 + step).wait_recv()
            arrived(chip - 1 - step)

        @pl.when(chip + 1 + step < chips)
        def _():
            across(chip + 1 + step, 1 - core, 1 + steps + step).wait_recv()
            arrived(chip + 1 + step)

    for step in range(steps):
        @pl.when((chip - step >= 0) & (chip + 1 < chips))
        def _():
            along(chip - step, chip + 1, 0, step).start()

        @pl.when((chip + step < chips) & (chip - 1 >= 0))
        def _():
            along(chip + step, chip - 1, 1, step).start()

        if step == 0:
            across(chip, core, 0).start()
            if during:
                during[0]()
        if step == (1 if during else 0):
            if during:
                during[1]()
            across(chip, 1 - core, 0).wait_recv()
            arrived(chip)
        if step:
            finish(step - 1)

        @pl.when(chip - 1 - step >= 0)
        def _():
            along(chip - 1 - step, chip, 0, step).wait_recv()
            across(chip - 1 - step, core, 1 + step).start()

        @pl.when(chip + 1 + step < chips)
        def _():
            along(chip + 1 + step, chip, 1, step).wait_recv()
            across(chip + 1 + step, core, 1 + steps + step).start()

    finish(steps - 1)
    across(chip, core, 0).wait_send()
    for step in range(steps):
        @pl.when((chip - step >= 0) & (chip + 1 < chips))
        def _():
            along(chip - step, chip + 1, 0, step).wait_send()

        @pl.when((chip + step < chips) & (chip - 1 >= 0))
        def _():
            along(chip + step, chip - 1, 1, step).wait_send()

        @pl.when(chip - 1 - step >= 0)
        def _():
            across(chip - 1 - step, core, 1 + step).wait_send()

        @pl.when(chip + 1 + step < chips)
        def _():
            across(chip + 1 + step, core, 1 + steps + step).wait_send()


def split_filter(
    slabs, shape, here, me, x_ref, pot_ref, own_ref, pack, land, pack_back, land_back, pot_land,
    wide_a, wide_b, level, gath, out_sems, pot_sems, back_sems,
):
    planes, rows_y, rows_z = shape
    points = planes * rows_y * rows_z
    slots = 2 * slabs
    width = LANES // slots
    rows = points // slots
    plane = 3 * rows
    thin = points // LANES
    step = 16
    slot = lax.broadcasted_iota(jnp.int32, (step, LANES), 1) // width

    def merge(parts):
        out = None
        for u, (value, v) in enumerate(parts):
            turn = ((u - v) * width) % LANES
            value = pltpu.roll(value, turn, 1) if turn else value
            out = value if out is None else jnp.where(slot == u, value, out)
        return out

    def over(body):
        def one(block, carry):
            body(pl.multiple_of(block * step, step))
            return carry

        lax.fori_loop(0, rows // step, one, 0)

    def half(buf, h):
        return buf.at[:, h * rows : (h + 1) * rows]

    def send(buf, landing, h, sems):
        exchange(slabs, here, *sems[h], lambda there: half(buf, h).at[there], half(landing, h))
        landing[here, h * rows : (h + 1) * rows] = buf[here, h * rows : (h + 1) * rows]

    def wait(buf, landing, h, sems):
        wait_exchange(slabs, here, *sems[h], lambda there: half(buf, h).at[there], half(landing, h))

    def pack_half(h):
        def body(at):
            parts = [x_ref[pl.ds(q * rows + at, step), :] for q in range(slots)]
            for j in range(slabs):
                pack[j, pl.ds(h * rows + at, step), :] = merge([(part, h * slabs + j) for part in parts])

        over(body)
        send(pack, land, h, out_sems)

    def put(target, p, row, value):
        odd = lax.rem(lax.broadcasted_iota(jnp.int32, value.shape, 1) // width, 2)
        size = value.shape[0]
        swapped = jnp.where(odd == 0, pltpu.roll(value, LANES - width, 1), pltpu.roll(value, width, 1))
        target[pl.ds((planes + p) * plane + rows + row, size), :] = value
        target[pl.ds((planes + p) * plane + row, size), :] = swapped
        target[pl.ds((planes + p) * plane + 2 * rows + row, size), :] = swapped
        target[pl.ds(p * plane + rows + row, size), :] = pltpu.roll(value, 2 * width, 1)
        target[pl.ds((2 * planes + p) * plane + rows + row, size), :] = pltpu.roll(value, LANES - 2 * width, 1)

    taps = [-0.5 * c / HALF_WIDTH for c in STENCIL]

    def sweep(source, target, first):
        def body(y, carry):
            for p in range(planes):
                def line(q, yy):
                    row = pl.multiple_of((planes + q) * plane + rows + yy * rows_z, rows_z)
                    return source[pl.ds(row, rows_z), :]

                row = pl.multiple_of(y * rows_z, rows_z)
                centre = line(p, y)
                total = level[pl.ds(p * rows + row, rows_z), :] * centre
                for m in range(1, REACH + 1):
                    near = line(p + m, y) + line(p - m, y) + line(p, y + m) + line(p, y - m)
                    near += pltpu.roll(centre, m, 0) + pltpu.roll(centre, rows_z - m, 0)
                    total += taps[m] * near
                if not first:
                    total = 2.0 * total - target[pl.ds((planes + p) * plane + rows + row, rows_z), :]
                put(target, p, row, total)
            return carry

        lax.fori_loop(0, rows_y // 2, body, 0)

    def filter_half(h):
        wait(pack, land, h, out_sems)

        def unpack(at):
            parts = [land[i, pl.ds(h * rows + at, step), :] for i in range(slabs)]
            for p in range(planes):
                put(wide_a, p, at, merge([(parts[u // 2], 2 * p + u % 2) for u in range(slots)]))

        over(unpack)
        sweep(wide_a, wide_b, True)
        source, target = wide_b, wide_a
        for _ in range(DEGREE - 1):
            sweep(source, target, False)
            source, target = target, source

        def body(at):
            parts = [source[pl.ds((planes + p) * plane + rows + at, step), :] for p in range(planes)]
            for i in range(slabs):
                pack_back[i, pl.ds(h * rows + at, step), :] = merge(
                    [(parts[q // 2], 2 * i + q % 2) for q in range(slots)]
                )

        over(body)
        send(pack_back, land_back, h, back_sems)

    pack_half(0)
    pack_half(1)
    pot_land[here] = pot_ref[...]
    wait_exchange(slabs, here, *pot_sems, lambda there: pot_ref, pot_land)
    lane_slot = lax.broadcasted_iota(jnp.int32, (thin, LANES), 1) // width
    fields = [pot_land[s] for s in range(slabs)]
    pieces = rows // thin
    for p in range(planes):
        for e in range(pieces):
            value = None
            for u in range(slots):
                l = (2 * p + u % 2) * pieces + e
                spread = jnp.broadcast_to(fields[u // 2][:, l : l + 1], (thin, LANES))
                value = spread if value is None else jnp.where(lane_slot == u, spread, value)
            level[pl.ds(p * rows + e * thin, thin), :] = (
                value - (SHIFT_MID + 1.5 * STENCIL[0])
            ) * (1.0 / HALF_WIDTH)

    filter_half(0)
    wait(pack_back, land_back, 0, back_sems)

    def fold_own(at):
        parts = [land_back[j, pl.ds(at, step), :] for j in range(slabs)]
        for k in range(slabs):
            gath[me, pl.ds(k * rows + at, step), :] = merge(
                [(parts[u % slabs], (u // slabs) * slabs + k) for u in range(slots)]
            )

    over(fold_own)

    def finish():
        wait(pack_back, land_back, 1, back_sems)

        def body(at):
            parts = [
                land_back[u % slabs, pl.ds((u // slabs) * rows + at, step), :] for u in range(slots)
            ]
            for q in range(slots):
                own_ref[pl.ds(q * rows + at, step), :] = merge([(part, q) for part in parts])

        over(body)

    return (lambda: filter_half(1)), finish


def filter_kernel(
    slabs, orbs, shape, split,
    x_ref, pot_ref, own_ref, panel_ref, gram_ref, cross_ref,
    pack, land, pack_back, land_back, pot_land, wide_a, wide_b, level, gath, part, part_land, rows_land,
    a_send, a_recv, p_send, p_recv, b_send, b_recv, c_send, c_recv, d_send, d_recv, e_send, e_recv, f_send, f_recv,
    g_send, g_recv, gs_send, gs_recv, h_send, h_recv, hs_send, hs_recv,
):
    planes, rows_y, rows_z = shape
    points = planes * rows_y * rows_z
    here, me = lax.axis_index("space"), lax.axis_index("orb")
    chunk = points // slabs
    width = LANES // slabs

    barrier = pltpu.get_barrier_semaphore()
    for hop in range(1, slabs):
        pl.semaphore_signal(
            barrier, inc=1, device_id={"space": lax.rem(here + hop, slabs)}, device_id_type=MESH
        )
    for hop in range(1, orbs):
        pl.semaphore_signal(
            barrier, inc=1, device_id={"orb": lax.rem(me + hop, orbs)}, device_id_type=MESH
        )
    pl.semaphore_wait(barrier, slabs - 1 + orbs - 1)

    exchange(slabs, here, p_send, p_recv, lambda there: pot_ref, pot_land)

    panel_dev = PANEL // orbs
    folds = LANES // panel_dev
    fold = points // folds
    during = None
    if split:
        during = split_filter(
            slabs, shape, here, me, x_ref, pot_ref, own_ref, pack, land, pack_back, land_back, pot_land,
            wide_a, wide_b, level, gath,
            ((a_send, a_recv), (e_send, e_recv)), (p_send, p_recv), ((b_send, b_recv), (f_send, f_recv)),
        )
    else:
        def store_pack(j, at, value):
            pack[j, at, :] = value

        regroup(lambda r, at: x_ref[pl.ds(r * chunk + at.start, at.size), :], store_pack, slabs, chunk)
        exchange(slabs, here, a_send, a_recv, lambda there: pack.at[there], land)
        land[here] = pack[here]
        pot_land[here] = pot_ref[...]
        wait_exchange(slabs, here, p_send, p_recv, lambda there: pot_ref, pot_land)

        thin = points // LANES
        lane_group = lax.broadcasted_iota(jnp.int32, (thin, LANES), 1) // width
        fields = [pot_land[s] for s in range(slabs)]
        for l in range(LANES):
            value = None
            for s in range(slabs):
                spread = jnp.broadcast_to(fields[s][:, l : l + 1], (thin, LANES))
                value = spread if value is None else jnp.where(lane_group == s, spread, value)
            level[pl.ds(l * thin, thin), :] = (value - (SHIFT_MID + 1.5 * STENCIL[0])) * (1.0 / HALF_WIDTH)

        wait_exchange(slabs, here, a_send, a_recv, lambda there: pack.at[there], land)

        def put(target, row, value):
            target[pl.ds(points + row, value.shape[0]), :] = value
            target[pl.ds(row, value.shape[0]), :] = pltpu.roll(value, width, 1)
            target[pl.ds(2 * points + row, value.shape[0]), :] = pltpu.roll(value, LANES - width, 1)

        regroup(
            lambda r, at: land[r, at, :],
            lambda j, at, value: put(wide_a, j * chunk + at.start, value),
            slabs, chunk,
        )

        plane = rows_y * rows_z
        taps = [-0.5 * c / HALF_WIDTH for c in STENCIL]

        def sweep(source, target, first):
            def body(y, carry):
                for p in range(planes):
                    def line(q, yy):
                        return source[pl.ds(pl.multiple_of(points + q * plane + yy * rows_z, rows_z), rows_z), :]

                    row = pl.multiple_of(p * plane + y * rows_z, rows_z)
                    centre = line(p, y)
                    total = level[pl.ds(row, rows_z), :] * centre
                    for m in range(1, REACH + 1):
                        near = line(p + m, y) + line(p - m, y)
                        near += line(p, lax.rem(y + m, rows_y)) + line(p, lax.rem(y + rows_y - m, rows_y))
                        near += pltpu.roll(centre, m, 0) + pltpu.roll(centre, rows_z - m, 0)
                        total += taps[m] * near
                    if not first:
                        before = target[pl.ds(pl.multiple_of(points + row, rows_z), rows_z), :]
                        total = 2.0 * total - before
                    put(target, row, total)
                return carry

            lax.fori_loop(0, rows_y, body, 0)

        sweep(wide_a, wide_b, True)
        source, target = wide_b, wide_a
        for _ in range(DEGREE - 1):
            sweep(source, target, False)
            source, target = target, source

        def store_back(j, at, value):
            pack_back[j, at, :] = value

        regroup(
            lambda r, at: source[pl.ds(points + r * chunk + at.start, at.size), :], store_back, slabs, chunk
        )
        exchange(slabs, here, b_send, b_recv, lambda there: pack_back.at[there], land_back)
        land_back[here] = pack_back[here]
        wait_exchange(slabs, here, b_send, b_recv, lambda there: pack_back.at[there], land_back)

        def store_own(j, at, value):
            own_ref[pl.ds(j * chunk + at.start, at.size), :] = value

        regroup(lambda r, at: land_back[r, at, :], store_own, slabs, chunk)

        step = min(fold, 32)
        fold_group = lax.broadcasted_iota(jnp.int32, (step, LANES), 1) // panel_dev

        def folded(block, carry):
            at = pl.multiple_of(block * step, step)
            out = None
            for r in range(folds):
                piece = own_ref[pl.ds(r * fold + at, step), :]
                piece = pltpu.roll(piece, r * panel_dev, 1) if r else piece
                out = piece if out is None else jnp.where(fold_group == r, piece, out)
            gath[me, pl.ds(at, step), :] = out
            return carry

        lax.fori_loop(0, fold // step, folded, 0)

    block = 512

    def take(tile):
        lanes = pl.ds(pl.multiple_of(tile * LANES, LANES), LANES)

        def store_panel(j, at, value):
            panel_ref[pl.ds(j * fold + at.start, at.size), lanes] = value

        regroup(lambda r, at: gath[tile * folds + r, at, :], store_panel, folds, fold)

        def product(k, total):
            at = pl.ds(pl.multiple_of(k * block, block), block)
            return total + dot(own_ref[at, :], panel_ref[at, lanes], (0, 0))

        part[:, lanes] = lax.fori_loop(
            0, points // block, product, jnp.zeros((LANES, LANES), jnp.float32)
        )

    if folds == 2:
        gather_orb(orbs, me, gath, g_send, g_recv, gs_send, gs_recv, take, during)
    else:
        gather_orb(orbs, me, gath, g_send, g_recv, gs_send, gs_recv)

        def each(tile, carry):
            take(tile)
            return carry

        lax.fori_loop(0, PANEL // LANES, each, 0)

    top, rest = part.at[:panel_dev], part.at[panel_dev:]
    top_land, rest_land = part_land.at[:, :panel_dev], part_land.at[:, panel_dev:]
    exchange(slabs, here, c_send, c_recv, lambda there: top, top_land)
    exchange(slabs, here, d_send, d_recv, lambda there: rest, rest_land)
    part_land[here] = part[...]
    points_all = points * slabs

    def summed(view):
        total = view[0]
        for s in range(1, slabs):
            total += view[s]
        return total / points_all

    wait_exchange(slabs, here, c_send, c_recv, lambda there: top, top_land)
    rows_land[me] = summed(top_land)
    gather_orb(orbs, me, rows_land, h_send, h_recv, hs_send, hs_recv)
    wait_exchange(slabs, here, d_send, d_recv, lambda there: rest, rest_land)
    cross_ref[:panel_dev, :] = jnp.zeros((panel_dev, PANEL), jnp.float32)
    cross_ref[panel_dev:, :] = summed(rest_land)
    for o in range(orbs):
        gram_ref[o * panel_dev : (o + 1) * panel_dev, :] = rows_land[o]


def block_inverse(a):
    n = LANES
    tiles = n // 8
    rows = lax.broadcasted_iota(jnp.int32, (8, n), 0)
    cols = lax.broadcasted_iota(jnp.int32, (8, n), 1)
    work = [a[8 * t : 8 * t + 8] for t in range(tiles)]
    unit = [jnp.where(rows + 8 * t == cols, 1.0, 0.0).astype(jnp.float32) for t in range(tiles)]
    for t0 in range(tiles):
        base = 8 * t0
        columns = [jnp.broadcast_to(work[t0][:, base + k : base + k + 1], (8, n)) for k in range(8)]
        small = {
            (i, k): jnp.broadcast_to(columns[k][i : i + 1], (8, n)) for i in range(8) for k in range(i + 1)
        }
        lower, scales = {}, []
        for j in range(8):
            scales.append(1.0 / small[j, j])
            for i in range(j + 1, 8):
                lower[i, j] = small[i, j] * scales[j]
            for i in range(j + 1, 8):
                for k in range(j + 1, i + 1):
                    small[i, k] = small[i, k] - lower[i, j] * small[k, j]
        turned = {}
        for j in range(8):
            for i in range(j + 1, 8):
                value = lower[i, j]
                for k in range(j + 1, i):
                    value = value + lower[i, k] * turned[k, j]
                turned[i, j] = -value
        a_row, u_row = work[t0], unit[t0]
        a_new, u_new = a_row, u_row
        for k in range(7):
            weight = jnp.zeros((8, n), jnp.float32)
            for i in range(k + 1, 8):
                weight = jnp.where(rows == i, turned[i, k], weight)
            a_new = a_new + weight * jnp.broadcast_to(a_row[k : k + 1], (8, n))
            u_new = u_new + weight * jnp.broadcast_to(u_row[k : k + 1], (8, n))
        work[t0], unit[t0] = a_new, u_new
        if t0 == tiles - 1:
            break
        a_out = u_out = None
        for i in range(8):
            weight = jnp.where(rows == i, scales[i], 0.0)
            for k in range(i):
                weight = jnp.where(rows == k, turned[i, k] * scales[i], weight)
            a_term = weight * jnp.broadcast_to(a_new[i : i + 1], (8, n))
            u_term = weight * jnp.broadcast_to(u_new[i : i + 1], (8, n))
            a_out = a_term if a_out is None else a_out + a_term
            u_out = u_term if u_out is None else u_out + u_term
        a_rows = [jnp.broadcast_to(a_out[k : k + 1], (8, n)) for k in range(8)]
        u_rows = [jnp.broadcast_to(u_out[k : k + 1], (8, n)) for k in range(8)]
        for t in range(t0 + 1, tiles):
            before = work[t]
            for k in range(8):
                column = jnp.broadcast_to(before[:, base + k : base + k + 1], (8, n))
                work[t] = work[t] - column * a_rows[k]
                unit[t] = unit[t] - column * u_rows[k]
    out = []
    for t in range(tiles):
        pivots = jnp.sum(jnp.where(rows + 8 * t == cols, work[t], 0.0), axis=1, keepdims=True)
        out.append(unit[t] * (1.0 / jnp.sqrt(pivots)))
    return jnp.concatenate(out, axis=0)


def solve_kernel(orbs, own_ref, panel_ref, gram_ref, cross_ref, out_ref, work, inverse, weights):
    panel_dev = PANEL // orbs
    me = lax.axis_index("orb")
    n = LANES
    blocks = PANEL // n
    work[...] = gram_ref[...]
    inverse[...] = jnp.zeros_like(inverse)

    def factor(b, carry):
        at = pl.multiple_of(b * n, n)
        diag = block_inverse(work[pl.ds(at, n), pl.ds(at, n)])
        inverse[pl.ds(at, n), pl.ds(at, n)] = diag
        for i in range(1, blocks):
            @pl.when(i > b)
            def _():
                work[i * n : (i + 1) * n, pl.ds(at, n)] = dot(
                    work[i * n : (i + 1) * n, pl.ds(at, n)], diag, (1, 1)
                )
        for i in range(1, blocks):
            @pl.when(i > b)
            def _():
                left = work[i * n : (i + 1) * n, pl.ds(at, n)]
                for k in range(1, i + 1):
                    @pl.when(k > b)
                    def _():
                        right = work[k * n : (k + 1) * n, pl.ds(at, n)]
                        work[i * n : (i + 1) * n, k * n : (k + 1) * n] -= dot(left, right, (1, 1))
        return carry

    lax.fori_loop(0, blocks, factor, 0)
    for i in range(1, blocks):
        span = i * n
        inner = dot(work[i * n : (i + 1) * n, :span], inverse[:span, :span], (1, 0))
        inverse[i * n : (i + 1) * n, :span] = -dot(
            inverse[i * n : (i + 1) * n, i * n : (i + 1) * n], inner, (1, 0)
        )

    middle = dot(cross_ref[...], inverse[...], (1, 1))
    weights[...] = -dot(middle, inverse[...], (1, 0))
    weights[:panel_dev, :] = inverse[pl.ds(pl.multiple_of(me * panel_dev, panel_dev), panel_dev), :]
    points = own_ref.shape[0]
    block = 256
    lanes = lax.broadcasted_iota(jnp.int32, (block, LANES), 1)

    def final(k, carry):
        at = pl.ds(pl.multiple_of(k * block, block), block)
        kept = jnp.where(lanes < panel_dev, 0.0, own_ref[at, :])
        out_ref[at, :] = kept + dot(panel_ref[at, :], weights[...], (1, 1))
        return carry

    lax.fori_loop(0, points // block, final, 0)


def pieces(x):
    high = x.astype(jnp.bfloat16)
    return high, (x - high.astype(jnp.float32)).astype(jnp.bfloat16)


def dot_pieces(a, b, dims):
    def one(left, right):
        return lax.dot_general(
            left, right, ((dims[:1], dims[1:]), ((), ())), preferred_element_type=jnp.float32
        )

    return one(a[0], b[0]) + (one(a[0], b[1]) + one(a[1], b[0]))


def unfolded(product, rows):
    half = LANES // 2
    lanes = lax.broadcasted_iota(jnp.int32, (half, LANES), 1)
    out = []
    for r in range(rows):
        sides = []
        for c in range(2):
            at = product[r * LANES : (r + 1) * LANES, c * LANES : (c + 1) * LANES]
            sides.append(at[:half] + pltpu.roll(at[half:], half, 1))
        out.append(jnp.where(lanes < half, sides[0], pltpu.roll(sides[1], half, 1)))
    return out


def link_orders():
    def both(table):
        out = {z: list(items) for z, items in table.items()}
        for z, items in table.items():
            out[3 - z] = [(1 - way, 3 - o, 1 - h) for way, o, h in items]
        return out

    starts = [
        {0: [(0, 0, 0)], 1: [(1, 1, 0)], 2: [(1, 2, 0), (0, 2, 0)]},
        {0: [(0, 0, 1)], 1: [(0, 1, 1), (1, 1, 1)], 2: [(0, 2, 1)], 3: [(1, 3, 1), (1, 3, 0)]},
    ]
    arrive = [
        both({1: [(1, 2, 0)]}),
        both({0: [(1, 1, 0), (1, 1, 1)], 1: [(0, 0, 0), (1, 3, 0)]}),
        both({0: [(1, 2, 0)], 1: [(0, 0, 1), (1, 2, 1)]}),
        both({0: [(1, 3, 0)], 1: [(1, 3, 1)]}),
        both({0: [(1, 2, 1)]}),
        both({0: [(1, 3, 1)]}),
    ]
    passed = [
        both({1: [(1, 2, 0)]}),
        both({1: [(0, 1, 0)]}),
        both({1: [(0, 0, 0), (1, 3, 0)]}),
        both({1: [(1, 2, 1)]}),
        both({1: [(1, 3, 1)]}),
    ]
    return starts, arrive, passed


def tile_inverse(a):
    n = LANES
    tiles = n // 8
    rows = lax.broadcasted_iota(jnp.int32, (8, n), 0)
    lanes = lax.broadcasted_iota(jnp.int32, (8, n), 1)

    def row_of(value, k):
        return jnp.broadcast_to(value[k : k + 1], (8, n))

    def column_of(value, k):
        return jnp.broadcast_to(value[:, k : k + 1], (8, n))

    def tree(terms):
        while len(terms) > 1:
            paired = [terms[i] + terms[i + 1] for i in range(0, len(terms) - 1, 2)]
            terms = paired + terms[len(terms) - len(terms) % 2 :]
        return terms[0]

    work = [a[8 * t : 8 * t + 8] for t in range(tiles)]
    cols = [column_of(work[0], k) for k in range(8)]
    out = []
    for t0 in range(tiles):
        base = 8 * t0
        last = t0 == tiles - 1
        if not last:
            side = [column_of(work[t0 + 1], base + k) for k in range(8)]
            ahead = [column_of(work[t0 + 1], base + 8 + k) for k in range(8)]
            moved = list(side)
        below, pivots, scales = [], [], []
        for j in range(8):
            pivot = row_of(cols[j], j)
            scale = 1.0 / pivot
            lead = jnp.where(rows > j, cols[j], 0.0)
            pivots.append(pivot)
            scales.append(scale)
            below.append(lead * scale)
            for k in range(j + 1, 8):
                part = row_of(cols[k], j) * scale
                cols[k] = cols[k] - lead * part
                if not last:
                    moved[k] = moved[k] - moved[j] * part
        above = cols
        if not last:
            scaled = [moved[j] * scales[j] for j in range(8)]
            cols = [
                ahead[k] - tree([scaled[j] * row_of(moved[j], k) for j in range(8)]) for k in range(8)
            ]
        inside = (lanes >= base) & (lanes < base + 8)
        value = jnp.where(inside, jnp.where(lanes == rows + base, 1.0, 0.0), work[t0])
        root, turn = pivots[0], scales[0]
        for j in range(8):
            value = value - below[j] * row_of(value, j)
            if j:
                root = jnp.where(rows == j, pivots[j], root)
                turn = jnp.where(rows == j, scales[j], turn)
        out.append(jnp.where(lanes < base + 8, value * lax.rsqrt(root), 0.0))
        if last:
            break
        value = value * turn
        for k in range(7, 0, -1):
            value = value - jnp.where(rows < k, above[k] * turn, 0.0) * row_of(value, k)
        leads = [row_of(value, k) for k in range(8)]
        for t in range(t0 + 1, tiles):
            before = work[t]
            columns = side if t == t0 + 1 else [column_of(before, base + k) for k in range(8)]
            work[t] = jnp.where(inside, 0.0, before) - tree([columns[k] * leads[k] for k in range(8)])
    return jnp.concatenate(out, axis=0)


def early_kernel(
    slabs, orbs, shape,
    x_hbm, pot_ref, gath, rest_ref, weight_ref,
    x_ref, pot_wide, pot_mine, pack, land, pack_back, land_back, pot_land, wide_a, wide_b, level,
    gram_part, gram_land, gram_chip, gram_all, cross_part, cross_land, cross, work, inverse,
    x_sem, a_send, a_recv, p_send, p_recv, b_send, b_recv,
    along_send, along_recv, direct_send, across_send, across_recv,
    r_send, r_recv, z_send, z_recv, s_send, s_recv, t_send, t_recv, c_send, c_recv,
):
    planes, rows_y, rows_z = shape
    points = planes * rows_y * rows_z
    here, me = lax.axis_index("space"), lax.axis_index("orb")
    chips = orbs // 2
    chip, core = me // 2, lax.rem(me, 2)
    partner = chip * 2 + (1 - core)
    slots = 2 * slabs
    width = LANES // slots
    rows = points // slots
    plane = 3 * rows
    sub = rows // 2
    fold = points // 2
    part_rows = fold // 2
    panel_dev = PANEL // orbs
    points_all = points * slabs
    step = 16

    def fetch(c):
        view = slice(c * sub, (c + 1) * sub)
        return pltpu.make_async_copy(x_hbm.at[:, view], x_ref.at[:, view], x_sem.at[c])

    for c in range(2):
        fetch(c).start()

    barrier = pltpu.get_barrier_semaphore()
    for hop in range(1, slabs):
        pl.semaphore_signal(
            barrier, inc=1, device_id={"space": lax.rem(here + hop, slabs)}, device_id_type=MESH
        )
    for hop in range(1, orbs):
        pl.semaphore_signal(
            barrier, inc=1, device_id={"orb": lax.rem(me + hop, orbs)}, device_id_type=MESH
        )

    def exchange_groups(x, unit):
        lane = lax.broadcasted_iota(jnp.int32, (step, LANES), 1) // unit
        outer, inner = lane // 2 % 2 == 0, lane % 2 == 0
        pairs = [None] * 4
        for a in range(2):
            pairs[a] = jnp.where(outer, x[a], pltpu.roll(x[a + 2], 2 * unit, 1))
            pairs[a + 2] = jnp.where(outer, pltpu.roll(x[a], LANES - 2 * unit, 1), x[a + 2])
        out = [None] * 4
        for a in (0, 2):
            out[a] = jnp.where(inner, pairs[a], pltpu.roll(pairs[a + 1], unit, 1))
            out[a + 1] = jnp.where(inner, pltpu.roll(pairs[a], LANES - unit, 1), pairs[a + 1])
        return out

    def over(c, body):
        def one(block, carry):
            body(pl.multiple_of(c * sub + block * step, step))
            return carry

        lax.fori_loop(0, sub // step, one, 0, unroll=2)

    def span(h, c):
        return slice(h * rows + c * sub, h * rows + (c + 1) * sub)

    def send(buf, landing, h, c, sems):
        at, k = span(h, c), h * 2 + c
        exchange(
            slabs, here, sems[0].at[k], sems[1].at[k], lambda there: buf.at[there, at], landing.at[:, at]
        )
        landing[here, at] = buf[here, at]

    def wait(buf, landing, h, c, sems):
        at, k = span(h, c), h * 2 + c
        wait_exchange(
            slabs, here, sems[0].at[k], sems[1].at[k], lambda there: buf.at[there, at], landing.at[:, at]
        )

    out_sems, back_sems = (a_send, a_recv), (b_send, b_recv)

    def pack_part(h, c):
        def body(at):
            parts = [x_ref[q, pl.ds(at, step), :] for q in range(slots)]
            lane = lax.broadcasted_iota(jnp.int32, (step, LANES), 1)
            turned = [pltpu.roll(part, LANES // 2, 1) for part in (parts[:slabs] if h else parts[slabs:])]
            joined = [
                jnp.where(lane < LANES // 2, turned[u] if h else parts[u], parts[u + slabs] if h else turned[u])
                for u in range(slabs)
            ]
            for j, value in enumerate(exchange_groups(joined, width)):
                pack[j, pl.ds(h * rows + at, step), :] = value

        with jax.named_scope("pack"):
            over(c, body)

    def put(target, p, row, value):
        lane = lax.broadcasted_iota(jnp.int32, value.shape, 1)
        size = value.shape[0]
        swapped = jnp.take_along_axis(value, jnp.where(lane // width % 2 == 0, lane + width, lane - width), axis=1)
        target[pl.ds((planes + p) * plane + rows + row, size), :] = value
        target[pl.ds((planes + p) * plane + row, size), :] = swapped
        target[pl.ds((planes + p) * plane + 2 * rows + row, size), :] = swapped
        target[pl.ds(p * plane + rows + row, size), :] = pltpu.roll(value, 2 * width, 1)
        target[pl.ds((2 * planes + p) * plane + rows + row, size), :] = pltpu.roll(value, LANES - 2 * width, 1)

    taps = [-0.5 * c / HALF_WIDTH for c in STENCIL]

    def sweep(source, target, first, low=0, high=rows_y // 2):
        def body(y, carry):
            for p in range(planes):
                def line(q, yy):
                    row = pl.multiple_of((planes + q) * plane + rows + yy * rows_z, rows_z)
                    return source[pl.ds(row, rows_z), :]

                row = pl.multiple_of(y * rows_z, rows_z)
                centre = line(p, y)
                total = level[pl.ds(p * rows + row, rows_z), :] * centre
                for m in range(1, REACH + 1):
                    near = line(p + m, y) + line(p - m, y) + line(p, y + m) + line(p, y - m)
                    near += pltpu.roll(centre, m, 0) + pltpu.roll(centre, rows_z - m, 0)
                    total += taps[m] * near
                if not first:
                    total = 2.0 * total - target[pl.ds((planes + p) * plane + rows + row, rows_z), :]
                put(target, p, row, total)
            return carry

        lax.fori_loop(low, high, body, 0, unroll=rows_y // 4)

    def filter_half(h, ready):
        for c in range(2):
            with jax.named_scope("wait_a"):
                wait(pack, land, h, c, out_sems)

            def unpack(at):
                parts = [land[i, pl.ds(h * rows + at, step), :] for i in range(slabs)]
                for p, value in enumerate(exchange_groups(parts, 2 * width)):
                    put(wide_a, p, at, value)

            with jax.named_scope("unpack"):
                over(c, unpack)
        source, target = wide_a, wide_b
        with jax.named_scope("sweep"):
            for order in range(DEGREE - 1):
                sweep(source, target, order == 0)
                source, target = target, source
        for c in range(2):
            with jax.named_scope("sweep"):
                sweep(source, target, False, c * rows_y // 4, (c + 1) * rows_y // 4)

            def body(at):
                parts = [target[pl.ds((planes + p) * plane + rows + at, step), :] for p in range(planes)]
                for i, value in enumerate(exchange_groups(parts, 2 * width)):
                    pack_back[i, pl.ds(h * rows + at, step), :] = value

            with jax.named_scope("pack_b"):
                over(c, body)
            ready(c)

    def fold_part(h, c, store):
        with jax.named_scope("wait_b"):
            wait(pack_back, land_back, h, c, back_sems)

        def body(at):
            parts = [land_back[j, pl.ds(h * rows + at, step), :] for j in range(slabs)]
            for k, value in enumerate(exchange_groups(parts, width)):
                row = pl.multiple_of(c * part_rows + k * sub + at - c * sub, step)
                store(pl.ds(row, step), value)

        with jax.named_scope("fold"):
            over(c, body)

    pot_wide[...] = jnp.zeros_like(pot_wide)
    pot_wide[: planes * rows_y, :rows_z] = pot_ref[...]
    pot_mine[...] = pot_wide[...].T[:rows_z]
    fetch(0).wait()
    pack_part(0, 0)
    with jax.named_scope("barrier"):
        pl.semaphore_wait(barrier, slabs - 1 + orbs - 1)
    exchange(slabs, here, p_send, p_recv, lambda there: pot_mine, pot_land)
    send(pack, land, 0, 0, out_sems)
    fetch(1).wait()
    pack_part(0, 1)
    send(pack, land, 0, 1, out_sems)
    for c in range(2):
        pack_part(1, c)
    pot_land[here] = pot_mine[...]
    with jax.named_scope("level"):
        wait_exchange(slabs, here, p_send, p_recv, lambda there: pot_mine, pot_land)
        lane = lax.broadcasted_iota(jnp.int32, (rows_z, LANES), 1)
        lane_slot = lane // width
        held = LANES // 2
        fields = [
            jnp.where(lane < held, pot_land[2 * s], pltpu.roll(pot_land[2 * s + 1], held, 1))
            for s in range(slabs // 2)
        ]
        first = lane_slot // 2 % 2 * held + lane_slot % 2 * (rows_y // 2)
        for p in range(planes):
            for y in range(rows_y // 2):
                taken = [
                    jnp.take_along_axis(field, first + (p * rows_y + y), axis=1) for field in fields
                ]
                value = jnp.where(lane < held, taken[0], taken[1])
                level[pl.ds(p * rows + y * rows_z, rows_z), :] = (
                    value - (SHIFT_MID + 1.5 * STENCIL[0])
                ) * (1.0 / HALF_WIDTH)

    starts, arrive, passed = link_orders()

    def along(way, origin, h):
        view = gath.at[origin * 2 + core, h * part_rows : (h + 1) * part_rows]
        return pltpu.make_async_remote_copy(
            src_ref=view,
            dst_ref=view,
            send_sem=along_send.at[way, origin * 2 + h],
            recv_sem=along_recv.at[way, origin * 2 + h],
            device_id={"orb": (chip + 1 - 2 * way) * 2 + core},
            device_id_type=MESH,
        )

    def direct(z):
        way, h = (0, 1) if z == 0 else (1, 0)
        view = gath.at[z * 2 + core, h * part_rows : (h + 1) * part_rows]
        return pltpu.make_async_remote_copy(
            src_ref=view,
            dst_ref=view,
            send_sem=direct_send.at[0],
            recv_sem=along_recv.at[way, z * 2 + h],
            device_id={"orb": (z + 2 - 4 * way) * 2 + core},
            device_id_type=MESH,
        )

    def across(origin, h, side):
        view = gath.at[origin * 2 + side, h * part_rows : (h + 1) * part_rows]
        return pltpu.make_async_remote_copy(
            src_ref=view,
            dst_ref=view,
            send_sem=across_send.at[origin * 2 + h],
            recv_sem=across_recv.at[origin * 2 + h],
            device_id={"orb": partner},
            device_id_type=MESH,
        )

    def on_chip(z, body):
        pl.when(chip == z)(body)

    def by_chip(table, body):
        for z in table:
            def run():
                for item in table[z]:
                    body(*item)

            on_chip(z, run)

    own_items = {z: [(0, z, h) for h in range(2)] for z in range(chips)}

    def begin(c):
        on_chip((chips - 1) * (1 - c), lambda: direct((chips - 1) * (1 - c)).start())
        by_chip(starts[c], lambda *item: along(*item).start())
        for z in range(chips):
            on_chip(z, lambda: across(z, c, core).start())

    def receive(t):
        def one(way, o, h):
            along(way, o, h).wait_recv()
            across(o, h, core).start()

        with jax.named_scope("receive"):
            by_chip(arrive[t], one)

    def forward(t):
        by_chip(passed[t], lambda *item: along(*item).start())

    def settle(t):
        with jax.named_scope("settle"):
            by_chip(arrive[t], lambda way, o, h: across(o, h, 1 - core).wait_recv())

    def settle_own():
        by_chip(own_items, lambda way, o, h: across(o, h, 1 - core).wait_recv())

    def drain(first, past):
        for z in range(chips):
            def run():
                if first == 0 and z in (0, chips - 1):
                    direct(z).wait_send()
                sent = (starts if first == 0 else []) + passed[first:past]
                for table in sent:
                    for item in table.get(z, []):
                        along(*item).wait_send()
                for h in range(2 if first == 0 else 0):
                    across(z, h, core).wait_send()
                for table in arrive[first:past]:
                    for way, o, h in table.get(z, []):
                        across(o, h, core).wait_send()

            on_chip(z, run)

    for c in range(2):
        send(pack, land, 1, c, out_sems)
    filter_half(0, lambda c: send(pack_back, land_back, 0, c, back_sems))

    def store_panel(at, value):
        gath[me, at, :] = value

    for c in range(2):
        fold_part(0, c, store_panel)
        begin(c)

    filter_half(1, lambda c: send(pack_back, land_back, 1, c, back_sems))
    receive(0)
    forward(0)
    receive(1)
    forward(1)
    settle_own()
    settle(0)
    settle(1)

    tiles = chips * (chips + 1) // 2
    share = tiles // 2
    duties = [[(3, (0, 1, 2, 3)), (0, (0,))], [(2, (0, 1, 2)), (1, (0, 1))]]
    block = share * LANES // slabs
    centre = (chip + 1) // 2 == 1

    piece = block // 2

    def block_at(s, g):
        return pl.ds(pl.multiple_of(s * block + g * piece, 8), piece)

    def pair(z, at):
        return jnp.concatenate([gath[z * 2, at, :], gath[z * 2 + 1, at, :]], axis=1)

    @pl.when(centre)
    def _():
        at = pl.ds(pl.multiple_of((chip - 1) * part_rows, part_rows), part_rows)

        with jax.named_scope("gram"):
            for c, groups in enumerate(duties):
                def run():
                    n = 0
                    for za, zbs in groups:
                        left = pieces(pair(za, at).T)
                        for zb in zbs:
                            product = dot_pieces(left, pieces(pair(zb, at)), (1, 0))
                            for r, value in enumerate(unfolded(product, 2)):
                                gram_part[n * LANES + r * panel_dev : n * LANES + (r + 1) * panel_dev, :] = value
                            n += 1

                pl.when(core == c)(run)
        for g in range(2):
            exchange(
                slabs, here, r_send.at[g], r_recv.at[g],
                lambda there: gram_part.at[block_at(there, g)], gram_land.at[g],
            )

    def spread(g, index, there):
        view = gram_chip.at[g, index]
        return pltpu.make_async_remote_copy(
            src_ref=view,
            dst_ref=view,
            send_sem=z_send.at[g, there],
            recv_sem=z_recv.at[g, index],
            device_id={"orb": there * 2 + core},
            device_id_type=MESH,
        )

    for g in range(2):
        @pl.when(centre)
        def _():
            with jax.named_scope("wait_r"):
                wait_exchange(
                    slabs, here, r_send.at[g], r_recv.at[g],
                    lambda there: gram_part.at[block_at(there, g)], gram_land.at[g],
                )
            gram_land[g, here] = gram_part[block_at(here, g), :]
            total = gram_land[g, 0]
            for s in range(1, slabs):
                total += gram_land[g, s]
            gram_chip[g, chip - 1] = total / points_all

        for z in range(1, 3):
            def body():
                for there in range(chips):
                    if there != z:
                        spread(g, z - 1, there).start()

            on_chip(z, body)
    forward(2)
    weight_ref[...] = jnp.zeros_like(weight_ref)

    def gram_side(g, side, s):
        view = gram_all.at[side, block_at(s, g)]
        return pltpu.make_async_remote_copy(
            src_ref=view,
            dst_ref=view,
            send_sem=t_send.at[g, s],
            recv_sem=t_recv.at[g, s],
            device_id={"orb": partner},
            device_id_type=MESH,
        )

    def plane_copy(g, hop, s, there):
        view = gram_all.at[core, block_at(s, g)]
        return pltpu.make_async_remote_copy(
            src_ref=view,
            dst_ref=view,
            send_sem=s_send.at[g, hop],
            recv_sem=s_recv.at[g, hop],
            device_id={"space": there},
            device_id_type=MESH,
        )

    for g in range(2):
        with jax.named_scope("wait_z"):
            for z in range(chips):
                def body():
                    for index in range(2):
                        if z != index + 1:
                            spread(g, index, z).wait_recv()

                on_chip(z, body)
        gram_all[core, block_at(here, g), :] = gram_chip[g, 0] + gram_chip[g, 1]
        for hop in range(1, slabs):
            plane_copy(g, hop, here, lax.rem(here + hop, slabs)).start()
        gram_side(g, core, here).start()

    def store_rest(at, value):
        rest_ref[at, :] = value

    for c in range(2):
        fold_part(1, c, store_rest)

    def couple_part(z, k):
        at = pl.ds(pl.multiple_of(k * 2 * LANES, 2 * LANES), 2 * LANES)
        return dot_pieces(pieces(rest_ref[at, :]), pieces(pair(z, at)), (0, 0))

    def couple_send(n, total):
        value = unfolded(total, 1)[0]
        cross_part[n] = value
        cross_land[n, here] = value
        exchange(slabs, here, c_send.at[n], c_recv.at[n], lambda there: cross_part.at[n], cross_land.at[n])

    def couple(n, z):
        with jax.named_scope("couple"):
            total = lax.fori_loop(
                0, fold // (2 * LANES), lambda k, total: total + couple_part(z, k),
                jnp.zeros((LANES, 2 * LANES), jnp.float32),
            )
        couple_send(n, total)

    lower = chip // 2
    order = [chip, chip + 1 - 2 * lax.rem(chip, 2), 2 - lower, 3 - 3 * lower]
    receive(2)
    forward(3)
    with jax.named_scope("drain"):
        drain(0, 3)
        for z in range(1, 3):
            def body():
                for g in range(2):
                    for there in range(chips):
                        if there != z:
                            spread(g, z - 1, there).wait_send()

            on_chip(z, body)
    with jax.named_scope("wait_s"):
        for g in range(2):
            for hop in range(1, slabs):
                source = lax.rem(here + slabs - hop, slabs)
                plane_copy(g, hop, source, lax.rem(here + hop, slabs)).wait_recv()
                gram_side(g, core, source).start()
    settle(2)
    with jax.named_scope("wait_t"):
        for g in range(2):
            for s in range(slabs):
                gram_side(g, 1 - core, s).wait_recv()

    n = LANES
    inverse[...] = jnp.zeros_like(inverse)
    for c, groups in enumerate(duties):
        for k, (za, zb) in enumerate([(za, zb) for za, zbs in groups for zb in zbs]):
            work[za * n : (za + 1) * n, zb * n : (zb + 1) * n] = gram_all[c, k * n : (k + 1) * n, :]

    def between(b):
        if b == 0:
            receive(3)
            forward(4)
            receive(4)
        if b == 1:
            settle(3)
            settle(4)
        if b == 2:
            receive(5)
            settle(5)
            couple(3, order[3])

    for b in range(chips):
        at, past = slice(b * n, (b + 1) * n), slice((b + 1) * n, PANEL)
        with jax.named_scope("diag"):
            diag_in = work[at, at]
            if b:
                before, done = slice((b - 1) * n, b * n), slice(0, b * n)
                if b < chips - 1:
                    lower_part = work[past, before]
                    work[past, at] -= dot(lower_part, work[at, before], (1, 1))
                    work[past, past] -= dot(lower_part, lower_part, (1, 1))
                inner = dot(work[at, done], inverse[done, done], (1, 0))
            tied = None
            for k in range(fold // (2 * LANES) if b < chips - 1 else 0):
                term = couple_part(order[b], k)
                tied = term if tied is None else tied + term
            diag = tile_inverse(diag_in)
            inverse[at, at] = diag
            if b < chips - 1:
                couple_send(b, tied)
        with jax.named_scope("panel"):
            if b < chips - 1:
                scaled = dot(work[past, at], diag, (1, 1))
                work[past, at] = scaled
                work[(b + 1) * n : (b + 2) * n, (b + 1) * n : (b + 2) * n] -= dot(scaled[:n], scaled[:n], (1, 1))
            if b:
                inverse[at, done] = -dot(diag, inner, (1, 0))
        between(b)

    with jax.named_scope("cross"):
        for k in range(chips):
            wait_exchange(
                slabs, here, c_send.at[k], c_recv.at[k], lambda there: cross_part.at[k], cross_land.at[k]
            )
            total = cross_land[k, 0]
            for s in range(1, slabs):
                total += cross_land[k, s]
            cross[:, pl.ds(pl.multiple_of(order[k] * LANES, LANES), LANES)] = total / points_all
    with jax.named_scope("weights"):
        factors = pieces(inverse[...])
        middle = dot_pieces(pieces(cross[...]), factors, (1, 1))
        trail = -dot_pieces(pieces(middle), factors, (1, 0))
        own = inverse[pl.ds(pl.multiple_of(me * panel_dev, panel_dev), panel_dev), :]
        turned = jnp.concatenate([own, trail], axis=0).T
        for o in range(orbs):
            value = turned[o * panel_dev : (o + 1) * panel_dev]
            weight_ref[o * LANES : o * LANES + panel_dev, :LANES] = value
            weight_ref[o * LANES + panel_dev : (o + 1) * LANES, LANES:] = value
    with jax.named_scope("last"):
        drain(3, 6)
    for g in range(2):
        for hop in range(1, slabs):
            plane_copy(g, hop, here, lax.rem(here + hop, slabs)).wait_send()
        for s in range(slabs):
            gram_side(g, core, s).wait_send()


def final_kernel(gath_ref, rest_ref, weight_ref, out_ref, high, low):
    orbs, fold, n = gath_ref.shape
    rows = out_ref.shape[1] * out_ref.shape[3]
    i = pl.program_id(0)

    @pl.when(i == 0)
    def _():
        high[...], low[...] = pieces(weight_ref[...])

    at = pl.ds(pl.multiple_of(i * rows, rows), rows)
    total = None
    for z in range(orbs // 2):
        k = slice(z * 2 * n, (z + 1) * 2 * n)
        pair = jnp.concatenate([gath_ref[z * 2, at, :], gath_ref[z * 2 + 1, at, :]], axis=1)
        value = dot_pieces(pieces(pair), (high[k, :], low[k, :]), (1, 0))
        total = value if total is None else total + value
    lanes = lax.broadcasted_iota(jnp.int32, (rows, n), 1)
    kept = rest_ref[at, :]
    count = out_ref.shape[1]
    for h in range(2):
        held = kept if h else pltpu.roll(kept, n // 2, 1)
        value = jnp.where(lanes < n // 2, 0.0, held) + total[:, h * n : (h + 1) * n]
        for k in range(count):
            out_ref[h, k, 0] = value[k * (rows // count) : (k + 1) * (rows // count)]


def early_device(slabs, orbs, orbitals, potential):
    planes, rows_y, rows_z, columns = orbitals.shape
    points = planes * rows_y * rows_z
    panel_dev = PANEL // orbs
    chips = orbs // 2
    slots = 2 * slabs
    rows = points // slots
    fold = points // 2
    tiles = chips * (chips + 1) // 2
    block = tiles // 2 * LANES // slabs
    f32 = jnp.float32
    vmem = pl.BlockSpec(memory_space=pltpu.VMEM)
    dma = pltpu.SemaphoreType.DMA
    gath, rest, weight = pl.pallas_call(
        functools.partial(early_kernel, slabs, orbs, (planes, rows_y, rows_z)),
        out_shape=[
            jax.ShapeDtypeStruct((orbs, fold, LANES), f32),
            jax.ShapeDtypeStruct((fold, LANES), f32),
            jax.ShapeDtypeStruct((orbs * LANES, 2 * LANES), f32),
        ],
        in_specs=[pl.BlockSpec(memory_space=pltpu.HBM), vmem],
        out_specs=[vmem] * 3,
        scratch_shapes=[
            pltpu.VMEM((slots, rows, LANES), f32),
            pltpu.VMEM((LANES, LANES), f32),
            pltpu.VMEM((rows_z, LANES), f32),
        ]
        + [pltpu.VMEM((slabs, points // slabs, LANES), f32)] * 4
        + [
            pltpu.VMEM((slabs, rows_z, LANES), f32),
            pltpu.VMEM((9 * points // 2, LANES), f32),
            pltpu.VMEM((9 * points // 2, LANES), f32),
            pltpu.VMEM((points // 2, LANES), f32),
            pltpu.VMEM((slabs * block, LANES), f32),
            pltpu.VMEM((2, slabs, block // 2, LANES), f32),
            pltpu.VMEM((2, 2, block // 2, LANES), f32),
            pltpu.VMEM((2, slabs * block, LANES), f32),
            pltpu.VMEM((chips, panel_dev, LANES), f32),
            pltpu.VMEM((chips, slabs, panel_dev, LANES), f32),
            pltpu.VMEM((panel_dev, PANEL), f32),
            pltpu.VMEM((PANEL, PANEL), f32),
            pltpu.VMEM((PANEL, PANEL), f32),
        ]
        + [dma((2,))]
        + [dma((4, slabs))] * 2
        + [dma((slabs,))] * 2
        + [dma((4, slabs))] * 2
        + [dma((2, orbs))] * 2
        + [dma((1,))]
        + [dma((orbs,))] * 2
        + [dma((2, slabs))] * 2
        + [dma((2, chips)), dma((2, 2))]
        + [dma((2, slabs))] * 4
        + [dma((chips, slabs))] * 2,
        compiler_params=pltpu.CompilerParams(
            collective_id=0, has_side_effects=True, vmem_limit_bytes=40 << 20
        ),
    )(orbitals.reshape(slots, rows, columns), potential.reshape(planes * rows_y, rows_z))
    whole = [pl.BlockSpec(memory_space=pltpu.VMEM)] * 3
    out = pl.pallas_call(
        final_kernel,
        grid=(slabs,),
        out_shape=jax.ShapeDtypeStruct((2, slabs, 2, rows // 2, LANES), f32),
        in_specs=whole,
        out_specs=pl.BlockSpec(
            (2, slabs // 2, 1, rows // 2, LANES), lambda i: (0, i % 2, i // 2, 0, 0)
        ),
        scratch_shapes=[pltpu.VMEM((orbs * LANES, 2 * LANES), jnp.bfloat16)] * 2,
        compiler_params=pltpu.CompilerParams(vmem_limit_bytes=16 << 20),
    )(gath, rest, weight)
    return out.reshape(planes, rows_y, rows_z, columns)


def per_device(slabs, orbs, orbitals, potential):
    planes, rows_y, rows_z, columns = orbitals.shape
    points = planes * rows_y * rows_z
    panel_dev = PANEL // orbs
    folds = LANES // panel_dev
    thin = points // LANES
    f32 = jnp.float32
    vmem = pl.BlockSpec(memory_space=pltpu.VMEM)
    dma = pltpu.SemaphoreType.DMA
    steps = max(orbs // 2 - 1, 1)
    split = folds == 2 and planes == slabs and rows_y // 2 >= REACH and steps >= 2
    if split and orbs == 8 and slabs == 4 and PANEL == 4 * LANES and 2 * planes * rows_y == LANES:
        return early_device(slabs, orbs, orbitals, potential)
    flat = orbitals.reshape(points, columns)
    own, panel, gram, cross = pl.pallas_call(
        functools.partial(filter_kernel, slabs, orbs, (planes, rows_y, rows_z), split),
        out_shape=[
            jax.ShapeDtypeStruct((points, LANES), f32),
            jax.ShapeDtypeStruct((points, PANEL), f32),
            jax.ShapeDtypeStruct((PANEL, PANEL), f32),
            jax.ShapeDtypeStruct((LANES, PANEL), f32),
        ],
        in_specs=[vmem] * 2,
        out_specs=[vmem] * 4,
        scratch_shapes=[pltpu.VMEM((slabs, points // slabs, LANES), f32)] * 4
        + [
            pltpu.VMEM((slabs, thin, LANES), f32),
            pltpu.VMEM(((9 if split else 6) * points // 2, LANES), f32),
            pltpu.VMEM(((9 if split else 6) * points // 2, LANES), f32),
            pltpu.VMEM((points, LANES), f32),
            pltpu.VMEM((orbs, points // folds, LANES), f32),
            pltpu.VMEM((LANES, PANEL), f32),
            pltpu.VMEM((slabs, LANES, PANEL), f32),
            pltpu.VMEM((orbs, panel_dev, PANEL), f32),
        ]
        + [dma((slabs,))] * 14
        + [dma((2, steps))] * 2 + [dma((2 * steps + 1,))] * 2
        + [dma((2, steps))] * 2 + [dma((2 * steps + 1,))] * 2,
        compiler_params=pltpu.CompilerParams(
            collective_id=0, has_side_effects=True, vmem_limit_bytes=32 << 20
        ),
    )(flat, potential.reshape(LANES, thin).T)
    out = pl.pallas_call(
        functools.partial(solve_kernel, orbs),
        out_shape=jax.ShapeDtypeStruct((points, LANES), f32),
        in_specs=[vmem] * 4,
        out_specs=vmem,
        scratch_shapes=[
            pltpu.VMEM((PANEL, PANEL), f32),
            pltpu.VMEM((PANEL, PANEL), f32),
            pltpu.VMEM((LANES, PANEL), f32),
        ],
        compiler_params=pltpu.CompilerParams(vmem_limit_bytes=32 << 20),
    )(own, panel, gram, cross)
    return out.reshape(planes, rows_y, rows_z, columns)


def solution(mesh):
    placed = (P("space", None, None, "orb"), P("space", None, None))
    return jax.shard_map(
        functools.partial(per_device, mesh.shape["space"], mesh.shape["orb"]),
        mesh=mesh,
        in_specs=placed,
        out_specs=P("space", None, None, "orb"),
        check_vma=False,
    )
```

```python
import functools

import jax
import jax.numpy as jnp
from jax import lax
from jax.experimental import pallas as pl
from jax.experimental.pallas import tpu as pltpu
from jax.sharding import PartitionSpec as P

PANEL = 512
DEGREE = 4

STENCIL = (-205.0 / 72.0, 8.0 / 5.0, -1.0 / 5.0, 8.0 / 315.0, -1.0 / 560.0)
SHIFT_MID = 7.25
HALF_WIDTH = 4.75
LANES = 128
REACH = 4
MESH = pl.DeviceIdType.MESH
HIGHEST = lax.Precision.HIGHEST


def dot(a, b, dims):
    return lax.dot_general(
        a, b, ((dims[:1], dims[1:]), ((), ())), precision=HIGHEST, preferred_element_type=jnp.float32
    )


def regroup(load, store, count, rows):
    width = LANES // count
    step = min(rows, max(8, 128 // count))
    group = lax.broadcasted_iota(jnp.int32, (step, LANES), 1) // width

    def body(block, carry):
        here = pl.ds(pl.multiple_of(block * step, step), step)
        parts = [load(r, here) for r in range(count)]
        for j in range(count):
            out = None
            for r in range(count):
                turn = ((r - j) * width) % LANES
                piece = pltpu.roll(parts[r], turn, 1) if turn else parts[r]
                out = piece if out is None else jnp.where(group == r, piece, out)
            store(j, here, out)
        return carry

    lax.fori_loop(0, rows // step, body, 0)


def exchange(slots, here, send_sem, recv_sem, send, land):
    copies = []
    for hop in range(1, slots):
        there = lax.rem(here + hop, slots)
        copy = pltpu.make_async_remote_copy(
            src_ref=send(there),
            dst_ref=land.at[here],
            send_sem=send_sem.at[hop - 1],
            recv_sem=recv_sem.at[hop - 1],
            device_id={"space": there},
            device_id_type=MESH,
        )
        copy.start()
        copies.append(copy)
    return copies


def wait_exchange(slots, here, send_sem, recv_sem, send, land):
    for hop in range(1, slots):
        there = lax.rem(here + hop, slots)
        source = lax.rem(here + slots - hop, slots)
        pltpu.make_async_remote_copy(
            src_ref=send(there),
            dst_ref=land.at[source],
            send_sem=send_sem.at[hop - 1],
            recv_sem=recv_sem.at[hop - 1],
            device_id={"space": there},
            device_id_type=MESH,
        ).wait()


def gather_orb(count, me, buf, send_sem, recv_sem, side_send, side_recv, arrived=lambda chip: None, during=None):
    chips = count // 2
    chip, core = me // 2, lax.rem(me, 2)
    partner = chip * 2 + (1 - core)

    def along(origin, to, way, step):
        slot = buf.at[origin * 2 + core]
        return pltpu.make_async_remote_copy(
            src_ref=slot,
            dst_ref=slot,
            send_sem=send_sem.at[way, step],
            recv_sem=recv_sem.at[way, step],
            device_id={"orb": to * 2 + core},
            device_id_type=MESH,
        )

    def across(origin, side, index):
        slot = buf.at[origin * 2 + side]
        return pltpu.make_async_remote_copy(
            src_ref=slot,
            dst_ref=slot,
            send_sem=side_send.at[index],
            recv_sem=side_recv.at[index],
            device_id={"orb": partner},
            device_id_type=MESH,
        )

    steps = chips - 1

    def finish(step):
        @pl.when(chip - 1 - step >= 0)
        def _():
            across(chip - 1 - step, 1 - core, 1 + step).wait_recv()
            arrived(chip - 1 - step)

        @pl.when(chip + 1 + step < chips)
        def _():
            across(chip + 1 + step, 1 - core, 1 + steps + step).wait_recv()
            arrived(chip + 1 + step)

    for step in range(steps):
        @pl.when((chip - step >= 0) & (chip + 1 < chips))
        def _():
            along(chip - step, chip + 1, 0, step).start()

        @pl.when((chip + step < chips) & (chip - 1 >= 0))
        def _():
            along(chip + step, chip - 1, 1, step).start()

        if step == 0:
            across(chip, core, 0).start()
            if during:
                during[0]()
        if step == (1 if during else 0):
            if during:
                during[1]()
            across(chip, 1 - core, 0).wait_recv()
            arrived(chip)
        if step:
            finish(step - 1)

        @pl.when(chip - 1 - step >= 0)
        def _():
            along(chip - 1 - step, chip, 0, step).wait_recv()
            across(chip - 1 - step, core, 1 + step).start()

        @pl.when(chip + 1 + step < chips)
        def _():
            along(chip + 1 + step, chip, 1, step).wait_recv()
            across(chip + 1 + step, core, 1 + steps + step).start()

    finish(steps - 1)
    across(chip, core, 0).wait_send()
    for step in range(steps):
        @pl.when((chip - step >= 0) & (chip + 1 < chips))
        def _():
            along(chip - step, chip + 1, 0, step).wait_send()

        @pl.when((chip + step < chips) & (chip - 1 >= 0))
        def _():
            along(chip + step, chip - 1, 1, step).wait_send()

        @pl.when(chip - 1 - step >= 0)
        def _():
            across(chip - 1 - step, core, 1 + step).wait_send()

        @pl.when(chip + 1 + step < chips)
        def _():
            across(chip + 1 + step, core, 1 + steps + step).wait_send()


def split_filter(
    slabs, shape, here, me, x_ref, pot_ref, own_ref, pack, land, pack_back, land_back, pot_land,
    wide_a, wide_b, level, gath, out_sems, pot_sems, back_sems,
):
    planes, rows_y, rows_z = shape
    points = planes * rows_y * rows_z
    slots = 2 * slabs
    width = LANES // slots
    rows = points // slots
    plane = 3 * rows
    thin = points // LANES
    step = 16
    slot = lax.broadcasted_iota(jnp.int32, (step, LANES), 1) // width

    def merge(parts):
        out = None
        for u, (value, v) in enumerate(parts):
            turn = ((u - v) * width) % LANES
            value = pltpu.roll(value, turn, 1) if turn else value
            out = value if out is None else jnp.where(slot == u, value, out)
        return out

    def over(body):
        def one(block, carry):
            body(pl.multiple_of(block * step, step))
            return carry

        lax.fori_loop(0, rows // step, one, 0)

    def half(buf, h):
        return buf.at[:, h * rows : (h + 1) * rows]

    def send(buf, landing, h, sems):
        exchange(slabs, here, *sems[h], lambda there: half(buf, h).at[there], half(landing, h))
        landing[here, h * rows : (h + 1) * rows] = buf[here, h * rows : (h + 1) * rows]

    def wait(buf, landing, h, sems):
        wait_exchange(slabs, here, *sems[h], lambda there: half(buf, h).at[there], half(landing, h))

    def pack_half(h):
        def body(at):
            parts = [x_ref[pl.ds(q * rows + at, step), :] for q in range(slots)]
            for j in range(slabs):
                pack[j, pl.ds(h * rows + at, step), :] = merge([(part, h * slabs + j) for part in parts])

        over(body)
        send(pack, land, h, out_sems)

    def put(target, p, row, value):
        odd = lax.rem(lax.broadcasted_iota(jnp.int32, value.shape, 1) // width, 2)
        size = value.shape[0]
        swapped = jnp.where(odd == 0, pltpu.roll(value, LANES - width, 1), pltpu.roll(value, width, 1))
        target[pl.ds((planes + p) * plane + rows + row, size), :] = value
        target[pl.ds((planes + p) * plane + row, size), :] = swapped
        target[pl.ds((planes + p) * plane + 2 * rows + row, size), :] = swapped
        target[pl.ds(p * plane + rows + row, size), :] = pltpu.roll(value, 2 * width, 1)
        target[pl.ds((2 * planes + p) * plane + rows + row, size), :] = pltpu.roll(value, LANES - 2 * width, 1)

    taps = [-0.5 * c / HALF_WIDTH for c in STENCIL]

    def sweep(source, target, first):
        def body(y, carry):
            for p in range(planes):
                def line(q, yy):
                    row = pl.multiple_of((planes + q) * plane + rows + yy * rows_z, rows_z)
                    return source[pl.ds(row, rows_z), :]

                row = pl.multiple_of(y * rows_z, rows_z)
                centre = line(p, y)
                total = level[pl.ds(p * rows + row, rows_z), :] * centre
                for m in range(1, REACH + 1):
                    near = line(p + m, y) + line(p - m, y) + line(p, y + m) + line(p, y - m)
                    near += pltpu.roll(centre, m, 0) + pltpu.roll(centre, rows_z - m, 0)
                    total += taps[m] * near
                if not first:
                    total = 2.0 * total - target[pl.ds((planes + p) * plane + rows + row, rows_z), :]
                put(target, p, row, total)
            return carry

        lax.fori_loop(0, rows_y // 2, body, 0)

    def filter_half(h):
        wait(pack, land, h, out_sems)

        def unpack(at):
            parts = [land[i, pl.ds(h * rows + at, step), :] for i in range(slabs)]
            for p in range(planes):
                put(wide_a, p, at, merge([(parts[u // 2], 2 * p + u % 2) for u in range(slots)]))

        over(unpack)
        sweep(wide_a, wide_b, True)
        source, target = wide_b, wide_a
        for _ in range(DEGREE - 1):
            sweep(source, target, False)
            source, target = target, source

        def body(at):
            parts = [source[pl.ds((planes + p) * plane + rows + at, step), :] for p in range(planes)]
            for i in range(slabs):
                pack_back[i, pl.ds(h * rows + at, step), :] = merge(
                    [(parts[q // 2], 2 * i + q % 2) for q in range(slots)]
                )

        over(body)
        send(pack_back, land_back, h, back_sems)

    pack_half(0)
    pack_half(1)
    pot_land[here] = pot_ref[...]
    wait_exchange(slabs, here, *pot_sems, lambda there: pot_ref, pot_land)
    lane_slot = lax.broadcasted_iota(jnp.int32, (thin, LANES), 1) // width
    fields = [pot_land[s] for s in range(slabs)]
    pieces = rows // thin
    for p in range(planes):
        for e in range(pieces):
            value = None
            for u in range(slots):
                l = (2 * p + u % 2) * pieces + e
                spread = jnp.broadcast_to(fields[u // 2][:, l : l + 1], (thin, LANES))
                value = spread if value is None else jnp.where(lane_slot == u, spread, value)
            level[pl.ds(p * rows + e * thin, thin), :] = (
                value - (SHIFT_MID + 1.5 * STENCIL[0])
            ) * (1.0 / HALF_WIDTH)

    filter_half(0)
    wait(pack_back, land_back, 0, back_sems)

    def fold_own(at):
        parts = [land_back[j, pl.ds(at, step), :] for j in range(slabs)]
        for k in range(slabs):
            gath[me, pl.ds(k * rows + at, step), :] = merge(
                [(parts[u % slabs], (u // slabs) * slabs + k) for u in range(slots)]
            )

    over(fold_own)

    def finish():
        wait(pack_back, land_back, 1, back_sems)

        def body(at):
            parts = [
                land_back[u % slabs, pl.ds((u // slabs) * rows + at, step), :] for u in range(slots)
            ]
            for q in range(slots):
                own_ref[pl.ds(q * rows + at, step), :] = merge([(part, q) for part in parts])

        over(body)

    return (lambda: filter_half(1)), finish


def filter_kernel(
    slabs, orbs, shape, split,
    x_ref, pot_ref, own_ref, panel_ref, gram_ref, cross_ref,
    pack, land, pack_back, land_back, pot_land, wide_a, wide_b, level, gath, part, part_land, rows_land,
    a_send, a_recv, p_send, p_recv, b_send, b_recv, c_send, c_recv, d_send, d_recv, e_send, e_recv, f_send, f_recv,
    g_send, g_recv, gs_send, gs_recv, h_send, h_recv, hs_send, hs_recv,
):
    planes, rows_y, rows_z = shape
    points = planes * rows_y * rows_z
    here, me = lax.axis_index("space"), lax.axis_index("orb")
    chunk = points // slabs
    width = LANES // slabs

    barrier = pltpu.get_barrier_semaphore()
    for hop in range(1, slabs):
        pl.semaphore_signal(
            barrier, inc=1, device_id={"space": lax.rem(here + hop, slabs)}, device_id_type=MESH
        )
    for hop in range(1, orbs):
        pl.semaphore_signal(
            barrier, inc=1, device_id={"orb": lax.rem(me + hop, orbs)}, device_id_type=MESH
        )
    pl.semaphore_wait(barrier, slabs - 1 + orbs - 1)

    exchange(slabs, here, p_send, p_recv, lambda there: pot_ref, pot_land)

    panel_dev = PANEL // orbs
    folds = LANES // panel_dev
    fold = points // folds
    during = None
    if split:
        during = split_filter(
            slabs, shape, here, me, x_ref, pot_ref, own_ref, pack, land, pack_back, land_back, pot_land,
            wide_a, wide_b, level, gath,
            ((a_send, a_recv), (e_send, e_recv)), (p_send, p_recv), ((b_send, b_recv), (f_send, f_recv)),
        )
    else:
        def store_pack(j, at, value):
            pack[j, at, :] = value

        regroup(lambda r, at: x_ref[pl.ds(r * chunk + at.start, at.size), :], store_pack, slabs, chunk)
        exchange(slabs, here, a_send, a_recv, lambda there: pack.at[there], land)
        land[here] = pack[here]
        pot_land[here] = pot_ref[...]
        wait_exchange(slabs, here, p_send, p_recv, lambda there: pot_ref, pot_land)

        thin = points // LANES
        lane_group = lax.broadcasted_iota(jnp.int32, (thin, LANES), 1) // width
        fields = [pot_land[s] for s in range(slabs)]
        for l in range(LANES):
            value = None
            for s in range(slabs):
                spread = jnp.broadcast_to(fields[s][:, l : l + 1], (thin, LANES))
                value = spread if value is None else jnp.where(lane_group == s, spread, value)
            level[pl.ds(l * thin, thin), :] = (value - (SHIFT_MID + 1.5 * STENCIL[0])) * (1.0 / HALF_WIDTH)

        wait_exchange(slabs, here, a_send, a_recv, lambda there: pack.at[there], land)

        def put(target, row, value):
            target[pl.ds(points + row, value.shape[0]), :] = value
            target[pl.ds(row, value.shape[0]), :] = pltpu.roll(value, width, 1)
            target[pl.ds(2 * points + row, value.shape[0]), :] = pltpu.roll(value, LANES - width, 1)

        regroup(
            lambda r, at: land[r, at, :],
            lambda j, at, value: put(wide_a, j * chunk + at.start, value),
            slabs, chunk,
        )

        plane = rows_y * rows_z
        taps = [-0.5 * c / HALF_WIDTH for c in STENCIL]

        def sweep(source, target, first):
            def body(y, carry):
                for p in range(planes):
                    def line(q, yy):
                        return source[pl.ds(pl.multiple_of(points + q * plane + yy * rows_z, rows_z), rows_z), :]

                    row = pl.multiple_of(p * plane + y * rows_z, rows_z)
                    centre = line(p, y)
                    total = level[pl.ds(row, rows_z), :] * centre
                    for m in range(1, REACH + 1):
                        near = line(p + m, y) + line(p - m, y)
                        near += line(p, lax.rem(y + m, rows_y)) + line(p, lax.rem(y + rows_y - m, rows_y))
                        near += pltpu.roll(centre, m, 0) + pltpu.roll(centre, rows_z - m, 0)
                        total += taps[m] * near
                    if not first:
                        before = target[pl.ds(pl.multiple_of(points + row, rows_z), rows_z), :]
                        total = 2.0 * total - before
                    put(target, row, total)
                return carry

            lax.fori_loop(0, rows_y, body, 0)

        sweep(wide_a, wide_b, True)
        source, target = wide_b, wide_a
        for _ in range(DEGREE - 1):
            sweep(source, target, False)
            source, target = target, source

        def store_back(j, at, value):
            pack_back[j, at, :] = value

        regroup(
            lambda r, at: source[pl.ds(points + r * chunk + at.start, at.size), :], store_back, slabs, chunk
        )
        exchange(slabs, here, b_send, b_recv, lambda there: pack_back.at[there], land_back)
        land_back[here] = pack_back[here]
        wait_exchange(slabs, here, b_send, b_recv, lambda there: pack_back.at[there], land_back)

        def store_own(j, at, value):
            own_ref[pl.ds(j * chunk + at.start, at.size), :] = value

        regroup(lambda r, at: land_back[r, at, :], store_own, slabs, chunk)

        step = min(fold, 32)
        fold_group = lax.broadcasted_iota(jnp.int32, (step, LANES), 1) // panel_dev

        def folded(block, carry):
            at = pl.multiple_of(block * step, step)
            out = None
            for r in range(folds):
                piece = own_ref[pl.ds(r * fold + at, step), :]
                piece = pltpu.roll(piece, r * panel_dev, 1) if r else piece
                out = piece if out is None else jnp.where(fold_group == r, piece, out)
            gath[me, pl.ds(at, step), :] = out
            return carry

        lax.fori_loop(0, fold // step, folded, 0)

    block = 512

    def take(tile):
        lanes = pl.ds(pl.multiple_of(tile * LANES, LANES), LANES)

        def store_panel(j, at, value):
            panel_ref[pl.ds(j * fold + at.start, at.size), lanes] = value

        regroup(lambda r, at: gath[tile * folds + r, at, :], store_panel, folds, fold)

        def product(k, total):
            at = pl.ds(pl.multiple_of(k * block, block), block)
            return total + dot(own_ref[at, :], panel_ref[at, lanes], (0, 0))

        part[:, lanes] = lax.fori_loop(
            0, points // block, product, jnp.zeros((LANES, LANES), jnp.float32)
        )

    if folds == 2:
        gather_orb(orbs, me, gath, g_send, g_recv, gs_send, gs_recv, take, during)
    else:
        gather_orb(orbs, me, gath, g_send, g_recv, gs_send, gs_recv)

        def each(tile, carry):
            take(tile)
            return carry

        lax.fori_loop(0, PANEL // LANES, each, 0)

    top, rest = part.at[:panel_dev], part.at[panel_dev:]
    top_land, rest_land = part_land.at[:, :panel_dev], part_land.at[:, panel_dev:]
    exchange(slabs, here, c_send, c_recv, lambda there: top, top_land)
    exchange(slabs, here, d_send, d_recv, lambda there: rest, rest_land)
    part_land[here] = part[...]
    points_all = points * slabs

    def summed(view):
        total = view[0]
        for s in range(1, slabs):
            total += view[s]
        return total / points_all

    wait_exchange(slabs, here, c_send, c_recv, lambda there: top, top_land)
    rows_land[me] = summed(top_land)
    gather_orb(orbs, me, rows_land, h_send, h_recv, hs_send, hs_recv)
    wait_exchange(slabs, here, d_send, d_recv, lambda there: rest, rest_land)
    cross_ref[:panel_dev, :] = jnp.zeros((panel_dev, PANEL), jnp.float32)
    cross_ref[panel_dev:, :] = summed(rest_land)
    for o in range(orbs):
        gram_ref[o * panel_dev : (o + 1) * panel_dev, :] = rows_land[o]


def block_inverse(a):
    n = LANES
    tiles = n // 8
    rows = lax.broadcasted_iota(jnp.int32, (8, n), 0)
    cols = lax.broadcasted_iota(jnp.int32, (8, n), 1)
    work = [a[8 * t : 8 * t + 8] for t in range(tiles)]
    unit = [jnp.where(rows + 8 * t == cols, 1.0, 0.0).astype(jnp.float32) for t in range(tiles)]
    for t0 in range(tiles):
        base = 8 * t0
        columns = [jnp.broadcast_to(work[t0][:, base + k : base + k + 1], (8, n)) for k in range(8)]
        small = {
            (i, k): jnp.broadcast_to(columns[k][i : i + 1], (8, n)) for i in range(8) for k in range(i + 1)
        }
        lower, scales = {}, []
        for j in range(8):
            scales.append(1.0 / small[j, j])
            for i in range(j + 1, 8):
                lower[i, j] = small[i, j] * scales[j]
            for i in range(j + 1, 8):
                for k in range(j + 1, i + 1):
                    small[i, k] = small[i, k] - lower[i, j] * small[k, j]
        turned = {}
        for j in range(8):
            for i in range(j + 1, 8):
                value = lower[i, j]
                for k in range(j + 1, i):
                    value = value + lower[i, k] * turned[k, j]
                turned[i, j] = -value
        a_row, u_row = work[t0], unit[t0]
        a_new, u_new = a_row, u_row
        for k in range(7):
            weight = jnp.zeros((8, n), jnp.float32)
            for i in range(k + 1, 8):
                weight = jnp.where(rows == i, turned[i, k], weight)
            a_new = a_new + weight * jnp.broadcast_to(a_row[k : k + 1], (8, n))
            u_new = u_new + weight * jnp.broadcast_to(u_row[k : k + 1], (8, n))
        work[t0], unit[t0] = a_new, u_new
        if t0 == tiles - 1:
            break
        a_out = u_out = None
        for i in range(8):
            weight = jnp.where(rows == i, scales[i], 0.0)
            for k in range(i):
                weight = jnp.where(rows == k, turned[i, k] * scales[i], weight)
            a_term = weight * jnp.broadcast_to(a_new[i : i + 1], (8, n))
            u_term = weight * jnp.broadcast_to(u_new[i : i + 1], (8, n))
            a_out = a_term if a_out is None else a_out + a_term
            u_out = u_term if u_out is None else u_out + u_term
        a_rows = [jnp.broadcast_to(a_out[k : k + 1], (8, n)) for k in range(8)]
        u_rows = [jnp.broadcast_to(u_out[k : k + 1], (8, n)) for k in range(8)]
        for t in range(t0 + 1, tiles):
            before = work[t]
            for k in range(8):
                column = jnp.broadcast_to(before[:, base + k : base + k + 1], (8, n))
                work[t] = work[t] - column * a_rows[k]
                unit[t] = unit[t] - column * u_rows[k]
    out = []
    for t in range(tiles):
        pivots = jnp.sum(jnp.where(rows + 8 * t == cols, work[t], 0.0), axis=1, keepdims=True)
        out.append(unit[t] * (1.0 / jnp.sqrt(pivots)))
    return jnp.concatenate(out, axis=0)


def solve_kernel(orbs, own_ref, panel_ref, gram_ref, cross_ref, out_ref, work, inverse, weights):
    panel_dev = PANEL // orbs
    me = lax.axis_index("orb")
    n = LANES
    blocks = PANEL // n
    work[...] = gram_ref[...]
    inverse[...] = jnp.zeros_like(inverse)

    def factor(b, carry):
        at = pl.multiple_of(b * n, n)
        diag = block_inverse(work[pl.ds(at, n), pl.ds(at, n)])
        inverse[pl.ds(at, n), pl.ds(at, n)] = diag
        for i in range(1, blocks):
            @pl.when(i > b)
            def _():
                work[i * n : (i + 1) * n, pl.ds(at, n)] = dot(
                    work[i * n : (i + 1) * n, pl.ds(at, n)], diag, (1, 1)
                )
        for i in range(1, blocks):
            @pl.when(i > b)
            def _():
                left = work[i * n : (i + 1) * n, pl.ds(at, n)]
                for k in range(1, i + 1):
                    @pl.when(k > b)
                    def _():
                        right = work[k * n : (k + 1) * n, pl.ds(at, n)]
                        work[i * n : (i + 1) * n, k * n : (k + 1) * n] -= dot(left, right, (1, 1))
        return carry

    lax.fori_loop(0, blocks, factor, 0)
    for i in range(1, blocks):
        span = i * n
        inner = dot(work[i * n : (i + 1) * n, :span], inverse[:span, :span], (1, 0))
        inverse[i * n : (i + 1) * n, :span] = -dot(
            inverse[i * n : (i + 1) * n, i * n : (i + 1) * n], inner, (1, 0)
        )

    middle = dot(cross_ref[...], inverse[...], (1, 1))
    weights[...] = -dot(middle, inverse[...], (1, 0))
    weights[:panel_dev, :] = inverse[pl.ds(pl.multiple_of(me * panel_dev, panel_dev), panel_dev), :]
    points = own_ref.shape[0]
    block = 256
    lanes = lax.broadcasted_iota(jnp.int32, (block, LANES), 1)

    def final(k, carry):
        at = pl.ds(pl.multiple_of(k * block, block), block)
        kept = jnp.where(lanes < panel_dev, 0.0, own_ref[at, :])
        out_ref[at, :] = kept + dot(panel_ref[at, :], weights[...], (1, 1))
        return carry

    lax.fori_loop(0, points // block, final, 0)


def pieces(x):
    high = x.astype(jnp.bfloat16)
    return high, (x - high.astype(jnp.float32)).astype(jnp.bfloat16)


def dot_pieces(a, b, dims):
    def one(left, right):
        return lax.dot_general(
            left, right, ((dims[:1], dims[1:]), ((), ())), preferred_element_type=jnp.float32
        )

    return one(a[0], b[0]) + (one(a[0], b[1]) + one(a[1], b[0]))


def unfolded(product, rows):
    half = LANES // 2
    lanes = lax.broadcasted_iota(jnp.int32, (half, LANES), 1)
    out = []
    for r in range(rows):
        sides = []
        for c in range(2):
            at = product[r * LANES : (r + 1) * LANES, c * LANES : (c + 1) * LANES]
            sides.append(at[:half] + pltpu.roll(at[half:], half, 1))
        out.append(jnp.where(lanes < half, sides[0], pltpu.roll(sides[1], half, 1)))
    return out


def link_orders():
    def both(table):
        out = {z: list(items) for z, items in table.items()}
        for z, items in table.items():
            out[3 - z] = [(1 - way, 3 - o, 1 - h) for way, o, h in items]
        return out

    starts = [
        {0: [(0, 0, 0)], 1: [(1, 1, 0)], 2: [(1, 2, 0), (0, 2, 0)]},
        {0: [(0, 0, 1)], 1: [(0, 1, 1), (1, 1, 1)], 2: [(0, 2, 1)], 3: [(1, 3, 1), (1, 3, 0)]},
    ]
    arrive = [
        both({1: [(1, 2, 0)]}),
        both({0: [(1, 1, 0), (1, 1, 1)], 1: [(0, 0, 0), (1, 3, 0)]}),
        both({0: [(1, 2, 0)], 1: [(0, 0, 1), (1, 2, 1)]}),
        both({0: [(1, 3, 0)], 1: [(1, 3, 1)]}),
        both({0: [(1, 2, 1)]}),
        both({0: [(1, 3, 1)]}),
    ]
    passed = [
        both({1: [(1, 2, 0)]}),
        both({1: [(0, 1, 0)]}),
        both({1: [(0, 0, 0), (1, 3, 0)]}),
        both({1: [(1, 2, 1)]}),
        both({1: [(1, 3, 1)]}),
    ]
    return starts, arrive, passed


def tile_inverse(a):
    n = LANES
    tiles = n // 8
    rows = lax.broadcasted_iota(jnp.int32, (8, n), 0)
    lanes = lax.broadcasted_iota(jnp.int32, (8, n), 1)

    def row_of(value, k):
        return jnp.broadcast_to(value[k : k + 1], (8, n))

    def column_of(value, k):
        return jnp.broadcast_to(value[:, k : k + 1], (8, n))

    def tree(terms):
        while len(terms) > 1:
            paired = [terms[i] + terms[i + 1] for i in range(0, len(terms) - 1, 2)]
            terms = paired + terms[len(terms) - len(terms) % 2 :]
        return terms[0]

    work = [a[8 * t : 8 * t + 8] for t in range(tiles)]
    cols = [column_of(work[0], k) for k in range(8)]
    out = []
    for t0 in range(tiles):
        base = 8 * t0
        last = t0 == tiles - 1
        if not last:
            side = [column_of(work[t0 + 1], base + k) for k in range(8)]
            ahead = [column_of(work[t0 + 1], base + 8 + k) for k in range(8)]
            moved = list(side)
        below, pivots, scales = [], [], []
        for j in range(8):
            pivot = row_of(cols[j], j)
            scale = 1.0 / pivot
            lead = jnp.where(rows > j, cols[j], 0.0)
            pivots.append(pivot)
            scales.append(scale)
            below.append(lead * scale)
            for k in range(j + 1, 8):
                part = row_of(cols[k], j) * scale
                cols[k] = cols[k] - lead * part
                if not last:
                    moved[k] = moved[k] - moved[j] * part
        above = cols
        if not last:
            scaled = [moved[j] * scales[j] for j in range(8)]
            cols = [
                ahead[k] - tree([scaled[j] * row_of(moved[j], k) for j in range(8)]) for k in range(8)
            ]
        inside = (lanes >= base) & (lanes < base + 8)
        value = jnp.where(inside, jnp.where(lanes == rows + base, 1.0, 0.0), work[t0])
        root, turn = pivots[0], scales[0]
        for j in range(8):
            value = value - below[j] * row_of(value, j)
            if j:
                root = jnp.where(rows == j, pivots[j], root)
                turn = jnp.where(rows == j, scales[j], turn)
        out.append(jnp.where(lanes < base + 8, value * lax.rsqrt(root), 0.0))
        if last:
            break
        value = value * turn
        for k in range(7, 0, -1):
            value = value - jnp.where(rows < k, above[k] * turn, 0.0) * row_of(value, k)
        leads = [row_of(value, k) for k in range(8)]
        for t in range(t0 + 1, tiles):
            before = work[t]
            columns = side if t == t0 + 1 else [column_of(before, base + k) for k in range(8)]
            work[t] = jnp.where(inside, 0.0, before) - tree([columns[k] * leads[k] for k in range(8)])
    return jnp.concatenate(out, axis=0)


def early_kernel(
    slabs, orbs, shape,
    x_hbm, pot_ref, gath, rest_ref, weight_ref,
    x_ref, pot_wide, pot_mine, pack, land, pack_back, land_back, pot_land, wide_a, wide_b, level,
    gram_part, gram_land, gram_chip, gram_all, cross_part, cross_land, cross, work, inverse,
    x_sem, a_send, a_recv, p_send, p_recv, b_send, b_recv,
    along_send, along_recv, direct_send, across_send, across_recv,
    r_send, r_recv, z_send, z_recv, s_send, s_recv, t_send, t_recv, c_send, c_recv,
):
    planes, rows_y, rows_z = shape
    points = planes * rows_y * rows_z
    here, me = lax.axis_index("space"), lax.axis_index("orb")
    chips = orbs // 2
    chip, core = me // 2, lax.rem(me, 2)
    partner = chip * 2 + (1 - core)
    slots = 2 * slabs
    width = LANES // slots
    rows = points // slots
    plane = 3 * rows
    sub = rows // 2
    fold = points // 2
    part_rows = fold // 2
    panel_dev = PANEL // orbs
    points_all = points * slabs
    step = 16

    def fetch(c):
        view = slice(c * sub, (c + 1) * sub)
        return pltpu.make_async_copy(x_hbm.at[:, view], x_ref.at[:, view], x_sem.at[c])

    for c in range(2):
        fetch(c).start()

    barrier = pltpu.get_barrier_semaphore()
    for hop in range(1, slabs):
        pl.semaphore_signal(
            barrier, inc=1, device_id={"space": lax.rem(here + hop, slabs)}, device_id_type=MESH
        )
    for hop in range(1, orbs):
        pl.semaphore_signal(
            barrier, inc=1, device_id={"orb": lax.rem(me + hop, orbs)}, device_id_type=MESH
        )

    def exchange_groups(x, unit):
        lane = lax.broadcasted_iota(jnp.int32, (step, LANES), 1) // unit
        outer, inner = lane // 2 % 2 == 0, lane % 2 == 0
        pairs = [None] * 4
        for a in range(2):
            pairs[a] = jnp.where(outer, x[a], pltpu.roll(x[a + 2], 2 * unit, 1))
            pairs[a + 2] = jnp.where(outer, pltpu.roll(x[a], LANES - 2 * unit, 1), x[a + 2])
        out = [None] * 4
        for a in (0, 2):
            out[a] = jnp.where(inner, pairs[a], pltpu.roll(pairs[a + 1], unit, 1))
            out[a + 1] = jnp.where(inner, pltpu.roll(pairs[a], LANES - unit, 1), pairs[a + 1])
        return out

    def over(c, body):
        def one(block, carry):
            body(pl.multiple_of(c * sub + block * step, step))
            return carry

        lax.fori_loop(0, sub // step, one, 0, unroll=2)

    def span(h, c):
        return slice(h * rows + c * sub, h * rows + (c + 1) * sub)

    def send(buf, landing, h, c, sems):
        at, k = span(h, c), h * 2 + c
        exchange(
            slabs, here, sems[0].at[k], sems[1].at[k], lambda there: buf.at[there, at], landing.at[:, at]
        )
        landing[here, at] = buf[here, at]

    def wait(buf, landing, h, c, sems):
        at, k = span(h, c), h * 2 + c
        wait_exchange(
            slabs, here, sems[0].at[k], sems[1].at[k], lambda there: buf.at[there, at], landing.at[:, at]
        )

    out_sems, back_sems = (a_send, a_recv), (b_send, b_recv)

    def pack_part(h, c):
        def body(at):
            parts = [x_ref[q, pl.ds(at, step), :] for q in range(slots)]
            lane = lax.broadcasted_iota(jnp.int32, (step, LANES), 1)
            turned = [pltpu.roll(part, LANES // 2, 1) for part in (parts[:slabs] if h else parts[slabs:])]
            joined = [
                jnp.where(lane < LANES // 2, turned[u] if h else parts[u], parts[u + slabs] if h else turned[u])
                for u in range(slabs)
            ]
            for j, value in enumerate(exchange_groups(joined, width)):
                pack[j, pl.ds(h * rows + at, step), :] = value

        with jax.named_scope("pack"):
            over(c, body)

    def put(target, p, row, value):
        lane = lax.broadcasted_iota(jnp.int32, value.shape, 1)
        size = value.shape[0]
        swapped = jnp.take_along_axis(value, jnp.where(lane // width % 2 == 0, lane + width, lane - width), axis=1)
        target[pl.ds((planes + p) * plane + rows + row, size), :] = value
        target[pl.ds((planes + p) * plane + row, size), :] = swapped
        target[pl.ds((planes + p) * plane + 2 * rows + row, size), :] = swapped
        target[pl.ds(p * plane + rows + row, size), :] = pltpu.roll(value, 2 * width, 1)
        target[pl.ds((2 * planes + p) * plane + rows + row, size), :] = pltpu.roll(value, LANES - 2 * width, 1)

    taps = [-0.5 * c / HALF_WIDTH for c in STENCIL]

    def sweep(source, target, first, low=0, high=rows_y // 2):
        def body(y, carry):
            for p in range(planes):
                def line(q, yy):
                    row = pl.multiple_of((planes + q) * plane + rows + yy * rows_z, rows_z)
                    return source[pl.ds(row, rows_z), :]

                row = pl.multiple_of(y * rows_z, rows_z)
                centre = line(p, y)
                total = level[pl.ds(p * rows + row, rows_z), :] * centre
                for m in range(1, REACH + 1):
                    near = line(p + m, y) + line(p - m, y) + line(p, y + m) + line(p, y - m)
                    near += pltpu.roll(centre, m, 0) + pltpu.roll(centre, rows_z - m, 0)
                    total += taps[m] * near
                if not first:
                    total = 2.0 * total - target[pl.ds((planes + p) * plane + rows + row, rows_z), :]
                put(target, p, row, total)
            return carry

        lax.fori_loop(low, high, body, 0, unroll=rows_y // 4)

    def filter_half(h, ready):
        for c in range(2):
            with jax.named_scope("wait_a"):
                wait(pack, land, h, c, out_sems)

            def unpack(at):
                parts = [land[i, pl.ds(h * rows + at, step), :] for i in range(slabs)]
                for p, value in enumerate(exchange_groups(parts, 2 * width)):
                    put(wide_a, p, at, value)

            with jax.named_scope("unpack"):
                over(c, unpack)
        source, target = wide_a, wide_b
        with jax.named_scope("sweep"):
            for order in range(DEGREE - 1):
                sweep(source, target, order == 0)
                source, target = target, source
        for c in range(2):
            with jax.named_scope("sweep"):
                sweep(source, target, False, c * rows_y // 4, (c + 1) * rows_y // 4)

            def body(at):
                parts = [target[pl.ds((planes + p) * plane + rows + at, step), :] for p in range(planes)]
                for i, value in enumerate(exchange_groups(parts, 2 * width)):
                    pack_back[i, pl.ds(h * rows + at, step), :] = value

            with jax.named_scope("pack_b"):
                over(c, body)
            ready(c)

    def fold_part(h, c, store):
        with jax.named_scope("wait_b"):
            wait(pack_back, land_back, h, c, back_sems)

        def body(at):
            parts = [land_back[j, pl.ds(h * rows + at, step), :] for j in range(slabs)]
            for k, value in enumerate(exchange_groups(parts, width)):
                row = pl.multiple_of(c * part_rows + k * sub + at - c * sub, step)
                store(pl.ds(row, step), value)

        with jax.named_scope("fold"):
            over(c, body)

    pot_wide[...] = jnp.zeros_like(pot_wide)
    pot_wide[: planes * rows_y, :rows_z] = pot_ref[...]
    pot_mine[...] = pot_wide[...].T[:rows_z]
    for c in range(2):
        fetch(c).wait()
        pack_part(0, c)
    with jax.named_scope("barrier"):
        pl.semaphore_wait(barrier, slabs - 1 + orbs - 1)
    exchange(slabs, here, p_send, p_recv, lambda there: pot_mine, pot_land)
    for c in range(2):
        send(pack, land, 0, c, out_sems)
    for c in range(2):
        pack_part(1, c)
    pot_land[here] = pot_mine[...]
    with jax.named_scope("level"):
        wait_exchange(slabs, here, p_send, p_recv, lambda there: pot_mine, pot_land)
        lane = lax.broadcasted_iota(jnp.int32, (rows_z, LANES), 1)
        lane_slot = lane // width
        held = LANES // 2
        fields = [
            jnp.where(lane < held, pot_land[2 * s], pltpu.roll(pot_land[2 * s + 1], held, 1))
            for s in range(slabs // 2)
        ]
        first = lane_slot // 2 % 2 * held + lane_slot % 2 * (rows_y // 2)
        for p in range(planes):
            for y in range(rows_y // 2):
                taken = [
                    jnp.take_along_axis(field, first + (p * rows_y + y), axis=1) for field in fields
                ]
                value = jnp.where(lane < held, taken[0], taken[1])
                level[pl.ds(p * rows + y * rows_z, rows_z), :] = (
                    value - (SHIFT_MID + 1.5 * STENCIL[0])
                ) * (1.0 / HALF_WIDTH)

    starts, arrive, passed = link_orders()

    def along(way, origin, h):
        view = gath.at[origin * 2 + core, h * part_rows : (h + 1) * part_rows]
        return pltpu.make_async_remote_copy(
            src_ref=view,
            dst_ref=view,
            send_sem=along_send.at[way, origin * 2 + h],
            recv_sem=along_recv.at[origin * 2 + h],
            device_id={"orb": (chip + 1 - 2 * way) * 2 + core},
            device_id_type=MESH,
        )

    def direct(z):
        way, h = (0, 1) if z == 0 else (1, 0)
        view = gath.at[z * 2 + core, h * part_rows : (h + 1) * part_rows]
        return pltpu.make_async_remote_copy(
            src_ref=view,
            dst_ref=view,
            send_sem=direct_send.at[0],
            recv_sem=along_recv.at[z * 2 + h],
            device_id={"orb": (z + 2 - 4 * way) * 2 + core},
            device_id_type=MESH,
        )

    def across(origin, h, side):
        view = gath.at[origin * 2 + side, h * part_rows : (h + 1) * part_rows]
        return pltpu.make_async_remote_copy(
            src_ref=view,
            dst_ref=view,
            send_sem=across_send.at[origin * 2 + h],
            recv_sem=across_recv.at[origin * 2 + h],
            device_id={"orb": partner},
            device_id_type=MESH,
        )

    def on_chip(z, body):
        pl.when(chip == z)(body)

    def by_chip(table, body):
        for z in table:
            def run():
                for item in table[z]:
                    body(*item)

            on_chip(z, run)

    own_items = {z: [(0, z, h) for h in range(2)] for z in range(chips)}

    def begin(c):
        on_chip((chips - 1) * (1 - c), lambda: direct((chips - 1) * (1 - c)).start())
        by_chip(starts[c], lambda *item: along(*item).start())
        for z in range(chips):
            on_chip(z, lambda: across(z, c, core).start())

    def receive(t):
        def one(way, o, h):
            along(way, o, h).wait_recv()
            across(o, h, core).start()

        with jax.named_scope("receive"):
            by_chip(arrive[t], one)

    def forward(t):
        by_chip(passed[t], lambda *item: along(*item).start())

    def settle(t):
        with jax.named_scope("settle"):
            by_chip(arrive[t], lambda way, o, h: across(o, h, 1 - core).wait_recv())

    def settle_own():
        by_chip(own_items, lambda way, o, h: across(o, h, 1 - core).wait_recv())

    def drain(first, past):
        for z in range(chips):
            def run():
                if first == 0 and z in (0, chips - 1):
                    direct(z).wait_send()
                sent = (starts if first == 0 else []) + passed[first:past]
                for table in sent:
                    for item in table.get(z, []):
                        along(*item).wait_send()
                for h in range(2 if first == 0 else 0):
                    across(z, h, core).wait_send()
                for table in arrive[first:past]:
                    for way, o, h in table.get(z, []):
                        across(o, h, core).wait_send()

            on_chip(z, run)

    for c in range(2):
        send(pack, land, 1, c, out_sems)
    filter_half(0, lambda c: send(pack_back, land_back, 0, c, back_sems))

    def store_panel(at, value):
        gath[me, at, :] = value

    for c in range(2):
        fold_part(0, c, store_panel)
        begin(c)

    filter_half(1, lambda c: None)
    receive(0)
    forward(0)
    receive(1)
    forward(1)
    settle_own()
    settle(0)
    settle(1)

    tiles = chips * (chips + 1) // 2
    share = tiles // 2
    duties = [[(3, (0, 1, 2, 3)), (0, (0,))], [(2, (0, 1, 2)), (1, (0, 1))]]
    block = share * LANES // slabs
    centre = (chip + 1) // 2 == 1

    piece = block // 2

    def block_at(s, g):
        return pl.ds(pl.multiple_of(s * block + g * piece, 8), piece)

    def pair(z, at):
        return jnp.concatenate([gath[z * 2, at, :], gath[z * 2 + 1, at, :]], axis=1)

    @pl.when(centre)
    def _():
        at = pl.ds(pl.multiple_of((chip - 1) * part_rows, part_rows), part_rows)

        with jax.named_scope("gram"):
            for c, groups in enumerate(duties):
                def run():
                    n = 0
                    for za, zbs in groups:
                        left = pieces(pair(za, at).T)
                        for zb in zbs:
                            product = dot_pieces(left, pieces(pair(zb, at)), (1, 0))
                            for r, value in enumerate(unfolded(product, 2)):
                                gram_part[n * LANES + r * panel_dev : n * LANES + (r + 1) * panel_dev, :] = value
                            n += 1

                pl.when(core == c)(run)
        for g in range(2):
            exchange(
                slabs, here, r_send.at[g], r_recv.at[g],
                lambda there: gram_part.at[block_at(there, g)], gram_land.at[g],
            )

    for c in range(2):
        send(pack_back, land_back, 1, c, back_sems)

    def spread(g, index, there):
        view = gram_chip.at[g, index]
        return pltpu.make_async_remote_copy(
            src_ref=view,
            dst_ref=view,
            send_sem=z_send.at[g, there],
            recv_sem=z_recv.at[g, index],
            device_id={"orb": there * 2 + core},
            device_id_type=MESH,
        )

    for g in range(2):
        @pl.when(centre)
        def _():
            with jax.named_scope("wait_r"):
                wait_exchange(
                    slabs, here, r_send.at[g], r_recv.at[g],
                    lambda there: gram_part.at[block_at(there, g)], gram_land.at[g],
                )
            gram_land[g, here] = gram_part[block_at(here, g), :]
            total = gram_land[g, 0]
            for s in range(1, slabs):
                total += gram_land[g, s]
            gram_chip[g, chip - 1] = total / points_all

        for z in range(1, 3):
            def body():
                for there in range(chips):
                    if there != z:
                        spread(g, z - 1, there).start()

            on_chip(z, body)
    forward(2)
    weight_ref[...] = jnp.zeros_like(weight_ref)
    with jax.named_scope("drain"):
        drain(0, 2)

    def gram_side(g, side, s):
        view = gram_all.at[side, block_at(s, g)]
        return pltpu.make_async_remote_copy(
            src_ref=view,
            dst_ref=view,
            send_sem=t_send.at[g, s],
            recv_sem=t_recv.at[g, s],
            device_id={"orb": partner},
            device_id_type=MESH,
        )

    def plane_copy(g, hop, s, there):
        view = gram_all.at[core, block_at(s, g)]
        return pltpu.make_async_remote_copy(
            src_ref=view,
            dst_ref=view,
            send_sem=s_send.at[g, hop - 1],
            recv_sem=s_recv.at[g, hop - 1],
            device_id={"space": there},
            device_id_type=MESH,
        )

    for g in range(2):
        with jax.named_scope("wait_z"):
            for z in range(chips):
                def body():
                    for index in range(2):
                        if z != index + 1:
                            spread(g, index, z).wait_recv()

                on_chip(z, body)
        gram_all[core, block_at(here, g), :] = gram_chip[g, 0] + gram_chip[g, 1]
        for hop in range(1, slabs):
            plane_copy(g, hop, here, lax.rem(here + hop, slabs)).start()
        gram_side(g, core, here).start()

    def store_rest(at, value):
        rest_ref[at, :] = value

    for c in range(2):
        fold_part(1, c, store_rest)

    def couple_part(z, k):
        at = pl.ds(pl.multiple_of(k * 2 * LANES, 2 * LANES), 2 * LANES)
        return dot_pieces(pieces(rest_ref[at, :]), pieces(pair(z, at)), (0, 0))

    def couple_send(n, total):
        value = unfolded(total, 1)[0]
        cross_part[n] = value
        cross_land[n, here] = value
        exchange(slabs, here, c_send.at[n], c_recv.at[n], lambda there: cross_part.at[n], cross_land.at[n])

    def couple(n, z):
        with jax.named_scope("couple"):
            total = couple_part(z, 0)
            for k in range(1, fold // (2 * LANES)):
                total += couple_part(z, k)
        couple_send(n, total)

    lower = chip // 2
    order = [chip, chip + 1 - 2 * lax.rem(chip, 2), 2 - lower, 3 - 3 * lower]
    receive(2)
    forward(3)
    with jax.named_scope("wait_s"):
        for g in range(2):
            for hop in range(1, slabs):
                source = lax.rem(here + slabs - hop, slabs)
                plane_copy(g, hop, source, lax.rem(here + hop, slabs)).wait_recv()
                gram_side(g, core, source).start()
    with jax.named_scope("wait_t"):
        for g in range(2):
            for s in range(slabs):
                gram_side(g, 1 - core, s).wait_recv()

    n = LANES
    inverse[...] = jnp.zeros_like(inverse)
    for c, groups in enumerate(duties):
        for k, (za, zb) in enumerate([(za, zb) for za, zbs in groups for zb in zbs]):
            work[za * n : (za + 1) * n, zb * n : (zb + 1) * n] = gram_all[c, k * n : (k + 1) * n, :]

    def between(b):
        if b == 0:
            settle(2)
            receive(3)
            forward(4)
            receive(4)
        if b == 1:
            settle(3)
            settle(4)
        if b == 2:
            receive(5)
            settle(5)
            couple(3, order[3])

    for b in range(chips):
        at, past = slice(b * n, (b + 1) * n), slice((b + 1) * n, PANEL)
        with jax.named_scope("diag"):
            diag_in = work[at, at]
            if b:
                before, done = slice((b - 1) * n, b * n), slice(0, b * n)
                if b < chips - 1:
                    lower_part = work[past, before]
                    work[past, at] -= dot(lower_part, work[at, before], (1, 1))
                    work[past, past] -= dot(lower_part, lower_part, (1, 1))
                inner = dot(work[at, done], inverse[done, done], (1, 0))
            tied = None
            for k in range(fold // (2 * LANES) if b < chips - 1 else 0):
                term = couple_part(order[b], k)
                tied = term if tied is None else tied + term
            diag = tile_inverse(diag_in)
            inverse[at, at] = diag
            if b < chips - 1:
                couple_send(b, tied)
        with jax.named_scope("panel"):
            if b < chips - 1:
                scaled = dot(work[past, at], diag, (1, 1))
                work[past, at] = scaled
                work[(b + 1) * n : (b + 2) * n, (b + 1) * n : (b + 2) * n] -= dot(scaled[:n], scaled[:n], (1, 1))
            if b:
                inverse[at, done] = -dot(diag, inner, (1, 0))
        between(b)

    with jax.named_scope("cross"):
        for k in range(chips):
            wait_exchange(
                slabs, here, c_send.at[k], c_recv.at[k], lambda there: cross_part.at[k], cross_land.at[k]
            )
            total = cross_land[k, 0]
            for s in range(1, slabs):
                total += cross_land[k, s]
            cross[:, pl.ds(pl.multiple_of(order[k] * LANES, LANES), LANES)] = total / points_all
    with jax.named_scope("weights"):
        factors = pieces(inverse[...])
        middle = dot_pieces(pieces(cross[...]), factors, (1, 1))
        trail = -dot_pieces(pieces(middle), factors, (1, 0))
        own = inverse[pl.ds(pl.multiple_of(me * panel_dev, panel_dev), panel_dev), :]
        turned = jnp.concatenate([own, trail], axis=0).T
        for o in range(orbs):
            value = turned[o * panel_dev : (o + 1) * panel_dev]
            weight_ref[o * LANES : o * LANES + panel_dev, :LANES] = value
            weight_ref[o * LANES + panel_dev : (o + 1) * LANES, LANES:] = value
    with jax.named_scope("last"):
        drain(2, 6)
        for z in range(1, 3):
            def body():
                for g in range(2):
                    for there in range(chips):
                        if there != z:
                            spread(g, z - 1, there).wait_send()

            on_chip(z, body)
    for g in range(2):
        for hop in range(1, slabs):
            plane_copy(g, hop, here, lax.rem(here + hop, slabs)).wait_send()
        for s in range(slabs):
            gram_side(g, core, s).wait_send()


def final_kernel(gath_ref, rest_ref, weight_ref, out_ref, high, low):
    orbs, fold, n = gath_ref.shape
    rows = out_ref.shape[1] * out_ref.shape[3]
    i = pl.program_id(0)

    @pl.when(i == 0)
    def _():
        high[...], low[...] = pieces(weight_ref[...])

    at = pl.ds(pl.multiple_of(i * rows, rows), rows)
    total = None
    for z in range(orbs // 2):
        k = slice(z * 2 * n, (z + 1) * 2 * n)
        pair = jnp.concatenate([gath_ref[z * 2, at, :], gath_ref[z * 2 + 1, at, :]], axis=1)
        value = dot_pieces(pieces(pair), (high[k, :], low[k, :]), (1, 0))
        total = value if total is None else total + value
    lanes = lax.broadcasted_iota(jnp.int32, (rows, n), 1)
    kept = rest_ref[at, :]
    count = out_ref.shape[1]
    for h in range(2):
        held = kept if h else pltpu.roll(kept, n // 2, 1)
        value = jnp.where(lanes < n // 2, 0.0, held) + total[:, h * n : (h + 1) * n]
        for k in range(count):
            out_ref[h, k, 0] = value[k * (rows // count) : (k + 1) * (rows // count)]


def early_device(slabs, orbs, orbitals, potential):
    planes, rows_y, rows_z, columns = orbitals.shape
    points = planes * rows_y * rows_z
    panel_dev = PANEL // orbs
    chips = orbs // 2
    slots = 2 * slabs
    rows = points // slots
    fold = points // 2
    tiles = chips * (chips + 1) // 2
    block = tiles // 2 * LANES // slabs
    f32 = jnp.float32
    vmem = pl.BlockSpec(memory_space=pltpu.VMEM)
    dma = pltpu.SemaphoreType.DMA
    gath, rest, weight = pl.pallas_call(
        functools.partial(early_kernel, slabs, orbs, (planes, rows_y, rows_z)),
        out_shape=[
            jax.ShapeDtypeStruct((orbs, fold, LANES), f32),
            jax.ShapeDtypeStruct((fold, LANES), f32),
            jax.ShapeDtypeStruct((orbs * LANES, 2 * LANES), f32),
        ],
        in_specs=[pl.BlockSpec(memory_space=pltpu.HBM), vmem],
        out_specs=[vmem] * 3,
        scratch_shapes=[
            pltpu.VMEM((slots, rows, LANES), f32),
            pltpu.VMEM((LANES, LANES), f32),
            pltpu.VMEM((rows_z, LANES), f32),
        ]
        + [pltpu.VMEM((slabs, points // slabs, LANES), f32)] * 4
        + [
            pltpu.VMEM((slabs, rows_z, LANES), f32),
            pltpu.VMEM((9 * points // 2, LANES), f32),
            pltpu.VMEM((9 * points // 2, LANES), f32),
            pltpu.VMEM((points // 2, LANES), f32),
            pltpu.VMEM((slabs * block, LANES), f32),
            pltpu.VMEM((2, slabs, block // 2, LANES), f32),
            pltpu.VMEM((2, 2, block // 2, LANES), f32),
            pltpu.VMEM((2, slabs * block, LANES), f32),
            pltpu.VMEM((chips, panel_dev, LANES), f32),
            pltpu.VMEM((chips, slabs, panel_dev, LANES), f32),
            pltpu.VMEM((panel_dev, PANEL), f32),
            pltpu.VMEM((PANEL, PANEL), f32),
            pltpu.VMEM((PANEL, PANEL), f32),
        ]
        + [dma((2,))]
        + [dma((4, slabs - 1))] * 2
        + [dma((slabs - 1,))] * 2
        + [dma((4, slabs - 1))] * 2
        + [dma((2, orbs)), dma((orbs,)), dma((1,))]
        + [dma((orbs,))] * 2
        + [dma((2, slabs - 1))] * 2
        + [dma((2, chips)), dma((2, 2))]
        + [dma((2, slabs - 1))] * 2
        + [dma((2, slabs))] * 2
        + [dma((chips, slabs - 1))] * 2,
        compiler_params=pltpu.CompilerParams(
            collective_id=0, has_side_effects=True, vmem_limit_bytes=40 << 20
        ),
    )(orbitals.reshape(slots, rows, columns), potential.reshape(planes * rows_y, rows_z))
    whole = [pl.BlockSpec(memory_space=pltpu.VMEM)] * 3
    out = pl.pallas_call(
        final_kernel,
        grid=(slabs,),
        out_shape=jax.ShapeDtypeStruct((2, slabs, 2, rows // 2, LANES), f32),
        in_specs=whole,
        out_specs=pl.BlockSpec(
            (2, slabs // 2, 1, rows // 2, LANES), lambda i: (0, i % 2, i // 2, 0, 0)
        ),
        scratch_shapes=[pltpu.VMEM((orbs * LANES, 2 * LANES), jnp.bfloat16)] * 2,
        compiler_params=pltpu.CompilerParams(vmem_limit_bytes=16 << 20),
    )(gath, rest, weight)
    return out.reshape(planes, rows_y, rows_z, columns)


def per_device(slabs, orbs, orbitals, potential):
    planes, rows_y, rows_z, columns = orbitals.shape
    points = planes * rows_y * rows_z
    panel_dev = PANEL // orbs
    folds = LANES // panel_dev
    thin = points // LANES
    f32 = jnp.float32
    vmem = pl.BlockSpec(memory_space=pltpu.VMEM)
    dma = pltpu.SemaphoreType.DMA
    steps = max(orbs // 2 - 1, 1)
    split = folds == 2 and planes == slabs and rows_y // 2 >= REACH and steps >= 2
    if split and orbs == 8 and slabs == 4 and PANEL == 4 * LANES and 2 * planes * rows_y == LANES:
        return early_device(slabs, orbs, orbitals, potential)
    flat = orbitals.reshape(points, columns)
    own, panel, gram, cross = pl.pallas_call(
        functools.partial(filter_kernel, slabs, orbs, (planes, rows_y, rows_z), split),
        out_shape=[
            jax.ShapeDtypeStruct((points, LANES), f32),
            jax.ShapeDtypeStruct((points, PANEL), f32),
            jax.ShapeDtypeStruct((PANEL, PANEL), f32),
            jax.ShapeDtypeStruct((LANES, PANEL), f32),
        ],
        in_specs=[vmem] * 2,
        out_specs=[vmem] * 4,
        scratch_shapes=[pltpu.VMEM((slabs, points // slabs, LANES), f32)] * 4
        + [
            pltpu.VMEM((slabs, thin, LANES), f32),
            pltpu.VMEM(((9 if split else 6) * points // 2, LANES), f32),
            pltpu.VMEM(((9 if split else 6) * points // 2, LANES), f32),
            pltpu.VMEM((points, LANES), f32),
            pltpu.VMEM((orbs, points // folds, LANES), f32),
            pltpu.VMEM((LANES, PANEL), f32),
            pltpu.VMEM((slabs, LANES, PANEL), f32),
            pltpu.VMEM((orbs, panel_dev, PANEL), f32),
        ]
        + [dma((slabs,))] * 14
        + [dma((2, steps))] * 2 + [dma((2 * steps + 1,))] * 2
        + [dma((2, steps))] * 2 + [dma((2 * steps + 1,))] * 2,
        compiler_params=pltpu.CompilerParams(
            collective_id=0, has_side_effects=True, vmem_limit_bytes=32 << 20
        ),
    )(flat, potential.reshape(LANES, thin).T)
    out = pl.pallas_call(
        functools.partial(solve_kernel, orbs),
        out_shape=jax.ShapeDtypeStruct((points, LANES), f32),
        in_specs=[vmem] * 4,
        out_specs=vmem,
        scratch_shapes=[
            pltpu.VMEM((PANEL, PANEL), f32),
            pltpu.VMEM((PANEL, PANEL), f32),
            pltpu.VMEM((LANES, PANEL), f32),
        ],
        compiler_params=pltpu.CompilerParams(vmem_limit_bytes=32 << 20),
    )(own, panel, gram, cross)
    return out.reshape(planes, rows_y, rows_z, columns)


def solution(mesh):
    placed = (P("space", None, None, "orb"), P("space", None, None))
    return jax.shard_map(
        functools.partial(per_device, mesh.shape["space"], mesh.shape["orb"]),
        mesh=mesh,
        in_specs=placed,
        out_specs=P("space", None, None, "orb"),
        check_vma=False,
    )
```

```python
import functools

import jax
import jax.numpy as jnp
from jax import lax
from jax.experimental import pallas as pl
from jax.experimental.pallas import tpu as pltpu
from jax.sharding import PartitionSpec as P

PANEL = 512
DEGREE = 4

STENCIL = (-205.0 / 72.0, 8.0 / 5.0, -1.0 / 5.0, 8.0 / 315.0, -1.0 / 560.0)
SHIFT_MID = 7.25
HALF_WIDTH = 4.75
LANES = 128
REACH = 4
MESH = pl.DeviceIdType.MESH
HIGHEST = lax.Precision.HIGHEST


def dot(a, b, dims):
    return lax.dot_general(
        a, b, ((dims[:1], dims[1:]), ((), ())), precision=HIGHEST, preferred_element_type=jnp.float32
    )


def regroup(load, store, count, rows):
    width = LANES // count
    step = min(rows, max(8, 128 // count))
    group = lax.broadcasted_iota(jnp.int32, (step, LANES), 1) // width

    def body(block, carry):
        here = pl.ds(pl.multiple_of(block * step, step), step)
        parts = [load(r, here) for r in range(count)]
        for j in range(count):
            out = None
            for r in range(count):
                turn = ((r - j) * width) % LANES
                piece = pltpu.roll(parts[r], turn, 1) if turn else parts[r]
                out = piece if out is None else jnp.where(group == r, piece, out)
            store(j, here, out)
        return carry

    lax.fori_loop(0, rows // step, body, 0)


def exchange(slots, here, send_sem, recv_sem, send, land):
    copies = []
    for hop in range(1, slots):
        there = lax.rem(here + hop, slots)
        copy = pltpu.make_async_remote_copy(
            src_ref=send(there),
            dst_ref=land.at[here],
            send_sem=send_sem.at[hop - 1],
            recv_sem=recv_sem.at[hop - 1],
            device_id={"space": there},
            device_id_type=MESH,
        )
        copy.start()
        copies.append(copy)
    return copies


def wait_exchange(slots, here, send_sem, recv_sem, send, land):
    for hop in range(1, slots):
        there = lax.rem(here + hop, slots)
        source = lax.rem(here + slots - hop, slots)
        pltpu.make_async_remote_copy(
            src_ref=send(there),
            dst_ref=land.at[source],
            send_sem=send_sem.at[hop - 1],
            recv_sem=recv_sem.at[hop - 1],
            device_id={"space": there},
            device_id_type=MESH,
        ).wait()


def gather_orb(count, me, buf, send_sem, recv_sem, side_send, side_recv, arrived=lambda chip: None, during=None):
    chips = count // 2
    chip, core = me // 2, lax.rem(me, 2)
    partner = chip * 2 + (1 - core)

    def along(origin, to, way, step):
        slot = buf.at[origin * 2 + core]
        return pltpu.make_async_remote_copy(
            src_ref=slot,
            dst_ref=slot,
            send_sem=send_sem.at[way, step],
            recv_sem=recv_sem.at[way, step],
            device_id={"orb": to * 2 + core},
            device_id_type=MESH,
        )

    def across(origin, side, index):
        slot = buf.at[origin * 2 + side]
        return pltpu.make_async_remote_copy(
            src_ref=slot,
            dst_ref=slot,
            send_sem=side_send.at[index],
            recv_sem=side_recv.at[index],
            device_id={"orb": partner},
            device_id_type=MESH,
        )

    steps = chips - 1

    def finish(step):
        @pl.when(chip - 1 - step >= 0)
        def _():
            across(chip - 1 - step, 1 - core, 1 + step).wait_recv()
            arrived(chip - 1 - step)

        @pl.when(chip + 1 + step < chips)
        def _():
            across(chip + 1 + step, 1 - core, 1 + steps + step).wait_recv()
            arrived(chip + 1 + step)

    for step in range(steps):
        @pl.when((chip - step >= 0) & (chip + 1 < chips))
        def _():
            along(chip - step, chip + 1, 0, step).start()

        @pl.when((chip + step < chips) & (chip - 1 >= 0))
        def _():
            along(chip + step, chip - 1, 1, step).start()

        if step == 0:
            across(chip, core, 0).start()
            if during:
                during[0]()
        if step == (1 if during else 0):
            if during:
                during[1]()
            across(chip, 1 - core, 0).wait_recv()
            arrived(chip)
        if step:
            finish(step - 1)

        @pl.when(chip - 1 - step >= 0)
        def _():
            along(chip - 1 - step, chip, 0, step).wait_recv()
            across(chip - 1 - step, core, 1 + step).start()

        @pl.when(chip + 1 + step < chips)
        def _():
            along(chip + 1 + step, chip, 1, step).wait_recv()
            across(chip + 1 + step, core, 1 + steps + step).start()

    finish(steps - 1)
    across(chip, core, 0).wait_send()
    for step in range(steps):
        @pl.when((chip - step >= 0) & (chip + 1 < chips))
        def _():
            along(chip - step, chip + 1, 0, step).wait_send()

        @pl.when((chip + step < chips) & (chip - 1 >= 0))
        def _():
            along(chip + step, chip - 1, 1, step).wait_send()

        @pl.when(chip - 1 - step >= 0)
        def _():
            across(chip - 1 - step, core, 1 + step).wait_send()

        @pl.when(chip + 1 + step < chips)
        def _():
            across(chip + 1 + step, core, 1 + steps + step).wait_send()


def split_filter(
    slabs, shape, here, me, x_ref, pot_ref, own_ref, pack, land, pack_back, land_back, pot_land,
    wide_a, wide_b, level, gath, out_sems, pot_sems, back_sems,
):
    planes, rows_y, rows_z = shape
    points = planes * rows_y * rows_z
    slots = 2 * slabs
    width = LANES // slots
    rows = points // slots
    plane = 3 * rows
    thin = points // LANES
    step = 16
    slot = lax.broadcasted_iota(jnp.int32, (step, LANES), 1) // width

    def merge(parts):
        out = None
        for u, (value, v) in enumerate(parts):
            turn = ((u - v) * width) % LANES
            value = pltpu.roll(value, turn, 1) if turn else value
            out = value if out is None else jnp.where(slot == u, value, out)
        return out

    def over(body):
        def one(block, carry):
            body(pl.multiple_of(block * step, step))
            return carry

        lax.fori_loop(0, rows // step, one, 0)

    def half(buf, h):
        return buf.at[:, h * rows : (h + 1) * rows]

    def send(buf, landing, h, sems):
        exchange(slabs, here, *sems[h], lambda there: half(buf, h).at[there], half(landing, h))
        landing[here, h * rows : (h + 1) * rows] = buf[here, h * rows : (h + 1) * rows]

    def wait(buf, landing, h, sems):
        wait_exchange(slabs, here, *sems[h], lambda there: half(buf, h).at[there], half(landing, h))

    def pack_half(h):
        def body(at):
            parts = [x_ref[pl.ds(q * rows + at, step), :] for q in range(slots)]
            for j in range(slabs):
                pack[j, pl.ds(h * rows + at, step), :] = merge([(part, h * slabs + j) for part in parts])

        over(body)
        send(pack, land, h, out_sems)

    def put(target, p, row, value):
        odd = lax.rem(lax.broadcasted_iota(jnp.int32, value.shape, 1) // width, 2)
        size = value.shape[0]
        swapped = jnp.where(odd == 0, pltpu.roll(value, LANES - width, 1), pltpu.roll(value, width, 1))
        target[pl.ds((planes + p) * plane + rows + row, size), :] = value
        target[pl.ds((planes + p) * plane + row, size), :] = swapped
        target[pl.ds((planes + p) * plane + 2 * rows + row, size), :] = swapped
        target[pl.ds(p * plane + rows + row, size), :] = pltpu.roll(value, 2 * width, 1)
        target[pl.ds((2 * planes + p) * plane + rows + row, size), :] = pltpu.roll(value, LANES - 2 * width, 1)

    taps = [-0.5 * c / HALF_WIDTH for c in STENCIL]

    def sweep(source, target, first):
        def body(y, carry):
            for p in range(planes):
                def line(q, yy):
                    row = pl.multiple_of((planes + q) * plane + rows + yy * rows_z, rows_z)
                    return source[pl.ds(row, rows_z), :]

                row = pl.multiple_of(y * rows_z, rows_z)
                centre = line(p, y)
                total = level[pl.ds(p * rows + row, rows_z), :] * centre
                for m in range(1, REACH + 1):
                    near = line(p + m, y) + line(p - m, y) + line(p, y + m) + line(p, y - m)
                    near += pltpu.roll(centre, m, 0) + pltpu.roll(centre, rows_z - m, 0)
                    total += taps[m] * near
                if not first:
                    total = 2.0 * total - target[pl.ds((planes + p) * plane + rows + row, rows_z), :]
                put(target, p, row, total)
            return carry

        lax.fori_loop(0, rows_y // 2, body, 0)

    def filter_half(h):
        wait(pack, land, h, out_sems)

        def unpack(at):
            parts = [land[i, pl.ds(h * rows + at, step), :] for i in range(slabs)]
            for p in range(planes):
                put(wide_a, p, at, merge([(parts[u // 2], 2 * p + u % 2) for u in range(slots)]))

        over(unpack)
        sweep(wide_a, wide_b, True)
        source, target = wide_b, wide_a
        for _ in range(DEGREE - 1):
            sweep(source, target, False)
            source, target = target, source

        def body(at):
            parts = [source[pl.ds((planes + p) * plane + rows + at, step), :] for p in range(planes)]
            for i in range(slabs):
                pack_back[i, pl.ds(h * rows + at, step), :] = merge(
                    [(parts[q // 2], 2 * i + q % 2) for q in range(slots)]
                )

        over(body)
        send(pack_back, land_back, h, back_sems)

    pack_half(0)
    pack_half(1)
    pot_land[here] = pot_ref[...]
    wait_exchange(slabs, here, *pot_sems, lambda there: pot_ref, pot_land)
    lane_slot = lax.broadcasted_iota(jnp.int32, (thin, LANES), 1) // width
    fields = [pot_land[s] for s in range(slabs)]
    pieces = rows // thin
    for p in range(planes):
        for e in range(pieces):
            value = None
            for u in range(slots):
                l = (2 * p + u % 2) * pieces + e
                spread = jnp.broadcast_to(fields[u // 2][:, l : l + 1], (thin, LANES))
                value = spread if value is None else jnp.where(lane_slot == u, spread, value)
            level[pl.ds(p * rows + e * thin, thin), :] = (
                value - (SHIFT_MID + 1.5 * STENCIL[0])
            ) * (1.0 / HALF_WIDTH)

    filter_half(0)
    wait(pack_back, land_back, 0, back_sems)

    def fold_own(at):
        parts = [land_back[j, pl.ds(at, step), :] for j in range(slabs)]
        for k in range(slabs):
            gath[me, pl.ds(k * rows + at, step), :] = merge(
                [(parts[u % slabs], (u // slabs) * slabs + k) for u in range(slots)]
            )

    over(fold_own)

    def finish():
        wait(pack_back, land_back, 1, back_sems)

        def body(at):
            parts = [
                land_back[u % slabs, pl.ds((u // slabs) * rows + at, step), :] for u in range(slots)
            ]
            for q in range(slots):
                own_ref[pl.ds(q * rows + at, step), :] = merge([(part, q) for part in parts])

        over(body)

    return (lambda: filter_half(1)), finish


def filter_kernel(
    slabs, orbs, shape, split,
    x_ref, pot_ref, own_ref, panel_ref, gram_ref, cross_ref,
    pack, land, pack_back, land_back, pot_land, wide_a, wide_b, level, gath, part, part_land, rows_land,
    a_send, a_recv, p_send, p_recv, b_send, b_recv, c_send, c_recv, d_send, d_recv, e_send, e_recv, f_send, f_recv,
    g_send, g_recv, gs_send, gs_recv, h_send, h_recv, hs_send, hs_recv,
):
    planes, rows_y, rows_z = shape
    points = planes * rows_y * rows_z
    here, me = lax.axis_index("space"), lax.axis_index("orb")
    chunk = points // slabs
    width = LANES // slabs

    barrier = pltpu.get_barrier_semaphore()
    for hop in range(1, slabs):
        pl.semaphore_signal(
            barrier, inc=1, device_id={"space": lax.rem(here + hop, slabs)}, device_id_type=MESH
        )
    for hop in range(1, orbs):
        pl.semaphore_signal(
            barrier, inc=1, device_id={"orb": lax.rem(me + hop, orbs)}, device_id_type=MESH
        )
    pl.semaphore_wait(barrier, slabs - 1 + orbs - 1)

    exchange(slabs, here, p_send, p_recv, lambda there: pot_ref, pot_land)

    panel_dev = PANEL // orbs
    folds = LANES // panel_dev
    fold = points // folds
    during = None
    if split:
        during = split_filter(
            slabs, shape, here, me, x_ref, pot_ref, own_ref, pack, land, pack_back, land_back, pot_land,
            wide_a, wide_b, level, gath,
            ((a_send, a_recv), (e_send, e_recv)), (p_send, p_recv), ((b_send, b_recv), (f_send, f_recv)),
        )
    else:
        def store_pack(j, at, value):
            pack[j, at, :] = value

        regroup(lambda r, at: x_ref[pl.ds(r * chunk + at.start, at.size), :], store_pack, slabs, chunk)
        exchange(slabs, here, a_send, a_recv, lambda there: pack.at[there], land)
        land[here] = pack[here]
        pot_land[here] = pot_ref[...]
        wait_exchange(slabs, here, p_send, p_recv, lambda there: pot_ref, pot_land)

        thin = points // LANES
        lane_group = lax.broadcasted_iota(jnp.int32, (thin, LANES), 1) // width
        fields = [pot_land[s] for s in range(slabs)]
        for l in range(LANES):
            value = None
            for s in range(slabs):
                spread = jnp.broadcast_to(fields[s][:, l : l + 1], (thin, LANES))
                value = spread if value is None else jnp.where(lane_group == s, spread, value)
            level[pl.ds(l * thin, thin), :] = (value - (SHIFT_MID + 1.5 * STENCIL[0])) * (1.0 / HALF_WIDTH)

        wait_exchange(slabs, here, a_send, a_recv, lambda there: pack.at[there], land)

        def put(target, row, value):
            target[pl.ds(points + row, value.shape[0]), :] = value
            target[pl.ds(row, value.shape[0]), :] = pltpu.roll(value, width, 1)
            target[pl.ds(2 * points + row, value.shape[0]), :] = pltpu.roll(value, LANES - width, 1)

        regroup(
            lambda r, at: land[r, at, :],
            lambda j, at, value: put(wide_a, j * chunk + at.start, value),
            slabs, chunk,
        )

        plane = rows_y * rows_z
        taps = [-0.5 * c / HALF_WIDTH for c in STENCIL]

        def sweep(source, target, first):
            def body(y, carry):
                for p in range(planes):
                    def line(q, yy):
                        return source[pl.ds(pl.multiple_of(points + q * plane + yy * rows_z, rows_z), rows_z), :]

                    row = pl.multiple_of(p * plane + y * rows_z, rows_z)
                    centre = line(p, y)
                    total = level[pl.ds(row, rows_z), :] * centre
                    for m in range(1, REACH + 1):
                        near = line(p + m, y) + line(p - m, y)
                        near += line(p, lax.rem(y + m, rows_y)) + line(p, lax.rem(y + rows_y - m, rows_y))
                        near += pltpu.roll(centre, m, 0) + pltpu.roll(centre, rows_z - m, 0)
                        total += taps[m] * near
                    if not first:
                        before = target[pl.ds(pl.multiple_of(points + row, rows_z), rows_z), :]
                        total = 2.0 * total - before
                    put(target, row, total)
                return carry

            lax.fori_loop(0, rows_y, body, 0)

        sweep(wide_a, wide_b, True)
        source, target = wide_b, wide_a
        for _ in range(DEGREE - 1):
            sweep(source, target, False)
            source, target = target, source

        def store_back(j, at, value):
            pack_back[j, at, :] = value

        regroup(
            lambda r, at: source[pl.ds(points + r * chunk + at.start, at.size), :], store_back, slabs, chunk
        )
        exchange(slabs, here, b_send, b_recv, lambda there: pack_back.at[there], land_back)
        land_back[here] = pack_back[here]
        wait_exchange(slabs, here, b_send, b_recv, lambda there: pack_back.at[there], land_back)

        def store_own(j, at, value):
            own_ref[pl.ds(j * chunk + at.start, at.size), :] = value

        regroup(lambda r, at: land_back[r, at, :], store_own, slabs, chunk)

        step = min(fold, 32)
        fold_group = lax.broadcasted_iota(jnp.int32, (step, LANES), 1) // panel_dev

        def folded(block, carry):
            at = pl.multiple_of(block * step, step)
            out = None
            for r in range(folds):
                piece = own_ref[pl.ds(r * fold + at, step), :]
                piece = pltpu.roll(piece, r * panel_dev, 1) if r else piece
                out = piece if out is None else jnp.where(fold_group == r, piece, out)
            gath[me, pl.ds(at, step), :] = out
            return carry

        lax.fori_loop(0, fold // step, folded, 0)

    block = 512

    def take(tile):
        lanes = pl.ds(pl.multiple_of(tile * LANES, LANES), LANES)

        def store_panel(j, at, value):
            panel_ref[pl.ds(j * fold + at.start, at.size), lanes] = value

        regroup(lambda r, at: gath[tile * folds + r, at, :], store_panel, folds, fold)

        def product(k, total):
            at = pl.ds(pl.multiple_of(k * block, block), block)
            return total + dot(own_ref[at, :], panel_ref[at, lanes], (0, 0))

        part[:, lanes] = lax.fori_loop(
            0, points // block, product, jnp.zeros((LANES, LANES), jnp.float32)
        )

    if folds == 2:
        gather_orb(orbs, me, gath, g_send, g_recv, gs_send, gs_recv, take, during)
    else:
        gather_orb(orbs, me, gath, g_send, g_recv, gs_send, gs_recv)

        def each(tile, carry):
            take(tile)
            return carry

        lax.fori_loop(0, PANEL // LANES, each, 0)

    top, rest = part.at[:panel_dev], part.at[panel_dev:]
    top_land, rest_land = part_land.at[:, :panel_dev], part_land.at[:, panel_dev:]
    exchange(slabs, here, c_send, c_recv, lambda there: top, top_land)
    exchange(slabs, here, d_send, d_recv, lambda there: rest, rest_land)
    part_land[here] = part[...]
    points_all = points * slabs

    def summed(view):
        total = view[0]
        for s in range(1, slabs):
            total += view[s]
        return total / points_all

    wait_exchange(slabs, here, c_send, c_recv, lambda there: top, top_land)
    rows_land[me] = summed(top_land)
    gather_orb(orbs, me, rows_land, h_send, h_recv, hs_send, hs_recv)
    wait_exchange(slabs, here, d_send, d_recv, lambda there: rest, rest_land)
    cross_ref[:panel_dev, :] = jnp.zeros((panel_dev, PANEL), jnp.float32)
    cross_ref[panel_dev:, :] = summed(rest_land)
    for o in range(orbs):
        gram_ref[o * panel_dev : (o + 1) * panel_dev, :] = rows_land[o]


def block_inverse(a):
    n = LANES
    tiles = n // 8
    rows = lax.broadcasted_iota(jnp.int32, (8, n), 0)
    cols = lax.broadcasted_iota(jnp.int32, (8, n), 1)
    work = [a[8 * t : 8 * t + 8] for t in range(tiles)]
    unit = [jnp.where(rows + 8 * t == cols, 1.0, 0.0).astype(jnp.float32) for t in range(tiles)]
    for t0 in range(tiles):
        base = 8 * t0
        columns = [jnp.broadcast_to(work[t0][:, base + k : base + k + 1], (8, n)) for k in range(8)]
        small = {
            (i, k): jnp.broadcast_to(columns[k][i : i + 1], (8, n)) for i in range(8) for k in range(i + 1)
        }
        lower, scales = {}, []
        for j in range(8):
            scales.append(1.0 / small[j, j])
            for i in range(j + 1, 8):
                lower[i, j] = small[i, j] * scales[j]
            for i in range(j + 1, 8):
                for k in range(j + 1, i + 1):
                    small[i, k] = small[i, k] - lower[i, j] * small[k, j]
        turned = {}
        for j in range(8):
            for i in range(j + 1, 8):
                value = lower[i, j]
                for k in range(j + 1, i):
                    value = value + lower[i, k] * turned[k, j]
                turned[i, j] = -value
        a_row, u_row = work[t0], unit[t0]
        a_new, u_new = a_row, u_row
        for k in range(7):
            weight = jnp.zeros((8, n), jnp.float32)
            for i in range(k + 1, 8):
                weight = jnp.where(rows == i, turned[i, k], weight)
            a_new = a_new + weight * jnp.broadcast_to(a_row[k : k + 1], (8, n))
            u_new = u_new + weight * jnp.broadcast_to(u_row[k : k + 1], (8, n))
        work[t0], unit[t0] = a_new, u_new
        if t0 == tiles - 1:
            break
        a_out = u_out = None
        for i in range(8):
            weight = jnp.where(rows == i, scales[i], 0.0)
            for k in range(i):
                weight = jnp.where(rows == k, turned[i, k] * scales[i], weight)
            a_term = weight * jnp.broadcast_to(a_new[i : i + 1], (8, n))
            u_term = weight * jnp.broadcast_to(u_new[i : i + 1], (8, n))
            a_out = a_term if a_out is None else a_out + a_term
            u_out = u_term if u_out is None else u_out + u_term
        a_rows = [jnp.broadcast_to(a_out[k : k + 1], (8, n)) for k in range(8)]
        u_rows = [jnp.broadcast_to(u_out[k : k + 1], (8, n)) for k in range(8)]
        for t in range(t0 + 1, tiles):
            before = work[t]
            for k in range(8):
                column = jnp.broadcast_to(before[:, base + k : base + k + 1], (8, n))
                work[t] = work[t] - column * a_rows[k]
                unit[t] = unit[t] - column * u_rows[k]
    out = []
    for t in range(tiles):
        pivots = jnp.sum(jnp.where(rows + 8 * t == cols, work[t], 0.0), axis=1, keepdims=True)
        out.append(unit[t] * (1.0 / jnp.sqrt(pivots)))
    return jnp.concatenate(out, axis=0)


def solve_kernel(orbs, own_ref, panel_ref, gram_ref, cross_ref, out_ref, work, inverse, weights):
    panel_dev = PANEL // orbs
    me = lax.axis_index("orb")
    n = LANES
    blocks = PANEL // n
    work[...] = gram_ref[...]
    inverse[...] = jnp.zeros_like(inverse)

    def factor(b, carry):
        at = pl.multiple_of(b * n, n)
        diag = block_inverse(work[pl.ds(at, n), pl.ds(at, n)])
        inverse[pl.ds(at, n), pl.ds(at, n)] = diag
        for i in range(1, blocks):
            @pl.when(i > b)
            def _():
                work[i * n : (i + 1) * n, pl.ds(at, n)] = dot(
                    work[i * n : (i + 1) * n, pl.ds(at, n)], diag, (1, 1)
                )
        for i in range(1, blocks):
            @pl.when(i > b)
            def _():
                left = work[i * n : (i + 1) * n, pl.ds(at, n)]
                for k in range(1, i + 1):
                    @pl.when(k > b)
                    def _():
                        right = work[k * n : (k + 1) * n, pl.ds(at, n)]
                        work[i * n : (i + 1) * n, k * n : (k + 1) * n] -= dot(left, right, (1, 1))
        return carry

    lax.fori_loop(0, blocks, factor, 0)
    for i in range(1, blocks):
        span = i * n
        inner = dot(work[i * n : (i + 1) * n, :span], inverse[:span, :span], (1, 0))
        inverse[i * n : (i + 1) * n, :span] = -dot(
            inverse[i * n : (i + 1) * n, i * n : (i + 1) * n], inner, (1, 0)
        )

    middle = dot(cross_ref[...], inverse[...], (1, 1))
    weights[...] = -dot(middle, inverse[...], (1, 0))
    weights[:panel_dev, :] = inverse[pl.ds(pl.multiple_of(me * panel_dev, panel_dev), panel_dev), :]
    points = own_ref.shape[0]
    block = 256
    lanes = lax.broadcasted_iota(jnp.int32, (block, LANES), 1)

    def final(k, carry):
        at = pl.ds(pl.multiple_of(k * block, block), block)
        kept = jnp.where(lanes < panel_dev, 0.0, own_ref[at, :])
        out_ref[at, :] = kept + dot(panel_ref[at, :], weights[...], (1, 1))
        return carry

    lax.fori_loop(0, points // block, final, 0)


def pieces(x):
    high = x.astype(jnp.bfloat16)
    return high, (x - high.astype(jnp.float32)).astype(jnp.bfloat16)


def dot_pieces(a, b, dims):
    def one(left, right):
        return lax.dot_general(
            left, right, ((dims[:1], dims[1:]), ((), ())), preferred_element_type=jnp.float32
        )

    return one(a[0], b[0]) + (one(a[0], b[1]) + one(a[1], b[0]))


def unfolded(product, rows):
    half = LANES // 2
    lanes = lax.broadcasted_iota(jnp.int32, (half, LANES), 1)
    out = []
    for r in range(rows):
        sides = []
        for c in range(2):
            at = product[r * LANES : (r + 1) * LANES, c * LANES : (c + 1) * LANES]
            sides.append(at[:half] + pltpu.roll(at[half:], half, 1))
        out.append(jnp.where(lanes < half, sides[0], pltpu.roll(sides[1], half, 1)))
    return out


def link_orders():
    def both(table):
        out = {z: list(items) for z, items in table.items()}
        for z, items in table.items():
            out[3 - z] = [(1 - way, 3 - o, 1 - h) for way, o, h in items]
        return out

    starts = [
        {0: [(0, 0, 0)], 1: [(1, 1, 0)], 2: [(1, 2, 0), (0, 2, 0)]},
        {0: [(0, 0, 1)], 1: [(0, 1, 1), (1, 1, 1)], 2: [(0, 2, 1)], 3: [(1, 3, 1), (1, 3, 0)]},
    ]
    arrive = [
        both({1: [(1, 2, 0)]}),
        both({0: [(1, 1, 0), (1, 1, 1)], 1: [(0, 0, 0), (1, 3, 0)]}),
        both({0: [(1, 2, 0)], 1: [(0, 0, 1), (1, 2, 1)]}),
        both({0: [(1, 3, 0)], 1: [(1, 3, 1)]}),
        both({0: [(1, 2, 1)]}),
        both({0: [(1, 3, 1)]}),
    ]
    passed = [
        both({1: [(1, 2, 0)]}),
        both({1: [(0, 1, 0)]}),
        both({1: [(0, 0, 0), (1, 3, 0)]}),
        both({1: [(1, 2, 1)]}),
        both({1: [(1, 3, 1)]}),
    ]
    return starts, arrive, passed


def tile_inverse(a):
    n = LANES
    tiles = n // 8
    rows = lax.broadcasted_iota(jnp.int32, (8, n), 0)
    lanes = lax.broadcasted_iota(jnp.int32, (8, n), 1)

    def row_of(value, k):
        return jnp.broadcast_to(value[k : k + 1], (8, n))

    def column_of(value, k):
        return jnp.broadcast_to(value[:, k : k + 1], (8, n))

    def tree(terms):
        while len(terms) > 1:
            paired = [terms[i] + terms[i + 1] for i in range(0, len(terms) - 1, 2)]
            terms = paired + terms[len(terms) - len(terms) % 2 :]
        return terms[0]

    work = [a[8 * t : 8 * t + 8] for t in range(tiles)]
    cols = [column_of(work[0], k) for k in range(8)]
    out = []
    for t0 in range(tiles):
        base = 8 * t0
        last = t0 == tiles - 1
        if not last:
            side = [column_of(work[t0 + 1], base + k) for k in range(8)]
            ahead = [column_of(work[t0 + 1], base + 8 + k) for k in range(8)]
            moved = list(side)
        below, pivots, scales = [], [], []
        for j in range(8):
            pivot = row_of(cols[j], j)
            scale = 1.0 / pivot
            lead = jnp.where(rows > j, cols[j], 0.0)
            pivots.append(pivot)
            scales.append(scale)
            below.append(lead * scale)
            for k in range(j + 1, 8):
                part = row_of(cols[k], j) * scale
                cols[k] = cols[k] - lead * part
                if not last:
                    moved[k] = moved[k] - moved[j] * part
        above = cols
        if not last:
            scaled = [moved[j] * scales[j] for j in range(8)]
            cols = [
                ahead[k] - tree([scaled[j] * row_of(moved[j], k) for j in range(8)]) for k in range(8)
            ]
        inside = (lanes >= base) & (lanes < base + 8)
        value = jnp.where(inside, jnp.where(lanes == rows + base, 1.0, 0.0), work[t0])
        root, turn = pivots[0], scales[0]
        for j in range(8):
            value = value - below[j] * row_of(value, j)
            if j:
                root = jnp.where(rows == j, pivots[j], root)
                turn = jnp.where(rows == j, scales[j], turn)
        out.append(jnp.where(lanes < base + 8, value * lax.rsqrt(root), 0.0))
        if last:
            break
        value = value * turn
        for k in range(7, 0, -1):
            value = value - jnp.where(rows < k, above[k] * turn, 0.0) * row_of(value, k)
        leads = [row_of(value, k) for k in range(8)]
        for t in range(t0 + 1, tiles):
            before = work[t]
            columns = side if t == t0 + 1 else [column_of(before, base + k) for k in range(8)]
            work[t] = jnp.where(inside, 0.0, before) - tree([columns[k] * leads[k] for k in range(8)])
    return jnp.concatenate(out, axis=0)


def early_kernel(
    slabs, orbs, shape,
    x_hbm, pot_ref, gath, rest_ref, weight_ref,
    x_ref, pot_wide, pot_mine, pack, land, pack_back, land_back, pot_land, wide_a, wide_b, level,
    gram_part, gram_land, gram_chip, gram_all, cross_part, cross_land, cross, work, inverse,
    x_sem, a_send, a_recv, p_send, p_recv, b_send, b_recv,
    along_send, along_recv, direct_send, across_send, across_recv,
    r_send, r_recv, z_send, z_recv, s_send, s_recv, t_send, t_recv, c_send, c_recv,
):
    planes, rows_y, rows_z = shape
    points = planes * rows_y * rows_z
    here, me = lax.axis_index("space"), lax.axis_index("orb")
    chips = orbs // 2
    chip, core = me // 2, lax.rem(me, 2)
    partner = chip * 2 + (1 - core)
    slots = 2 * slabs
    width = LANES // slots
    rows = points // slots
    plane = 3 * rows
    sub = rows // 2
    fold = points // 2
    part_rows = fold // 2
    panel_dev = PANEL // orbs
    points_all = points * slabs
    step = 16

    def fetch(c):
        view = slice(c * sub, (c + 1) * sub)
        return pltpu.make_async_copy(x_hbm.at[:, view], x_ref.at[:, view], x_sem.at[c])

    for c in range(2):
        fetch(c).start()

    barrier = pltpu.get_barrier_semaphore()
    for hop in range(1, slabs):
        pl.semaphore_signal(
            barrier, inc=1, device_id={"space": lax.rem(here + hop, slabs)}, device_id_type=MESH
        )
    for hop in range(1, orbs):
        pl.semaphore_signal(
            barrier, inc=1, device_id={"orb": lax.rem(me + hop, orbs)}, device_id_type=MESH
        )

    def exchange_groups(x, unit):
        lane = lax.broadcasted_iota(jnp.int32, (step, LANES), 1) // unit
        outer, inner = lane // 2 % 2 == 0, lane % 2 == 0
        pairs = [None] * 4
        for a in range(2):
            pairs[a] = jnp.where(outer, x[a], pltpu.roll(x[a + 2], 2 * unit, 1))
            pairs[a + 2] = jnp.where(outer, pltpu.roll(x[a], LANES - 2 * unit, 1), x[a + 2])
        out = [None] * 4
        for a in (0, 2):
            out[a] = jnp.where(inner, pairs[a], pltpu.roll(pairs[a + 1], unit, 1))
            out[a + 1] = jnp.where(inner, pltpu.roll(pairs[a], LANES - unit, 1), pairs[a + 1])
        return out

    def over(c, body):
        def one(block, carry):
            body(pl.multiple_of(c * sub + block * step, step))
            return carry

        lax.fori_loop(0, sub // step, one, 0, unroll=2)

    def span(h, c):
        return slice(h * rows + c * sub, h * rows + (c + 1) * sub)

    def send(buf, landing, h, c, sems):
        at, k = span(h, c), h * 2 + c
        exchange(
            slabs, here, sems[0].at[k], sems[1].at[k], lambda there: buf.at[there, at], landing.at[:, at]
        )
        landing[here, at] = buf[here, at]

    def wait(buf, landing, h, c, sems):
        at, k = span(h, c), h * 2 + c
        wait_exchange(
            slabs, here, sems[0].at[k], sems[1].at[k], lambda there: buf.at[there, at], landing.at[:, at]
        )

    out_sems, back_sems = (a_send, a_recv), (b_send, b_recv)

    def pack_part(h, c):
        def body(at):
            parts = [x_ref[q, pl.ds(at, step), :] for q in range(slots)]
            lane = lax.broadcasted_iota(jnp.int32, (step, LANES), 1)
            turned = [pltpu.roll(part, LANES // 2, 1) for part in (parts[:slabs] if h else parts[slabs:])]
            joined = [
                jnp.where(lane < LANES // 2, turned[u] if h else parts[u], parts[u + slabs] if h else turned[u])
                for u in range(slabs)
            ]
            for j, value in enumerate(exchange_groups(joined, width)):
                pack[j, pl.ds(h * rows + at, step), :] = value

        with jax.named_scope("pack"):
            over(c, body)

    def put(target, p, row, value):
        lane = lax.broadcasted_iota(jnp.int32, value.shape, 1)
        size = value.shape[0]
        swapped = jnp.take_along_axis(value, jnp.where(lane // width % 2 == 0, lane + width, lane - width), axis=1)
        target[pl.ds((planes + p) * plane + rows + row, size), :] = value
        target[pl.ds((planes + p) * plane + row, size), :] = swapped
        target[pl.ds((planes + p) * plane + 2 * rows + row, size), :] = swapped
        target[pl.ds(p * plane + rows + row, size), :] = pltpu.roll(value, 2 * width, 1)
        target[pl.ds((2 * planes + p) * plane + rows + row, size), :] = pltpu.roll(value, LANES - 2 * width, 1)

    taps = [-0.5 * c / HALF_WIDTH for c in STENCIL]

    def sweep(source, target, first, low=0, high=rows_y // 2):
        def body(y, carry):
            for p in range(planes):
                def line(q, yy):
                    row = pl.multiple_of((planes + q) * plane + rows + yy * rows_z, rows_z)
                    return source[pl.ds(row, rows_z), :]

                row = pl.multiple_of(y * rows_z, rows_z)
                centre = line(p, y)
                total = level[pl.ds(p * rows + row, rows_z), :] * centre
                for m in range(1, REACH + 1):
                    near = line(p + m, y) + line(p - m, y) + line(p, y + m) + line(p, y - m)
                    near += pltpu.roll(centre, m, 0) + pltpu.roll(centre, rows_z - m, 0)
                    total += taps[m] * near
                if not first:
                    total = 2.0 * total - target[pl.ds((planes + p) * plane + rows + row, rows_z), :]
                put(target, p, row, total)
            return carry

        lax.fori_loop(low, high, body, 0, unroll=rows_y // 4)

    def filter_half(h, ready):
        for c in range(2):
            with jax.named_scope("wait_a"):
                wait(pack, land, h, c, out_sems)

            def unpack(at):
                parts = [land[i, pl.ds(h * rows + at, step), :] for i in range(slabs)]
                for p, value in enumerate(exchange_groups(parts, 2 * width)):
                    put(wide_a, p, at, value)

            with jax.named_scope("unpack"):
                over(c, unpack)
        source, target = wide_a, wide_b
        with jax.named_scope("sweep"):
            for order in range(DEGREE - 1):
                sweep(source, target, order == 0)
                source, target = target, source
        for c in range(2):
            with jax.named_scope("sweep"):
                sweep(source, target, False, c * rows_y // 4, (c + 1) * rows_y // 4)

            def body(at):
                parts = [target[pl.ds((planes + p) * plane + rows + at, step), :] for p in range(planes)]
                for i, value in enumerate(exchange_groups(parts, 2 * width)):
                    pack_back[i, pl.ds(h * rows + at, step), :] = value

            with jax.named_scope("pack_b"):
                over(c, body)
            ready(c)

    def fold_part(h, c, store):
        with jax.named_scope("wait_b"):
            wait(pack_back, land_back, h, c, back_sems)

        def body(at):
            parts = [land_back[j, pl.ds(h * rows + at, step), :] for j in range(slabs)]
            for k, value in enumerate(exchange_groups(parts, width)):
                row = pl.multiple_of(c * part_rows + k * sub + at - c * sub, step)
                store(pl.ds(row, step), value)

        with jax.named_scope("fold"):
            over(c, body)

    pot_wide[...] = jnp.zeros_like(pot_wide)
    pot_wide[: planes * rows_y, :rows_z] = pot_ref[...]
    pot_mine[...] = pot_wide[...].T[:rows_z]
    for c in range(2):
        fetch(c).wait()
        pack_part(0, c)
    with jax.named_scope("barrier"):
        pl.semaphore_wait(barrier, slabs - 1 + orbs - 1)
    exchange(slabs, here, p_send, p_recv, lambda there: pot_mine, pot_land)
    for c in range(2):
        send(pack, land, 0, c, out_sems)
    for c in range(2):
        pack_part(1, c)
    pot_land[here] = pot_mine[...]
    with jax.named_scope("level"):
        wait_exchange(slabs, here, p_send, p_recv, lambda there: pot_mine, pot_land)
        lane = lax.broadcasted_iota(jnp.int32, (rows_z, LANES), 1)
        lane_slot = lane // width
        held = LANES // 2
        fields = [
            jnp.where(lane < held, pot_land[2 * s], pltpu.roll(pot_land[2 * s + 1], held, 1))
            for s in range(slabs // 2)
        ]
        first = lane_slot // 2 % 2 * held + lane_slot % 2 * (rows_y // 2)
        for p in range(planes):
            for y in range(rows_y // 2):
                taken = [
                    jnp.take_along_axis(field, first + (p * rows_y + y), axis=1) for field in fields
                ]
                value = jnp.where(lane < held, taken[0], taken[1])
                level[pl.ds(p * rows + y * rows_z, rows_z), :] = (
                    value - (SHIFT_MID + 1.5 * STENCIL[0])
                ) * (1.0 / HALF_WIDTH)

    starts, arrive, passed = link_orders()

    def along(way, origin, h):
        view = gath.at[origin * 2 + core, h * part_rows : (h + 1) * part_rows]
        return pltpu.make_async_remote_copy(
            src_ref=view,
            dst_ref=view,
            send_sem=along_send.at[way, origin * 2 + h],
            recv_sem=along_recv.at[origin * 2 + h],
            device_id={"orb": (chip + 1 - 2 * way) * 2 + core},
            device_id_type=MESH,
        )

    def direct(z):
        way, h = (0, 1) if z == 0 else (1, 0)
        view = gath.at[z * 2 + core, h * part_rows : (h + 1) * part_rows]
        return pltpu.make_async_remote_copy(
            src_ref=view,
            dst_ref=view,
            send_sem=direct_send.at[0],
            recv_sem=along_recv.at[z * 2 + h],
            device_id={"orb": (z + 2 - 4 * way) * 2 + core},
            device_id_type=MESH,
        )

    def across(origin, h, side):
        view = gath.at[origin * 2 + side, h * part_rows : (h + 1) * part_rows]
        return pltpu.make_async_remote_copy(
            src_ref=view,
            dst_ref=view,
            send_sem=across_send.at[origin * 2 + h],
            recv_sem=across_recv.at[origin * 2 + h],
            device_id={"orb": partner},
            device_id_type=MESH,
        )

    def on_chip(z, body):
        pl.when(chip == z)(body)

    def by_chip(table, body):
        for z in table:
            def run():
                for item in table[z]:
                    body(*item)

            on_chip(z, run)

    own_items = {z: [(0, z, h) for h in range(2)] for z in range(chips)}

    def begin(c):
        on_chip((chips - 1) * (1 - c), lambda: direct((chips - 1) * (1 - c)).start())
        by_chip(starts[c], lambda *item: along(*item).start())
        for z in range(chips):
            on_chip(z, lambda: across(z, c, core).start())

    def receive(t):
        def one(way, o, h):
            along(way, o, h).wait_recv()
            across(o, h, core).start()

        with jax.named_scope("receive"):
            by_chip(arrive[t], one)

    def forward(t):
        by_chip(passed[t], lambda *item: along(*item).start())

    def settle(t):
        with jax.named_scope("settle"):
            by_chip(arrive[t], lambda way, o, h: across(o, h, 1 - core).wait_recv())

    def settle_own():
        by_chip(own_items, lambda way, o, h: across(o, h, 1 - core).wait_recv())

    def drain(first, past):
        for z in range(chips):
            def run():
                if first == 0 and z in (0, chips - 1):
                    direct(z).wait_send()
                sent = (starts if first == 0 else []) + passed[first:past]
                for table in sent:
                    for item in table.get(z, []):
                        along(*item).wait_send()
                for h in range(2 if first == 0 else 0):
                    across(z, h, core).wait_send()
                for table in arrive[first:past]:
                    for way, o, h in table.get(z, []):
                        across(o, h, core).wait_send()

            on_chip(z, run)

    for c in range(2):
        send(pack, land, 1, c, out_sems)
    filter_half(0, lambda c: send(pack_back, land_back, 0, c, back_sems))

    def store_panel(at, value):
        gath[me, at, :] = value

    for c in range(2):
        fold_part(0, c, store_panel)
        begin(c)

    filter_half(1, lambda c: None)
    receive(0)
    forward(0)
    receive(1)
    forward(1)
    settle_own()
    settle(0)
    settle(1)

    tiles = chips * (chips + 1) // 2
    share = tiles // 2
    duties = [[(3, (0, 1, 2, 3)), (0, (0,))], [(2, (0, 1, 2)), (1, (0, 1))]]
    block = share * LANES // slabs
    centre = (chip + 1) // 2 == 1

    piece = block // 2

    def block_at(s, g):
        return pl.ds(pl.multiple_of(s * block + g * piece, 8), piece)

    def pair(z, at):
        return jnp.concatenate([gath[z * 2, at, :], gath[z * 2 + 1, at, :]], axis=1)

    @pl.when(centre)
    def _():
        at = pl.ds(pl.multiple_of((chip - 1) * part_rows, part_rows), part_rows)

        with jax.named_scope("gram"):
            for c, groups in enumerate(duties):
                def run():
                    n = 0
                    for za, zbs in groups:
                        left = pieces(pair(za, at).T)
                        for zb in zbs:
                            product = dot_pieces(left, pieces(pair(zb, at)), (1, 0))
                            for r, value in enumerate(unfolded(product, 2)):
                                gram_part[n * LANES + r * panel_dev : n * LANES + (r + 1) * panel_dev, :] = value
                            n += 1

                pl.when(core == c)(run)
        for g in range(2):
            exchange(
                slabs, here, r_send.at[g], r_recv.at[g],
                lambda there: gram_part.at[block_at(there, g)], gram_land.at[g],
            )

    for c in range(2):
        send(pack_back, land_back, 1, c, back_sems)

    def spread(g, index, there):
        view = gram_chip.at[g, index]
        return pltpu.make_async_remote_copy(
            src_ref=view,
            dst_ref=view,
            send_sem=z_send.at[g, there],
            recv_sem=z_recv.at[g, index],
            device_id={"orb": there * 2 + core},
            device_id_type=MESH,
        )

    for g in range(2):
        @pl.when(centre)
        def _():
            with jax.named_scope("wait_r"):
                wait_exchange(
                    slabs, here, r_send.at[g], r_recv.at[g],
                    lambda there: gram_part.at[block_at(there, g)], gram_land.at[g],
                )
            gram_land[g, here] = gram_part[block_at(here, g), :]
            total = gram_land[g, 0]
            for s in range(1, slabs):
                total += gram_land[g, s]
            gram_chip[g, chip - 1] = total / points_all

        for z in range(1, 3):
            def body():
                for there in range(chips):
                    if there != z:
                        spread(g, z - 1, there).start()

            on_chip(z, body)
    forward(2)
    weight_ref[...] = jnp.zeros_like(weight_ref)
    with jax.named_scope("drain"):
        drain(0, 2)

    def gram_side(g, side, s):
        view = gram_all.at[side, block_at(s, g)]
        return pltpu.make_async_remote_copy(
            src_ref=view,
            dst_ref=view,
            send_sem=t_send.at[g, s],
            recv_sem=t_recv.at[g, s],
            device_id={"orb": partner},
            device_id_type=MESH,
        )

    def plane_copy(g, hop, s, there):
        view = gram_all.at[core, block_at(s, g)]
        return pltpu.make_async_remote_copy(
            src_ref=view,
            dst_ref=view,
            send_sem=s_send.at[g, hop - 1],
            recv_sem=s_recv.at[g, hop - 1],
            device_id={"space": there},
            device_id_type=MESH,
        )

    for g in range(2):
        with jax.named_scope("wait_z"):
            for z in range(chips):
                def body():
                    for index in range(2):
                        if z != index + 1:
                            spread(g, index, z).wait_recv()

                on_chip(z, body)
        gram_all[core, block_at(here, g), :] = gram_chip[g, 0] + gram_chip[g, 1]
        for hop in range(1, slabs):
            plane_copy(g, hop, here, lax.rem(here + hop, slabs)).start()
        gram_side(g, core, here).start()

    def store_rest(at, value):
        rest_ref[at, :] = value


    def couple_part(z, k):
        at = pl.ds(pl.multiple_of(k * 2 * LANES, 2 * LANES), 2 * LANES)
        return dot_pieces(pieces(rest_ref[at, :]), pieces(pair(z, at)), (0, 0))

    def couple_send(n, total):
        value = unfolded(total, 1)[0]
        cross_part[n] = value
        cross_land[n, here] = value
        exchange(slabs, here, c_send.at[n], c_recv.at[n], lambda there: cross_part.at[n], cross_land.at[n])

    def couple(n, z):
        with jax.named_scope("couple"):
            total = couple_part(z, 0)
            for k in range(1, fold // (2 * LANES)):
                total += couple_part(z, k)
        couple_send(n, total)

    lower = chip // 2
    order = [chip, chip + 1 - 2 * lax.rem(chip, 2), 2 - lower, 3 - 3 * lower]
    receive(2)
    forward(3)
    with jax.named_scope("wait_s"):
        for g in range(2):
            for hop in range(1, slabs):
                source = lax.rem(here + slabs - hop, slabs)
                plane_copy(g, hop, source, lax.rem(here + hop, slabs)).wait_recv()
                gram_side(g, core, source).start()
    for c in range(2):
        fold_part(1, c, store_rest)
    with jax.named_scope("wait_t"):
        for g in range(2):
            for s in range(slabs):
                gram_side(g, 1 - core, s).wait_recv()

    n = LANES
    inverse[...] = jnp.zeros_like(inverse)
    for c, groups in enumerate(duties):
        for k, (za, zb) in enumerate([(za, zb) for za, zbs in groups for zb in zbs]):
            work[za * n : (za + 1) * n, zb * n : (zb + 1) * n] = gram_all[c, k * n : (k + 1) * n, :]

    def between(b):
        if b == 0:
            settle(2)
            receive(3)
            forward(4)
            receive(4)
        if b == 1:
            settle(3)
            settle(4)
        if b == 2:
            receive(5)
            settle(5)
            couple(3, order[3])

    for b in range(chips):
        at, past = slice(b * n, (b + 1) * n), slice((b + 1) * n, PANEL)
        with jax.named_scope("diag"):
            diag_in = work[at, at]
            if b:
                before, done = slice((b - 1) * n, b * n), slice(0, b * n)
                if b < chips - 1:
                    lower_part = work[past, before]
                    work[past, at] -= dot(lower_part, work[at, before], (1, 1))
                    work[past, past] -= dot(lower_part, lower_part, (1, 1))
                inner = dot(work[at, done], inverse[done, done], (1, 0))
            tied = None
            for k in range(fold // (2 * LANES) if b < chips - 1 else 0):
                term = couple_part(order[b], k)
                tied = term if tied is None else tied + term
            diag = tile_inverse(diag_in)
            inverse[at, at] = diag
            if b < chips - 1:
                couple_send(b, tied)
        with jax.named_scope("panel"):
            if b < chips - 1:
                scaled = dot(work[past, at], diag, (1, 1))
                work[past, at] = scaled
                work[(b + 1) * n : (b + 2) * n, (b + 1) * n : (b + 2) * n] -= dot(scaled[:n], scaled[:n], (1, 1))
            if b:
                inverse[at, done] = -dot(diag, inner, (1, 0))
        between(b)

    with jax.named_scope("cross"):
        for k in range(chips):
            wait_exchange(
                slabs, here, c_send.at[k], c_recv.at[k], lambda there: cross_part.at[k], cross_land.at[k]
            )
            total = cross_land[k, 0]
            for s in range(1, slabs):
                total += cross_land[k, s]
            cross[:, pl.ds(pl.multiple_of(order[k] * LANES, LANES), LANES)] = total / points_all
    with jax.named_scope("weights"):
        factors = pieces(inverse[...])
        middle = dot_pieces(pieces(cross[...]), factors, (1, 1))
        trail = -dot_pieces(pieces(middle), factors, (1, 0))
        own = inverse[pl.ds(pl.multiple_of(me * panel_dev, panel_dev), panel_dev), :]
        turned = jnp.concatenate([own, trail], axis=0).T
        for o in range(orbs):
            value = turned[o * panel_dev : (o + 1) * panel_dev]
            weight_ref[o * LANES : o * LANES + panel_dev, :LANES] = value
            weight_ref[o * LANES + panel_dev : (o + 1) * LANES, LANES:] = value
    with jax.named_scope("last"):
        drain(2, 6)
        for z in range(1, 3):
            def body():
                for g in range(2):
                    for there in range(chips):
                        if there != z:
                            spread(g, z - 1, there).wait_send()

            on_chip(z, body)
    for g in range(2):
        for hop in range(1, slabs):
            plane_copy(g, hop, here, lax.rem(here + hop, slabs)).wait_send()
        for s in range(slabs):
            gram_side(g, core, s).wait_send()


def final_kernel(gath_ref, rest_ref, weight_ref, out_ref, high, low):
    orbs, fold, n = gath_ref.shape
    rows = out_ref.shape[1] * out_ref.shape[3]
    i = pl.program_id(0)

    @pl.when(i == 0)
    def _():
        high[...], low[...] = pieces(weight_ref[...])

    at = pl.ds(pl.multiple_of(i * rows, rows), rows)
    total = None
    for z in range(orbs // 2):
        k = slice(z * 2 * n, (z + 1) * 2 * n)
        pair = jnp.concatenate([gath_ref[z * 2, at, :], gath_ref[z * 2 + 1, at, :]], axis=1)
        value = dot_pieces(pieces(pair), (high[k, :], low[k, :]), (1, 0))
        total = value if total is None else total + value
    lanes = lax.broadcasted_iota(jnp.int32, (rows, n), 1)
    kept = rest_ref[at, :]
    count = out_ref.shape[1]
    for h in range(2):
        held = kept if h else pltpu.roll(kept, n // 2, 1)
        value = jnp.where(lanes < n // 2, 0.0, held) + total[:, h * n : (h + 1) * n]
        for k in range(count):
            out_ref[h, k, 0] = value[k * (rows // count) : (k + 1) * (rows // count)]


def early_device(slabs, orbs, orbitals, potential):
    planes, rows_y, rows_z, columns = orbitals.shape
    points = planes * rows_y * rows_z
    panel_dev = PANEL // orbs
    chips = orbs // 2
    slots = 2 * slabs
    rows = points // slots
    fold = points // 2
    tiles = chips * (chips + 1) // 2
    block = tiles // 2 * LANES // slabs
    f32 = jnp.float32
    vmem = pl.BlockSpec(memory_space=pltpu.VMEM)
    dma = pltpu.SemaphoreType.DMA
    gath, rest, weight = pl.pallas_call(
        functools.partial(early_kernel, slabs, orbs, (planes, rows_y, rows_z)),
        out_shape=[
            jax.ShapeDtypeStruct((orbs, fold, LANES), f32),
            jax.ShapeDtypeStruct((fold, LANES), f32),
            jax.ShapeDtypeStruct((orbs * LANES, 2 * LANES), f32),
        ],
        in_specs=[pl.BlockSpec(memory_space=pltpu.HBM), vmem],
        out_specs=[vmem] * 3,
        scratch_shapes=[
            pltpu.VMEM((slots, rows, LANES), f32),
            pltpu.VMEM((LANES, LANES), f32),
            pltpu.VMEM((rows_z, LANES), f32),
        ]
        + [pltpu.VMEM((slabs, points // slabs, LANES), f32)] * 4
        + [
            pltpu.VMEM((slabs, rows_z, LANES), f32),
            pltpu.VMEM((9 * points // 2, LANES), f32),
            pltpu.VMEM((9 * points // 2, LANES), f32),
            pltpu.VMEM((points // 2, LANES), f32),
            pltpu.VMEM((slabs * block, LANES), f32),
            pltpu.VMEM((2, slabs, block // 2, LANES), f32),
            pltpu.VMEM((2, 2, block // 2, LANES), f32),
            pltpu.VMEM((2, slabs * block, LANES), f32),
            pltpu.VMEM((chips, panel_dev, LANES), f32),
            pltpu.VMEM((chips, slabs, panel_dev, LANES), f32),
            pltpu.VMEM((panel_dev, PANEL), f32),
            pltpu.VMEM((PANEL, PANEL), f32),
            pltpu.VMEM((PANEL, PANEL), f32),
        ]
        + [dma((2,))]
        + [dma((4, slabs - 1))] * 2
        + [dma((slabs - 1,))] * 2
        + [dma((4, slabs - 1))] * 2
        + [dma((2, orbs)), dma((orbs,)), dma((1,))]
        + [dma((orbs,))] * 2
        + [dma((2, slabs - 1))] * 2
        + [dma((2, chips)), dma((2, 2))]
        + [dma((2, slabs - 1))] * 2
        + [dma((2, slabs))] * 2
        + [dma((chips, slabs - 1))] * 2,
        compiler_params=pltpu.CompilerParams(
            collective_id=0, has_side_effects=True, vmem_limit_bytes=40 << 20
        ),
    )(orbitals.reshape(slots, rows, columns), potential.reshape(planes * rows_y, rows_z))
    whole = [pl.BlockSpec(memory_space=pltpu.VMEM)] * 3
    out = pl.pallas_call(
        final_kernel,
        grid=(slabs,),
        out_shape=jax.ShapeDtypeStruct((2, slabs, 2, rows // 2, LANES), f32),
        in_specs=whole,
        out_specs=pl.BlockSpec(
            (2, slabs // 2, 1, rows // 2, LANES), lambda i: (0, i % 2, i // 2, 0, 0)
        ),
        scratch_shapes=[pltpu.VMEM((orbs * LANES, 2 * LANES), jnp.bfloat16)] * 2,
        compiler_params=pltpu.CompilerParams(vmem_limit_bytes=16 << 20),
    )(gath, rest, weight)
    return out.reshape(planes, rows_y, rows_z, columns)


def per_device(slabs, orbs, orbitals, potential):
    planes, rows_y, rows_z, columns = orbitals.shape
    points = planes * rows_y * rows_z
    panel_dev = PANEL // orbs
    folds = LANES // panel_dev
    thin = points // LANES
    f32 = jnp.float32
    vmem = pl.BlockSpec(memory_space=pltpu.VMEM)
    dma = pltpu.SemaphoreType.DMA
    steps = max(orbs // 2 - 1, 1)
    split = folds == 2 and planes == slabs and rows_y // 2 >= REACH and steps >= 2
    if split and orbs == 8 and slabs == 4 and PANEL == 4 * LANES and 2 * planes * rows_y == LANES:
        return early_device(slabs, orbs, orbitals, potential)
    flat = orbitals.reshape(points, columns)
    own, panel, gram, cross = pl.pallas_call(
        functools.partial(filter_kernel, slabs, orbs, (planes, rows_y, rows_z), split),
        out_shape=[
            jax.ShapeDtypeStruct((points, LANES), f32),
            jax.ShapeDtypeStruct((points, PANEL), f32),
            jax.ShapeDtypeStruct((PANEL, PANEL), f32),
            jax.ShapeDtypeStruct((LANES, PANEL), f32),
        ],
        in_specs=[vmem] * 2,
        out_specs=[vmem] * 4,
        scratch_shapes=[pltpu.VMEM((slabs, points // slabs, LANES), f32)] * 4
        + [
            pltpu.VMEM((slabs, thin, LANES), f32),
            pltpu.VMEM(((9 if split else 6) * points // 2, LANES), f32),
            pltpu.VMEM(((9 if split else 6) * points // 2, LANES), f32),
            pltpu.VMEM((points, LANES), f32),
            pltpu.VMEM((orbs, points // folds, LANES), f32),
            pltpu.VMEM((LANES, PANEL), f32),
            pltpu.VMEM((slabs, LANES, PANEL), f32),
            pltpu.VMEM((orbs, panel_dev, PANEL), f32),
        ]
        + [dma((slabs,))] * 14
        + [dma((2, steps))] * 2 + [dma((2 * steps + 1,))] * 2
        + [dma((2, steps))] * 2 + [dma((2 * steps + 1,))] * 2,
        compiler_params=pltpu.CompilerParams(
            collective_id=0, has_side_effects=True, vmem_limit_bytes=32 << 20
        ),
    )(flat, potential.reshape(LANES, thin).T)
    out = pl.pallas_call(
        functools.partial(solve_kernel, orbs),
        out_shape=jax.ShapeDtypeStruct((points, LANES), f32),
        in_specs=[vmem] * 4,
        out_specs=vmem,
        scratch_shapes=[
            pltpu.VMEM((PANEL, PANEL), f32),
            pltpu.VMEM((PANEL, PANEL), f32),
            pltpu.VMEM((LANES, PANEL), f32),
        ],
        compiler_params=pltpu.CompilerParams(vmem_limit_bytes=32 << 20),
    )(own, panel, gram, cross)
    return out.reshape(planes, rows_y, rows_z, columns)


def solution(mesh):
    placed = (P("space", None, None, "orb"), P("space", None, None))
    return jax.shard_map(
        functools.partial(per_device, mesh.shape["space"], mesh.shape["orb"]),
        mesh=mesh,
        in_specs=placed,
        out_specs=P("space", None, None, "orb"),
        check_vma=False,
    )
```
